32 devices in a mesh: dp: 16 (over z, y, core), head: 2 (over x).
Axes of the slice: x: 2, y: 2, z: 4, core: 2. Of those that a mesh axis runs over, the one named last changes fastest.
Arguments:
- frames: bfloat16 [48000, 512], P(('dp', 'head')), may hold values from -6 to 6
- cotangent: bfloat16 [48000, 512], P(('dp', 'head')), may hold values from -6 to 6
- window_live: int32 [32], replicated, may hold values from 0 to 1, as said below
- language: int32 [32], replicated, may hold values from 0 to 98
- task: int32 [32], replicated, may hold values from 0 to 1
- ln1_gain: float32 [512], replicated, may hold values from 0.5 to 1.5
- ln1_offset: float32 [512], replicated, may hold values from -1.5 to 1.5
- query_weight: bfloat16 [512, 512], P('dp', 'head'), may hold values from -0.375 to 0.375
- query_bias: float32 [512], replicated, may hold values from -1.5 to 1.5
- key_weight: bfloat16 [512, 512], P('dp', 'head'), may hold values from -0.25 to 0.25
- value_weight: bfloat16 [512, 512], P('dp', 'head'), may hold values from -0.25 to 0.25
- value_bias: float32 [512], replicated, may hold values from -1.5 to 1.5
- out_weight: bfloat16 [512, 512], P('head', 'dp'), may hold values from -2.5 to 2.5
- out_bias: float32 [512], replicated, may hold values from -1.5 to 1.5
- ln2_gain: float32 [512], replicated, may hold values from 0.5 to 1.5
- ln2_offset: float32 [512], replicated, may hold values from -1.5 to 1.5
- up_weight: bfloat16 [512, 2048], P(None, ('dp', 'head')), may hold values from -0.25 to 0.25
- up_bias: float32 [2048], replicated, may hold values from -1.5 to 1.5
- down_weight: bfloat16 [2048, 512], P(('dp', 'head')), may hold values from -0.125 to 0.125
- down_bias: float32 [512], replicated, may hold values from -1.5 to 1.5
Outputs:
- output: bfloat16 [48000, 512], P(('dp', 'head'))
- grad_frames: bfloat16 [48000, 512], P(('dp', 'head'))
- grad_ln1_gain: float32 [512], replicated
- grad_ln1_offset: float32 [512], replicated
- grad_query_weight: float32 [512, 512], P('dp', 'head')
- grad_query_bias: float32 [512], replicated
- grad_key_weight: float32 [512, 512], P('dp', 'head')
- grad_value_weight: float32 [512, 512], P('dp', 'head')
- grad_value_bias: float32 [512], replicated
- grad_out_weight: float32 [512, 512], P('head', 'dp')
- grad_out_bias: float32 [512], replicated
- grad_ln2_gain: float32 [512], replicated
- grad_ln2_offset: float32 [512], replicated
- grad_up_weight: float32 [512, 2048], P(None, ('dp', 'head'))
- grad_up_bias: float32 [2048], replicated
- grad_down_weight: float32 [2048, 512], P(('dp', 'head'))
- grad_down_bias: float32 [512], replicated
The draws below stay inside these ranges and needn't reach their ends.
Inputs may be any that keep to these rules, and one draw needn't show every extreme that they name: `window_live`: on each index of dp the first slots of its 2 hold windows (1) and the rest are empty (0); at least half of them hold windows, and some index of dp has all 2 full.
All inputs are finite; a program needn't handle non-finite values.
Results may differ from the reference program's by a relative error of at most 0.012.
The reference program's roundings to bfloat16 on the way count: a program that leaves them out, or rounds other values in their place, can miss the bound.
Values may be sent and summed in bfloat16 or wider, within the bound.
No kernel may reach another device: no remote copies, remote signals or barrier semaphores. Data moves between devices by JAX's collectives and lax.ppermute only.
A program may use at most 256 MiB of HBM per device.

```python
import math
import jax
import jax.numpy as jnp
import numpy as np
from jax import lax

D = 512
HEADS = 8
FF = 2048
FRAMES = 1500
LANGS = 99
TASKS = 2
SLOTS = 2
HEAD_DIM = 64
WINDOWS = 32
TOTAL_FRAMES = 48000


def draw_window_live(key, part):
    devices_dp = WINDOWS // SLOTS
    first_key, second_key = jax.random.split(jax.random.fold_in(key, 11))
    filled = jax.random.randint(first_key, (devices_dp,), SLOTS // 2, SLOTS + 1)
    busiest = jax.random.randint(second_key, (), 0, devices_dp)
    filled = jnp.where(jnp.arange(devices_dp) == busiest, SLOTS, filled)
    positions = jnp.arange(SLOTS)
    return (positions[None, :] < filled[:, None]).astype(jnp.int32).reshape(-1)


def touch_ends(values, rng, low, high):
    shape = values.shape
    place = [jax.random.randint(jax.random.fold_in(rng, axis), (), 0, shape[axis]) for axis in range(len(shape))]
    values = values.at[tuple(place)].set(low)
    longest = shape.index(max(shape))
    place[longest] = (place[longest] + 1) % shape[longest]
    return values.at[tuple(place)].set(high)


def block_levels(rng, dims, pieces, low, high):
    level = 1.0
    for axis_at, parts in pieces:
        steps = jax.random.uniform(jax.random.fold_in(jax.random.fold_in(rng, 6), axis_at), (parts,), jnp.float32, low / len(pieces), high / len(pieces))
        level = level * jnp.repeat(jnp.exp(steps), dims[axis_at] // parts).reshape((-1,) + (1,) * (len(dims) - 1 - axis_at))
    return level


def rank_bounds(amount, lean):
    portions = [(1 << 20) // math.isqrt(rank ** lean) + 1 for rank in range(1, amount + 1)]
    width = 1 + sum(portions) // (1 << 30)
    return np.cumsum(np.array([max(1, weight // width) for weight in portions]))


def ranked_ids(stream_key, shape, count, lean):
    grid = rank_bounds(count, lean)
    ticket = jax.random.randint(jax.random.fold_in(stream_key, 1), shape, 0, int(grid[count - 1]))
    standing = jnp.searchsorted(jnp.asarray(grid, jnp.int32), ticket, side="right")
    return jax.random.permutation(jax.random.fold_in(stream_key, 2), count)[standing].astype(jnp.int32)


def bell_draw(rng, dims, scale, limit, shards=(), kind=jnp.bfloat16):
    entries = scale * jax.random.normal(rng, dims, jnp.float32)
    if shards:
        entries = entries * block_levels(rng, dims, shards, -0.22, 0.18)
    return jnp.clip(entries, -limit, limit).astype(kind)


def setup_inputs(seed: int = 0) -> dict:
    streams_of = jax.random.split(jax.random.key(seed), 21)
    return {
        "frames": bell_draw(streams_of[0], (TOTAL_FRAMES, D), 1.0, 6.0, ((0, 32),)),
        "cotangent": bell_draw(streams_of[1], (TOTAL_FRAMES, D), 1.0, 6.0, ((0, 32),)),
        "window_live": draw_window_live(jax.random.fold_in(streams_of[20], 71), 0),
        "language": touch_ends(ranked_ids(streams_of[3], (WINDOWS,), LANGS, 2), jax.random.fold_in(streams_of[3], 3), 0, LANGS - 1).astype(jnp.int32),
        "task": touch_ends(jax.random.randint(streams_of[4], (WINDOWS,), 0, TASKS), jax.random.fold_in(streams_of[4], 1), 0, TASKS - 1).astype(jnp.int32),
        "ln1_gain": jnp.clip(1.0 + 0.1 * jax.random.normal(streams_of[5], (D,), jnp.float32), 0.5, 1.5),
        "ln1_offset": bell_draw(streams_of[6], (D,), 0.3, 1.5, (), jnp.float32),
        "query_weight": bell_draw(streams_of[7], (D, D), (D // 2) ** -0.5, 0.375, ((0, 16), (1, 2))),
        "query_bias": bell_draw(streams_of[8], (D,), 0.3, 1.5, (), jnp.float32),
        "key_weight": bell_draw(streams_of[9], (D, D), D ** -0.5, 0.25, ((0, 16), (1, 2))),
        "value_weight": bell_draw(streams_of[10], (D, D), D ** -0.5, 0.25, ((0, 16), (1, 2))),
        "value_bias": bell_draw(streams_of[11], (D,), 0.3, 1.5, (), jnp.float32),
        "out_weight": bell_draw(streams_of[12], (D, D), (D * 16 // FRAMES) ** -0.5, 2.5, ((0, 2), (1, 16))),
        "out_bias": bell_draw(streams_of[13], (D,), 0.3, 1.5, (), jnp.float32),
        "ln2_gain": jnp.clip(1.0 + 0.1 * jax.random.normal(streams_of[14], (D,), jnp.float32), 0.5, 1.5),
        "ln2_offset": bell_draw(streams_of[15], (D,), 0.3, 1.5, (), jnp.float32),
        "up_weight": bell_draw(streams_of[16], (D, FF), D ** -0.5, 0.25, ((1, 32),)),
        "up_bias": bell_draw(streams_of[17], (FF,), 0.3, 1.5, (), jnp.float32),
        "down_weight": bell_draw(streams_of[18], (FF, D), FF ** -0.5, 0.125, ((0, 32),)),
        "down_bias": bell_draw(streams_of[19], (D,), 0.3, 1.5, (), jnp.float32),
    }


@jax.custom_vjp
def low(v):
    return lax.optimization_barrier(v.astype(jnp.bfloat16)).astype(jnp.float32)

@jax.custom_vjp
def low_back(v):
    return v

def low_keep(v):
    return (low(v), None)

def low_pass(kept, grad):
    return (grad,)

def back_keep(v):
    return (v, None)

def back_low(kept, grad):
    return (low(grad),)
low.defvjp(low_keep, low_pass)
low_back.defvjp(back_keep, back_low)
highest = lax.Precision.HIGHEST

def matmul(first_mat, second_mat):
    return jnp.dot(first_mat, second_mat, precision=highest)

def layer_norm(values, gain_vec, offset_vec):
    center = lax.optimization_barrier(jnp.mean(values, axis=-1, keepdims=True))
    centred = values - center
    spread = lax.optimization_barrier(jnp.mean(centred * centred, axis=-1, keepdims=True))
    return centred * lax.rsqrt(spread + 1e-05) * gain_vec + offset_vec

def window_weights(window_live, language, task):
    groups = language * TASKS + task
    labels = jnp.arange(LANGS * TASKS, dtype=jnp.int32)
    matches = groups[:, None] == labels[None, :]
    live_float = window_live.astype(jnp.float32)
    counts = lax.optimization_barrier(jnp.sum(jnp.where(matches, live_float[:, None], 0.0), axis=0))
    present = jnp.sum((counts > 0.5).astype(jnp.float32))
    own_count = lax.optimization_barrier(jnp.sum(jnp.where(matches, counts[None, :], 0.0), axis=1))
    return live_float * jnp.sum(live_float) / (present * jnp.maximum(own_count, 1.0))

def layer(params, inputs):
    ln1_gain, ln1_offset, query_mat, query_vec, key_mat, value_mat, value_vec, out_mat, out_vec, ln2_gain, ln2_offset, up_mat, up_vec, down_mat, down_vec = params
    normed = low(layer_norm(inputs, ln1_gain, ln1_offset))
    queries = low(low_back(matmul(normed, query_mat) + query_vec)).reshape(FRAMES, HEADS, HEAD_DIM)
    keys_all = low(low_back(matmul(normed, key_mat))).reshape(FRAMES, HEADS, HEAD_DIM)
    values_all = low(low_back(matmul(normed, value_mat) + value_vec)).reshape(FRAMES, HEADS, HEAD_DIM)
    scores = low_back(jnp.einsum('qhd,khd->hqk', queries, keys_all, precision=highest) * 0.125)
    attn_probs = low(jax.nn.softmax(scores, axis=-1))
    context = jnp.einsum('hqk,khd->qhd', attn_probs, values_all, precision=highest)
    context = low(low_back(context)).reshape(FRAMES, D)
    hidden = inputs + low_back(matmul(context, out_mat) + out_vec)
    normed_two = low(layer_norm(hidden, ln2_gain, ln2_offset))
    pre_act = low_back(matmul(normed_two, up_mat) + up_vec)
    activated = low(jax.nn.gelu(pre_act, approximate=False))
    return hidden + low_back(matmul(activated, down_mat) + down_vec)

def reference(frames, cotangent, window_live, language, task, ln1_gain, ln1_offset, query_weight, query_bias, key_weight, value_weight, value_bias, out_weight, out_bias, ln2_gain, ln2_offset, up_weight, up_bias, down_weight, down_bias):
    params = tuple((member.astype(jnp.float32) for member in (ln1_gain, ln1_offset, query_weight, query_bias, key_weight, value_weight, value_bias, out_weight, out_bias, ln2_gain, ln2_offset, up_weight, up_bias, down_weight, down_bias)))
    per_window = window_weights(window_live, language, task)
    inputs = (frames.reshape(WINDOWS, FRAMES, D), cotangent.reshape(WINDOWS, FRAMES, D), per_window, window_live.astype(jnp.float32))

    def window_step(carry, record):
        frame_win, cot_win, weight_win, live_win = record
        result, backward = jax.vjp(layer, params, frame_win.astype(jnp.float32))
        grad_params, grad_input = backward(cot_win.astype(jnp.float32) * weight_win)
        carry = tuple((running + update for running, update in zip(carry, grad_params)))
        return (carry, ((result * live_win).astype(jnp.bfloat16), grad_input.astype(jnp.bfloat16)))
    start_carry = tuple((jnp.zeros(member.shape, jnp.float32) for member in params))
    grads, (outputs, grad_frames) = lax.scan(window_step, start_carry, inputs)
    return (outputs.reshape(TOTAL_FRAMES, D), grad_frames.reshape(TOTAL_FRAMES, D), grads[0], grads[1], grads[2], grads[3], grads[4], grads[5], grads[6], grads[7], grads[8], grads[9], grads[10], grads[11], grads[12], grads[13], grads[14])
```

```python
import functools

import jax
import jax.numpy as jnp
from jax import lax
from jax.experimental import pallas as pl
from jax.experimental.pallas import tpu as pltpu
from jax.sharding import PartitionSpec as P

FRAMES = 1500
LANGS = 99
TASKS = 2
SLOTS = 2
HEAD_DIM = 64


def layer_norm(values, gain_vec, offset_vec):
    center = jnp.mean(values, axis=-1, keepdims=True)
    centred = values - center
    spread = jnp.mean(centred * centred, axis=-1, keepdims=True)
    return centred * lax.rsqrt(spread + 1e-05) * gain_vec + offset_vec


def gelu_exact(values):
    return jax.nn.gelu(values, approximate=False)


def contract(first_mat, second_mat):
    return lax.dot_general(
        first_mat, second_mat, (((0,), (0,)), ((), ())), preferred_element_type=jnp.float32
    )


def times_t(first_mat, second_mat):
    return lax.dot_general(
        first_mat, second_mat, (((1,), (1,)), ((), ())), preferred_element_type=jnp.float32
    )


def window_weights(window_live, language, task):
    groups = language * TASKS + task
    labels = jnp.arange(LANGS * TASKS, dtype=jnp.int32)
    matches = groups[:, None] == labels[None, :]
    live_float = window_live.astype(jnp.float32)
    counts = jnp.sum(jnp.where(matches, live_float[:, None], 0.0), axis=0)
    present = jnp.sum((counts > 0.5).astype(jnp.float32))
    own_count = jnp.sum(jnp.where(matches, counts[None, :], 0.0), axis=1)
    return live_float * jnp.sum(live_float) / (present * jnp.maximum(own_count, 1.0))


def window_scores(queries, keys_all):
    return jnp.einsum("qhd,khd->hqk", queries, keys_all, preferred_element_type=jnp.float32) * 0.125


def attend_forward(record):
    queries, keys_all, values_all = record
    scores = window_scores(queries, keys_all)
    highest_score = jnp.max(scores, axis=-1, keepdims=True)
    expo = jnp.exp(scores - highest_score)
    totals = jnp.sum(expo, axis=-1, keepdims=True)
    attn_probs = (expo / totals).astype(jnp.bfloat16)
    context = jnp.einsum("hqk,khd->qhd", attn_probs, values_all, preferred_element_type=jnp.float32)
    return (context.astype(jnp.bfloat16), (highest_score + jnp.log(totals))[..., 0])


def attend_backward(record):
    queries, keys_all, values_all, log_totals, grad_context = record
    scores = window_scores(queries, keys_all)
    attn_probs = jnp.exp(scores - log_totals[..., None])
    grad_probs = jnp.einsum(
        "qhd,khd->hqk", grad_context, values_all, preferred_element_type=jnp.float32
    )
    grad_values = jnp.einsum(
        "hqk,qhd->khd",
        attn_probs.astype(jnp.bfloat16),
        grad_context,
        preferred_element_type=jnp.float32,
    )
    row_delta = jnp.sum(grad_probs * attn_probs, axis=-1, keepdims=True)
    grad_scores = (attn_probs * (grad_probs - row_delta)).astype(jnp.bfloat16)
    grad_queries = (
        jnp.einsum("hqk,khd->qhd", grad_scores, keys_all, preferred_element_type=jnp.float32)
        * 0.125
    )
    grad_keys = (
        jnp.einsum("hqk,qhd->khd", grad_scores, queries, preferred_element_type=jnp.float32) * 0.125
    )
    return (
        grad_queries.astype(jnp.bfloat16),
        grad_keys.astype(jnp.bfloat16),
        grad_values.astype(jnp.bfloat16),
    )


def on_device(
    frames,
    cotangent,
    window_live,
    language,
    task,
    ln1_gain,
    ln1_offset,
    query_weight,
    query_bias,
    key_weight,
    value_weight,
    value_bias,
    out_weight,
    out_bias,
    ln2_gain,
    ln2_offset,
    up_weight,
    up_bias,
    down_weight,
    down_bias,
):
    local_rows = frames.shape[0]
    head_index = lax.axis_index("head")
    data_index = lax.axis_index("dp")
    per_window = window_weights(window_live, language, task)
    slot_ids = (
        head_index * local_rows + jnp.arange(local_rows, dtype=jnp.int32)
    ) // FRAMES + data_index * SLOTS
    window_ids = jnp.arange(per_window.shape[0], dtype=jnp.int32)
    frame_match = slot_ids[:, None] == window_ids[None, :]
    frame_weight = jnp.sum(jnp.where(frame_match, per_window[None, :], 0.0), axis=1)
    frame_live = jnp.sum(
        jnp.where(frame_match, window_live.astype(jnp.float32)[None, :], 0.0), axis=1
    )
    inputs = frames.astype(jnp.float32)
    normed, ln1_back = jax.vjp(layer_norm, inputs, ln1_gain, ln1_offset)
    normed_low = normed.astype(jnp.bfloat16)
    query_head, key_head, value_head, out_head = (
        lax.all_gather(query_weight, "dp", axis=0, tiled=True),
        lax.all_gather(key_weight, "dp", axis=0, tiled=True),
        lax.all_gather(value_weight, "dp", axis=0, tiled=True),
        lax.all_gather(out_weight, "dp", axis=1, tiled=True),
    )
    head_width = query_head.shape[1]
    local_heads = head_width // HEAD_DIM
    joint_weight = jnp.concatenate([query_head, key_head, value_head], axis=1)
    joint_bias = jnp.concatenate(
        [
            lax.dynamic_slice_in_dim(query_bias, head_index * head_width, head_width),
            jnp.zeros((head_width,), jnp.float32),
            lax.dynamic_slice_in_dim(value_bias, head_index * head_width, head_width),
        ]
    )
    normed_all = lax.all_gather(normed_low, "head", axis=0, tiled=True)
    projected = (
        jnp.dot(normed_all, joint_weight, preferred_element_type=jnp.float32) + joint_bias
    ).astype(jnp.bfloat16)
    shaped = projected.reshape(-1, FRAMES, 3, local_heads, HEAD_DIM)
    queries = shaped[:, :, 0]
    keys_all = shaped[:, :, 1]
    values_all = shaped[:, :, 2]
    context, log_totals = lax.map(attend_forward, (queries, keys_all, values_all))
    context_flat = context.reshape(-1, head_width)
    branch = lax.psum_scatter(
        jnp.dot(context_flat, out_head, preferred_element_type=jnp.float32),
        "head",
        scatter_dimension=0,
        tiled=True,
    )
    hidden = inputs + branch + out_bias
    normed_two, ln2_back = jax.vjp(layer_norm, hidden, ln2_gain, ln2_offset)
    normed_two_low = normed_two.astype(jnp.bfloat16)
    up_full, down_full = (
        lax.all_gather(up_weight, ("dp", "head"), axis=1, tiled=True),
        lax.all_gather(down_weight, ("dp", "head"), axis=0, tiled=True),
    )
    pre_act = jnp.dot(normed_two_low, up_full, preferred_element_type=jnp.float32) + up_bias
    activated, gelu_back = jax.vjp(gelu_exact, pre_act)
    activated_low = activated.astype(jnp.bfloat16)
    result = (
        hidden + jnp.dot(activated_low, down_full, preferred_element_type=jnp.float32) + down_bias
    )
    output = (result * frame_live[:, None]).astype(jnp.bfloat16)
    grad_result = cotangent.astype(jnp.float32) * frame_weight[:, None]
    grad_two = grad_result.astype(jnp.bfloat16)
    grad_down = contract(activated_low, grad_two)
    grad_down_bias = jnp.sum(grad_two.astype(jnp.float32), axis=0)
    grad_activated = times_t(grad_two, down_full)
    grad_pre = gelu_back(grad_activated)[0].astype(jnp.bfloat16)
    grad_up = contract(normed_two_low, grad_pre)
    grad_up_bias = jnp.sum(grad_pre.astype(jnp.float32), axis=0)
    grad_normed_two = times_t(grad_pre, up_full)
    grad_hidden_ln, grad_ln2_gain, grad_ln2_offset = ln2_back(grad_normed_two)
    grad_hidden = grad_result + grad_hidden_ln
    grad_branch = grad_hidden.astype(jnp.bfloat16)
    grad_out_bias = jnp.sum(grad_branch.astype(jnp.float32), axis=0)
    branch_all = lax.all_gather(grad_branch, "head", axis=0, tiled=True)
    grad_context = times_t(branch_all, out_head).astype(jnp.bfloat16)
    grad_out_head = contract(context_flat, branch_all)
    grad_context_win = grad_context.reshape(-1, FRAMES, local_heads, HEAD_DIM)
    grad_queries, grad_keys, grad_values = lax.map(
        attend_backward, (queries, keys_all, values_all, log_totals, grad_context_win)
    )
    grad_joint = jnp.concatenate(
        [
            grad_queries.reshape(-1, head_width),
            grad_keys.reshape(-1, head_width),
            grad_values.reshape(-1, head_width),
        ],
        axis=1,
    )
    grad_joint_weight = contract(normed_all, grad_joint)
    joint_sums = jnp.sum(grad_joint.astype(jnp.float32), axis=0)
    empty_vec = jnp.zeros((query_bias.shape[0],), jnp.float32)
    grad_query_bias = lax.dynamic_update_slice(
        empty_vec, joint_sums[:head_width], (head_index * head_width,)
    )
    grad_value_bias = lax.dynamic_update_slice(
        empty_vec, joint_sums[2 * head_width :], (head_index * head_width,)
    )
    grad_normed = lax.psum_scatter(
        times_t(grad_joint, joint_weight), "head", scatter_dimension=0, tiled=True
    )
    grad_inputs_ln, grad_ln1_gain, grad_ln1_offset = ln1_back(grad_normed)
    grad_frames = (grad_hidden + grad_inputs_ln).astype(jnp.bfloat16)
    grad_query_w, grad_key_w, grad_value_w, grad_out_w = (
        lax.psum_scatter(grad_joint_weight[:, :head_width], "dp", scatter_dimension=0, tiled=True),
        lax.psum_scatter(
            grad_joint_weight[:, head_width : 2 * head_width], "dp", scatter_dimension=0, tiled=True
        ),
        lax.psum_scatter(
            grad_joint_weight[:, 2 * head_width :], "dp", scatter_dimension=0, tiled=True
        ),
        lax.psum_scatter(grad_out_head, "dp", scatter_dimension=1, tiled=True),
    )
    grad_up_w, grad_down_w = (
        lax.psum_scatter(grad_up, ("dp", "head"), scatter_dimension=1, tiled=True),
        lax.psum_scatter(grad_down, ("dp", "head"), scatter_dimension=0, tiled=True),
    )
    (
        sum_ln1_gain,
        sum_ln1_offset,
        sum_query_bias,
        sum_value_bias,
        sum_out_bias,
        sum_ln2_gain,
        sum_ln2_offset,
        sum_up_bias,
        sum_down_bias,
    ) = lax.psum(
        (
            grad_ln1_gain,
            grad_ln1_offset,
            grad_query_bias,
            grad_value_bias,
            grad_out_bias,
            grad_ln2_gain,
            grad_ln2_offset,
            grad_up_bias,
            grad_down_bias,
        ),
        ("dp", "head"),
    )
    return (
        output,
        grad_frames,
        sum_ln1_gain,
        sum_ln1_offset,
        grad_query_w,
        sum_query_bias,
        grad_key_w,
        grad_value_w,
        sum_value_bias,
        grad_out_w,
        sum_out_bias,
        sum_ln2_gain,
        sum_ln2_offset,
        grad_up_w,
        sum_up_bias,
        grad_down_w,
        sum_down_bias,
    )


LANES = 128
PADDED = 1536
LOG2E = 1.4426950408889634
MASKED = -30000.0
F32 = jnp.float32
BF16 = jnp.bfloat16
VMEM_BYTES = 58 << 20


def dot_on(first_mat, second_mat, first_dim, second_dim):
    return lax.dot_general(
        first_mat,
        second_mat,
        (((first_dim,), (second_dim,)), ((), ())),
        preferred_element_type=F32,
    )


def params(cost):
    return dict(
        compiler_params=pltpu.CompilerParams(vmem_limit_bytes=VMEM_BYTES),
        cost_estimate=pl.CostEstimate(flops=cost, bytes_accessed=1 << 20, transcendentals=0),
    )


def whole(shape):
    return pl.BlockSpec(shape, lambda *_: (0,) * len(shape), pipeline_mode=pl.Buffered(1))


def norm_kernel(x_ref, gain_ref, offset_ref, n_ref, nt_ref):
    rows = x_ref.shape[0]
    row = pl.program_id(0) * rows + lax.broadcasted_iota(jnp.int32, x_ref.shape, 0)
    values = jnp.where(row < FRAMES, x_ref[...].astype(F32), 0.0)
    centred = values - jnp.mean(values, axis=1, keepdims=True)
    spread = jnp.mean(centred * centred, axis=1, keepdims=True)
    normed = centred * lax.rsqrt(spread + 1e-05) * gain_ref[...] + offset_ref[...]
    n_ref[...] = normed.astype(BF16)
    nt_ref[...] = normed.T.astype(BF16)


def first_norm(frames, gain, offset):
    width = frames.shape[1]
    tile = 512
    vec = pl.BlockSpec((1, width), lambda i: (0, 0))
    return pl.pallas_call(
        norm_kernel,
        grid=(PADDED // tile,),
        in_specs=[pl.BlockSpec((tile, width), lambda i: (i, 0)), vec, vec],
        out_specs=[
            pl.BlockSpec((tile, width), lambda i: (i, 0)),
            pl.BlockSpec((width, tile), lambda i: (0, i)),
        ],
        out_shape=[
            jax.ShapeDtypeStruct((PADDED, width), BF16),
            jax.ShapeDtypeStruct((width, PADDED), BF16),
        ],
        name="first_norm",
        **params(3 << 30),
    )(frames, gain.reshape(1, -1), offset.reshape(1, -1))


def project_kernel(pos_ref, n_ref, pieces_ref, bias_ref, q_ref, k_ref, v_ref, w_ref):
    count, rows3, half = pieces_ref.shape
    rows = rows3 // 3

    @pl.when(pl.program_id(0) == 0)
    def _():
        for d in range(count):
            piece = pieces_ref[d ^ pos_ref[0]]
            for j in range(3):
                w_ref[j, d * rows : (d + 1) * rows, :] = piece[j * rows : (j + 1) * rows, :]

    for j, out in enumerate((q_ref, k_ref, v_ref)):
        out[...] = (dot_on(n_ref[...], w_ref[j], 1, 0) + bias_ref[j]).astype(BF16)


def project(pos, normed, pieces, bias):
    width = normed.shape[1]
    half = pieces.shape[2]
    tile = 512
    block = pl.BlockSpec((tile, half), lambda i, *_: (i, 0))
    return pl.pallas_call(
        project_kernel,
        grid_spec=pltpu.PrefetchScalarGridSpec(
            num_scalar_prefetch=1,
            grid=(PADDED // tile,),
            in_specs=[
                pl.BlockSpec((tile, width), lambda i, *_: (i, 0)),
                whole(pieces.shape),
                whole((3, 1, half)),
            ],
            out_specs=[block] * 3 + [whole((3, width, half))],
        ),
        out_shape=[jax.ShapeDtypeStruct((PADDED, half), BF16)] * 3
        + [jax.ShapeDtypeStruct((3, width, half), BF16)],
        name="project",
        **params(4 << 30),
    )(pos, normed, pieces, bias)


def lane_masks(shape, h):
    lane = lax.broadcasted_iota(jnp.int32, shape, 1)
    if h == 0:
        return lane < HEAD_DIM, lane - HEAD_DIM
    return lane >= HEAD_DIM, jnp.where(lane < HEAD_DIM, lane, -1)


def split_three(values):
    high = values.astype(BF16).astype(F32)
    rest = values - high
    middle = rest.astype(BF16).astype(F32)
    return high, middle, rest - middle


def spread_three(extra, values, base):
    high, middle, small = split_three(values)
    return jnp.where(
        extra == 0, high, jnp.where(extra == 1, middle, jnp.where(extra == 2, small, base))
    )


def store_keys(k_ref, keys_ref, h):
    keys = k_ref[...].astype(F32)
    own, extra = lane_masks(keys.shape, h)
    row = lax.broadcasted_iota(jnp.int32, keys.shape, 0)
    ones = (extra >= 0) & (extra < 3)
    fill = jnp.where(ones, 1.0, jnp.where((extra == 3) & (row >= FRAMES), MASKED, 0.0))
    keys_ref[h, :, 0:LANES] = jnp.where(own, keys, fill).astype(BF16)
    keys_ref[h, :, LANES:] = jnp.where(own, keys, 0.0).astype(BF16)


def wide_queries(scaled, h, log_totals):
    own, extra = lane_masks(scaled.shape, h)
    high = scaled.astype(BF16).astype(F32)
    fill = jnp.where(extra == 3, 1.0, 0.0)
    if log_totals is not None:
        fill = spread_three(extra, -log_totals, fill)
    return jnp.concatenate(
        [
            jnp.where(own, high, fill).astype(BF16),
            jnp.where(own, scaled - high, 0.0).astype(BF16),
        ],
        axis=1,
    )


def forward_kernel(q_ref, k_ref, v_ref, c_ref, lse_ref, keys_ref, vt_ref):
    @pl.when(pl.program_id(1) == 0)
    def _():
        flipped = v_ref[...].astype(F32).T.astype(BF16)
        shape = (vt_ref.shape[1] - HEAD_DIM, flipped.shape[1])
        ones = jnp.where(lax.broadcasted_iota(jnp.int32, shape, 0) == 0, 1.0, 0.0).astype(BF16)
        for h in (0, 1):
            store_keys(k_ref, keys_ref, h)
            vt_ref[h, 0:HEAD_DIM, :] = flipped[HEAD_DIM * h : HEAD_DIM * (h + 1), :]
            vt_ref[h, HEAD_DIM:, :] = ones

    scaled = q_ref[...].astype(F32) * (LOG2E * 0.125)
    contexts, totals = [], []
    for h in (0, 1):
        scores = dot_on(keys_ref[h], wide_queries(scaled, h, None), 1, 1)
        highest = jnp.max(scores, axis=0, keepdims=True)
        probs = jnp.exp2(scores - highest).astype(BF16)
        summed = dot_on(vt_ref[h], probs, 1, 0)
        total = summed[HEAD_DIM : HEAD_DIM + 1, :]
        contexts.append(summed[0:HEAD_DIM, :] / total)
        log_total = highest + jnp.log2(total)
        totals.append(jnp.broadcast_to(log_total, (HEAD_DIM, log_total.shape[1])))
    c_ref[...] = jnp.concatenate(contexts, axis=0).T.astype(BF16)
    lse_ref[...] = jnp.concatenate(totals, axis=0).T


def attend_forward_fast(q, k, v):
    rows, width = q.shape
    tile = 768
    block = pl.BlockSpec((tile, LANES), lambda p, i: (i, p))
    full = pl.BlockSpec((rows, LANES), lambda p, i: (0, p))
    return pl.pallas_call(
        forward_kernel,
        grid=(width // LANES, rows // tile),
        in_specs=[block, full, full],
        out_specs=[block, block],
        out_shape=[
            jax.ShapeDtypeStruct((rows, width), BF16),
            jax.ShapeDtypeStruct((rows, width), F32),
        ],
        scratch_shapes=[
            pltpu.VMEM((2, rows, 2 * LANES), BF16),
            pltpu.VMEM((2, HEAD_DIM + 16, rows), BF16),
        ],
        name="attend_forward",
        **params(17 << 30),
    )(q, k, v)


def backward_kernel(
    q_ref, k_ref, v_ref, lse_ref, c_ref, g_ref, dq_ref, dk_ref, dv_ref, keys_ref, vals_ref, kt_ref, acck, accv
):
    step = pl.program_id(1)

    @pl.when(step == 0)
    def _():
        for h in (0, 1):
            store_keys(k_ref, keys_ref, h)
            values = v_ref[...].astype(F32)
            own, _ = lane_masks(values.shape, h)
            vals_ref[h] = jnp.where(own, values, 1.0).astype(BF16)
        kt_ref[...] = k_ref[...].astype(F32).T.astype(BF16)
        acck[...] = jnp.zeros_like(acck)
        accv[...] = jnp.zeros_like(accv)

    plain = q_ref[...].astype(F32)
    scaled = plain * (LOG2E * 0.125)
    grads = g_ref[...].astype(F32)
    products = grads * c_ref[...].astype(F32)
    log_totals = pltpu.roll(lse_ref[...], HEAD_DIM, 1)
    probs, diffs, queries, outers, flipped = [], [], [], [], []
    for h in (0, 1):
        own, extra = lane_masks(grads.shape, h)
        row_delta = jnp.sum(jnp.where(own, products, 0.0), axis=1, keepdims=True)
        wide = jnp.where(own, grads, spread_three(extra, -row_delta, 0.0)).astype(BF16)
        prob = jnp.exp2(dot_on(keys_ref[h], wide_queries(scaled, h, log_totals), 1, 1))
        diff = (prob * dot_on(vals_ref[h], wide, 1, 1)).astype(BF16)
        probs.append(prob.astype(BF16))
        diffs.append(diff)
        outers.append(jnp.where(own, grads, 0.0).astype(BF16))
        queries.append(jnp.where(own, plain, 0.0).astype(BF16))
        flipped.append(dot_on(kt_ref[HEAD_DIM * h : HEAD_DIM * (h + 1), :], diff, 1, 0))
    accv[...] += dot_on(probs[0], outers[0], 1, 0) + dot_on(probs[1], outers[1], 1, 0)
    acck[...] += dot_on(diffs[0], queries[0], 1, 0) + dot_on(diffs[1], queries[1], 1, 0)
    dq_ref[...] = (jnp.concatenate(flipped, axis=0) * 0.125).T.astype(BF16)

    @pl.when(step == pl.num_programs(1) - 1)
    def _():
        dk_ref[...] = (acck[...] * 0.125).astype(BF16)
        dv_ref[...] = accv[...].astype(BF16)


def attend_backward_fast(q, k, v, lse, context, grads):
    rows, width = q.shape
    tile = 512
    block = pl.BlockSpec((tile, LANES), lambda p, i: (i, p))
    full = pl.BlockSpec((rows, LANES), lambda p, i: (0, p))
    return pl.pallas_call(
        backward_kernel,
        grid=(width // LANES, rows // tile),
        in_specs=[block, full, full, block, block, block],
        out_specs=[block, full, full],
        out_shape=[jax.ShapeDtypeStruct((rows, width), BF16)] * 3,
        scratch_shapes=[
            pltpu.VMEM((2, rows, 2 * LANES), BF16),
            pltpu.VMEM((2, rows, LANES), BF16),
            pltpu.VMEM((LANES, rows), BF16),
            pltpu.VMEM((rows, LANES), F32),
            pltpu.VMEM((rows, LANES), F32),
        ],
        name="attend_backward",
        **params(29 << 30),
    )(q, k, v, lse, context, grads)


def middle_kernel(
    place_ref,
    weight_ref,
    cown_ref,
    coth_ref,
    x_ref,
    cot_ref,
    pieces_ref,
    vecs_ref,
    upb_ref,
    out_ref,
    gown_ref,
    goth_ref,
    gh_ref,
    send_ref,
    keep_ref,
    vec_ref,
    up_t,
    up_n,
    down_n,
    down_t,
    out_t,
    upb_t,
    acc_up,
    acc_down,
    acc_out,
    acc_upb,
    acc_vec,
):
    step = pl.program_id(0)
    core, side = place_ref[0], place_ref[1]
    devices, piece_rows, half = pieces_ref.shape
    ff = piece_rows // 2 // 2 - half // 32
    ff = 64
    ow = piece_rows - 4 * ff
    width = 2 * half
    hidden_all = devices * ff
    chunk = 512
    chunks = hidden_all // chunk

    @pl.when(step == 0)
    def _():
        for d in range(devices):
            rows = slice(d * ff, (d + 1) * ff)
            down_n[rows, 0:half] = pieces_ref[d, 0:ff, :]
            down_n[rows, half:] = pieces_ref[d, ff : 2 * ff, :]
            up_t[rows, 0:half] = pieces_ref[d, 2 * ff : 3 * ff, :]
            up_t[rows, half:] = pieces_ref[d, 3 * ff : 4 * ff, :]
        for d in range(devices // 2):
            for j in (0, 1):
                out_t[j, d * ow : (d + 1) * ow, :] = pieces_ref[2 * d + (side ^ j), 4 * ff :, :]
        for j in range(chunks):
            rows = slice(j * chunk, (j + 1) * chunk)
            up_n[:, rows] = up_t[rows, :].T
            down_t[:, rows] = down_n[rows, :].T
            upb_t[rows, :] = jnp.broadcast_to(upb_ref[:, rows], (LANES, chunk)).T
        acc_up[...] = jnp.zeros_like(acc_up)
        acc_down[...] = jnp.zeros_like(acc_down)
        acc_out[...] = jnp.zeros_like(acc_out)
        acc_upb[...] = jnp.zeros_like(acc_upb)
        acc_vec[...] = jnp.zeros_like(acc_vec)

    tile = x_ref.shape[0]
    row = step * tile + lax.broadcasted_iota(jnp.int32, x_ref.shape, 0)
    real = row < FRAMES
    out_bias, gain, offset, down_bias = (vecs_ref[j : j + 1, :] for j in range(4))
    branch = dot_on(cown_ref[...], out_t[0], 1, 1) + dot_on(coth_ref[...], out_t[1], 1, 1)
    hidden = jnp.where(real, x_ref[...].astype(F32), 0.0) + branch + out_bias
    centred = hidden - jnp.mean(hidden, axis=1, keepdims=True)
    scale = lax.rsqrt(jnp.mean(centred * centred, axis=1, keepdims=True) + 1e-05)
    unit = centred * scale
    normed = (unit * gain + offset).astype(BF16)
    grad_result = jnp.where(real, cot_ref[...].astype(F32), 0.0) * weight_ref[0]
    grad_two = grad_result.astype(BF16)
    result_t = jnp.zeros((width, tile), F32)
    grad_normed_t = jnp.zeros((width, tile), F32)
    for j in range(chunks):
        rows = slice(j * chunk, (j + 1) * chunk)
        slots = slice(j * chunk // ff, (j + 1) * chunk // ff)
        pre = dot_on(up_t[rows, :], normed, 1, 1) + upb_t[rows, 0:1]
        bell = 0.5 + 0.5 * lax.erf(pre * 0.7071067811865476)
        slope = bell + pre * (jnp.exp2(pre * pre * (-0.5 * LOG2E)) * 0.3989422804014327)
        activated = (pre * bell).astype(BF16)
        result_t += dot_on(down_t[:, rows], activated, 1, 0)
        acc_down[slots] += dot_on(activated, grad_two, 1, 0).reshape(-1, ff, width)
        grad_pre_full = dot_on(down_n[rows, :], grad_two, 1, 1) * slope
        grad_pre = grad_pre_full.astype(BF16)
        rounded = grad_pre.astype(F32)
        partial = rounded[:, 0:LANES]
        for lanes in range(LANES, tile, LANES):
            partial += rounded[:, lanes : lanes + LANES]
        acc_upb[rows, :] += partial
        acc_up[slots] += dot_on(grad_pre, normed, 1, 0).reshape(-1, ff, width)
        grad_normed_t += dot_on(up_n[:, rows], grad_pre, 1, 0)
    result = hidden + result_t.T + down_bias
    out_ref[...] = (result * weight_ref[1]).astype(BF16)
    grad_normed = grad_normed_t.T
    lifted = grad_normed * gain
    mean_one = jnp.mean(lifted, axis=1, keepdims=True)
    mean_two = jnp.mean(lifted * unit, axis=1, keepdims=True)
    grad_hidden = grad_result + scale * (lifted - mean_one - unit * mean_two)
    gh_ref[...] = grad_hidden
    grad_branch = grad_hidden.astype(BF16)
    gown_ref[...] = dot_on(grad_branch, out_t[0], 1, 0).astype(BF16)
    goth_ref[...] = dot_on(grad_branch, out_t[1], 1, 0).astype(BF16)
    branch_t = grad_hidden.T.astype(BF16)
    acc_out[0] += dot_on(branch_t, cown_ref[...], 1, 0).reshape(-1, ow, half)
    acc_out[1] += dot_on(branch_t, coth_ref[...], 1, 0).reshape(-1, ow, half)
    for j, term in enumerate(
        (grad_branch.astype(F32), grad_normed * unit, grad_normed, grad_two.astype(F32))
    ):
        acc_vec[8 * j : 8 * j + 8, :] += jnp.sum(term.reshape(-1, 8, width), axis=0)

    @pl.when(step == pl.num_programs(0) - 1)
    def _():
        targets = devices // 2
        for ref, bit in ((keep_ref, core), (send_ref, 1 - core)):
            for t in range(targets):
                place, x = t // 2, t % 2
                at = t * piece_rows
                slot = place * 4 + bit * 2 + x
                ref[at : at + ff, :] = acc_down[slot, :, 0:half].astype(BF16)
                ref[at + ff : at + 2 * ff, :] = acc_down[slot, :, half:].astype(BF16)
                ref[at + 2 * ff : at + 3 * ff, :] = acc_up[slot, :, 0:half].astype(BF16)
                ref[at + 3 * ff : at + 4 * ff, :] = acc_up[slot, :, half:].astype(BF16)
                ref[at + 4 * ff : at + piece_rows, :] = acc_out[
                    side ^ x, place * 2 + bit
                ].astype(BF16)
        for j in range(4):
            total = jnp.sum(acc_vec[8 * j : 8 * j + 8, :], axis=0, keepdims=True)
            vec_ref[2 * j : 2 * j + 1, :] = total[:, 0:half]
            vec_ref[2 * j + 1 : 2 * j + 2, :] = total[:, half:]
        for j in range(chunks):
            total = jnp.sum(acc_upb[j * chunk : (j + 1) * chunk, :].T, axis=0, keepdims=True)
            for i in range(chunk // half):
                at = 8 + j * (chunk // half) + i
                vec_ref[at : at + 1, :] = total[:, i * half : (i + 1) * half]
        high = vec_ref[...].astype(BF16)
        send_ref[targets * piece_rows : targets * piece_rows + 16, :] = high
        send_ref[targets * piece_rows + 16 :, :] = (vec_ref[...] - high.astype(F32)).astype(BF16)


def middle(place, weight, cown, coth, frames, cotangent, pieces, vecs, up_bias):
    rows, half = cown.shape
    width = frames.shape[1]
    devices, piece_rows, _ = pieces.shape
    hidden_all = up_bias.shape[1]
    tile = 512
    ow = width // (devices // 2)
    ff = hidden_all // devices
    targets = devices // 2
    halfs = pl.BlockSpec((tile, half), lambda i, *_: (i, 0))
    wide = pl.BlockSpec((tile, width), lambda i, *_: (i, 0))
    return pl.pallas_call(
        middle_kernel,
        grid_spec=pltpu.PrefetchScalarGridSpec(
            num_scalar_prefetch=2,
            grid=(rows // tile,),
            in_specs=[
                halfs,
                halfs,
                wide,
                wide,
                whole(pieces.shape),
                whole(vecs.shape),
                whole(up_bias.shape),
            ],
            out_specs=[
                wide,
                halfs,
                halfs,
                wide,
                whole((targets * piece_rows + 32, half)),
                whole((targets * piece_rows, half)),
                whole((16, half)),
            ],
            scratch_shapes=[
                pltpu.VMEM((hidden_all, width), BF16),
                pltpu.VMEM((width, hidden_all), BF16),
                pltpu.VMEM((hidden_all, width), BF16),
                pltpu.VMEM((width, hidden_all), BF16),
                pltpu.VMEM((2, width, half), BF16),
                pltpu.VMEM((hidden_all, LANES), F32),
                pltpu.VMEM((devices, ff, width), F32),
                pltpu.VMEM((devices, ff, width), F32),
                pltpu.VMEM((2, width // ow, ow, half), F32),
                pltpu.VMEM((hidden_all, LANES), F32),
                pltpu.VMEM((32, width), F32),
            ],
        ),
        out_shape=[
            jax.ShapeDtypeStruct(frames.shape, BF16),
            jax.ShapeDtypeStruct((rows, half), BF16),
            jax.ShapeDtypeStruct((rows, half), BF16),
            jax.ShapeDtypeStruct((rows, width), F32),
            jax.ShapeDtypeStruct((targets * piece_rows + 32, half), BF16),
            jax.ShapeDtypeStruct((targets * piece_rows, half), BF16),
            jax.ShapeDtypeStruct((16, half), F32),
        ],
        name="middle",
        **params(35 << 30),
    )(place, weight, cown, coth, frames, cotangent, pieces, vecs, up_bias)


def weight_grad_kernel(nt_ref, q_ref, k_ref, v_ref, dw_ref, sums_ref):
    rows = dw_ref.shape[1]
    for j, ref in enumerate((q_ref, k_ref, v_ref)):
        grads = ref[...]
        dw_ref[j] = dot_on(nt_ref[...], grads, 1, 0).astype(BF16)
        sums_ref[j : j + 1, :] = jnp.sum(grads.astype(F32), axis=0, keepdims=True)


def weight_grads(nt, dq, dk, dv):
    width, rows = nt.shape
    half = dq.shape[1]
    return pl.pallas_call(
        weight_grad_kernel,
        out_shape=[
            jax.ShapeDtypeStruct((3, width, half), BF16),
            jax.ShapeDtypeStruct((8, half), F32),
        ],
        name="weight_grads",
        **params(4 << 30),
    )(nt, dq, dk, dv)


def input_grad_kernel(
    first, x_ref, q_ref, k_ref, v_ref, w_ref, *refs
):
    total = dot_on(q_ref[...], w_ref[0], 1, 1)
    total += dot_on(k_ref[...], w_ref[1], 1, 1)
    total += dot_on(v_ref[...], w_ref[2], 1, 1)
    if first:
        refs[0][...] = total
        return
    other_ref, gh_ref, gain_ref, gf_ref, vec_ref, acc = refs
    total += other_ref[...]
    step = pl.program_id(0)
    tile, width = x_ref.shape

    @pl.when(step == 0)
    def _():
        acc[...] = jnp.zeros_like(acc)

    row = step * tile + lax.broadcasted_iota(jnp.int32, x_ref.shape, 0)
    values = jnp.where(row < FRAMES, x_ref[...].astype(F32), 0.0)
    centred = values - jnp.mean(values, axis=1, keepdims=True)
    scale = lax.rsqrt(jnp.mean(centred * centred, axis=1, keepdims=True) + 1e-05)
    unit = centred * scale
    lifted = total * gain_ref[...]
    mean_one = jnp.mean(lifted, axis=1, keepdims=True)
    mean_two = jnp.mean(lifted * unit, axis=1, keepdims=True)
    gf_ref[...] = (gh_ref[...] + scale * (lifted - mean_one - unit * mean_two)).astype(BF16)
    for j, term in enumerate((total * unit, total)):
        acc[8 * j : 8 * j + 8, :] += jnp.sum(term.reshape(-1, 8, width), axis=0)

    @pl.when(step == pl.num_programs(0) - 1)
    def _():
        for j in (0, 1):
            vec_ref[j : j + 1, :] = jnp.sum(acc[8 * j : 8 * j + 8, :], axis=0, keepdims=True)


def input_grads(frames, grads, weights, rest=None):
    rows, half = grads[0].shape
    width = frames.shape[1]
    tile = 512
    halfs = pl.BlockSpec((tile, half), lambda i: (i, 0))
    wide = pl.BlockSpec((tile, width), lambda i: (i, 0))
    args = [frames, *grads, weights]
    in_specs = [wide, halfs, halfs, halfs, whole(weights.shape)]
    if rest is None:
        out_specs, scratch = [wide], []
        out_shape = [jax.ShapeDtypeStruct((rows, width), F32)]
    else:
        args += rest
        in_specs += [wide, wide, whole((1, width))]
        out_specs = [wide, whole((8, width))]
        out_shape = [
            jax.ShapeDtypeStruct(frames.shape, BF16),
            jax.ShapeDtypeStruct((8, width), F32),
        ]
        scratch = [pltpu.VMEM((16, width), F32)]
    return pl.pallas_call(
        functools.partial(input_grad_kernel, rest is None),
        grid=(rows // tile,),
        in_specs=in_specs,
        out_specs=out_specs,
        out_shape=out_shape,
        scratch_shapes=scratch,
        name="input_grads",
        **params(6 << 30),
    )(*args)


def swap(values, devices, mask):
    return lax.ppermute(values, ("dp", "head"), [(i, i ^ mask) for i in range(devices)])


def both_halves(values):
    high = values.astype(BF16)
    return jnp.concatenate([high, (values - high.astype(F32)).astype(BF16)], axis=0)


def joined(values):
    rows = values.shape[0] // 2
    return values[:rows].astype(F32) + values[rows:].astype(F32)


def on_whole_windows(
    dp_size,
    frames,
    cotangent,
    window_live,
    language,
    task,
    ln1_gain,
    ln1_offset,
    query_weight,
    query_bias,
    key_weight,
    value_weight,
    value_bias,
    out_weight,
    out_bias,
    ln2_gain,
    ln2_offset,
    up_weight,
    up_bias,
    down_weight,
    down_bias,
):
    devices = 2 * dp_size
    width = frames.shape[1]
    half = query_weight.shape[1]
    ow = query_weight.shape[0]
    ff = up_weight.shape[1]
    side = lax.axis_index("head")
    dp = lax.axis_index("dp")
    core, chip = dp % 2, dp // 2
    bit_x, bit_core, bit_y, bit_z = 1, 2, 4, 8
    layers = devices // bit_z

    pieces = jnp.concatenate([query_weight, key_weight, value_weight], axis=0)[None]
    for bit in [bit_z << j for j in range(layers.bit_length() - 1)][::-1] + [bit_y, bit_core]:
        other = swap(pieces, devices, bit)
        pieces = jnp.concatenate([pieces, other], axis=0)
    bits = dp_size.bit_length() - 1
    pieces = pieces.reshape((2,) * bits + pieces.shape[1:])
    pieces = jnp.transpose(
        pieces, tuple(reversed(range(bits))) + (bits, bits + 1)
    ).reshape(dp_size, 3 * ow, half)
    own_pieces = pieces
    oth_pieces = swap(pieces, devices, bit_x)
    up_rows, down_rows = up_weight.T, down_weight
    big = jnp.concatenate(
        [
            down_rows[:, :half],
            down_rows[:, half:],
            up_rows[:, :half],
            up_rows[:, half:],
            out_weight.T,
        ],
        axis=0,
    )
    big = lax.all_gather(big, ("dp", "head"), axis=0, tiled=False)

    per_window = window_weights(window_live, language, task)
    slot = dp * SLOTS + side
    weight = jnp.stack(
        [
            lax.dynamic_index_in_dim(per_window, slot, keepdims=False),
            lax.dynamic_index_in_dim(window_live, slot, keepdims=False).astype(F32),
        ]
    )
    zeros = jnp.zeros_like(query_bias)
    biases = jnp.stack([query_bias, zeros, value_bias]).reshape(3, 2, 1, half)
    own_bias = lax.dynamic_index_in_dim(biases, side, axis=1, keepdims=False)
    oth_bias = lax.dynamic_index_in_dim(biases, 1 - side, axis=1, keepdims=False)
    vecs = jnp.stack([out_bias, ln2_gain, ln2_offset, down_bias])

    pos = dp.astype(jnp.int32).reshape(1)
    normed, normed_t = first_norm(frames, ln1_gain, ln1_offset)
    q1, k1, v1, w1 = project(pos, normed, own_pieces, own_bias)
    c1, l1 = attend_forward_fast(q1, k1, v1)
    q2, k2, v2, w2 = project(pos, normed, oth_pieces, oth_bias)
    c2, l2 = attend_forward_fast(q2, k2, v2)

    place = jnp.stack([core, side]).astype(jnp.int32)
    output, g1, g2, grad_hidden, send, keep, vec = middle(
        place, weight, c1, c2, frames, cotangent, big, vecs, up_bias.reshape(1, -1)
    )
    targets = devices // 2
    piece_rows = big.shape[1]
    got = swap(send, devices, bit_core)

    d2 = attend_backward_fast(q2, k2, v2, l2, c2, g2)
    dw2, s2 = weight_grads(normed_t, *d2)
    (dn2,) = input_grads(frames, d2, w2)
    got_w = swap(dw2, devices, bit_x)

    body = targets * piece_rows
    total = (keep.astype(F32) + got[:body].astype(F32)).reshape(layers, 2, 2, piece_rows, half)
    vec = vec + joined(got[body:])
    yy = chip % 2

    def part(values, y, x):
        start = (0, y, x, 0, 0)
        return lax.dynamic_slice(values, start, (layers, 1, 1, piece_rows, half)).reshape(-1, half)

    mine = part(total, yy, side)
    low_vec = both_halves(vec)
    for mask, y, x in ((bit_x, yy, 1 - side), (bit_y, 1 - yy, side), (bit_x | bit_y, 1 - yy, 1 - side)):
        message = jnp.concatenate([part(total, y, x).astype(BF16), low_vec], axis=0)
        got = swap(message, devices, mask)
        mine += got[: layers * piece_rows].astype(F32)
        vec += joined(got[layers * piece_rows :])

    d1 = attend_backward_fast(q1, k1, v1, l1, c1, g1)

    zz = dp // 4
    mine = mine.reshape(layers, piece_rows, half)
    low_vec = both_halves(vec)
    final = lax.dynamic_index_in_dim(mine, zz, keepdims=False)
    for j in range(1, layers):
        block = lax.dynamic_index_in_dim(mine, zz ^ j, keepdims=False)
        got = swap(jnp.concatenate([block.astype(BF16), low_vec], axis=0), devices, j * bit_z)
        final += got[:piece_rows].astype(F32)
        vec += joined(got[piece_rows:])

    dw1, s1 = weight_grads(normed_t, *d1)
    grad_frames, ln1_vec = input_grads(
        frames, d1, w1, [dn2, grad_hidden, ln1_gain.reshape(1, -1)]
    )
    qkv = dw1.astype(F32) + got_w.astype(F32)
    qkv = qkv.reshape(3, layers, 2, 2, ow, half).transpose(1, 2, 3, 0, 4, 5)
    qkv = qkv.reshape(layers, 2, 2, 3 * ow, half)

    def pick(values, index, axis):
        return lax.dynamic_index_in_dim(values, index, axis=axis, keepdims=False)

    got = swap(pick(qkv, 1 - core, 2).astype(BF16), devices, bit_core)
    qkv = pick(qkv, core, 2) + got.astype(F32)
    got = swap(pick(qkv, 1 - yy, 1).astype(BF16), devices, bit_y)
    qkv = pick(qkv, yy, 1) + got.astype(F32)
    qkv_final = pick(qkv, zz, 0)
    for j in range(1, layers):
        got = swap(pick(qkv, zz ^ j, 0).astype(BF16), devices, j * bit_z)
        qkv_final += got.astype(F32)

    def by_side(own, other):
        return jnp.where(side == 0, jnp.concatenate([own, other]), jnp.concatenate([other, own]))

    tail_vec = jnp.stack(
        [ln1_vec[0], ln1_vec[1], by_side(s1[0], s2[0]), by_side(s1[2], s2[2])]
    )
    for bit in [bit_core, bit_x, bit_y] + [bit_z << j for j in range(layers.bit_length() - 1)]:
        tail_vec = tail_vec + swap(tail_vec, devices, bit)

    down_grad = jnp.concatenate([final[:ff], final[ff : 2 * ff]], axis=1)
    up_grad = jnp.concatenate([final[2 * ff : 3 * ff], final[3 * ff : 4 * ff]], axis=1).T
    out_grad = final[4 * ff :].T
    vec = vec.reshape(8, width)
    return (
        output,
        grad_frames,
        tail_vec[0],
        tail_vec[1],
        qkv_final[:ow],
        tail_vec[2],
        qkv_final[ow : 2 * ow],
        qkv_final[2 * ow :],
        tail_vec[3],
        out_grad,
        vec[0],
        vec[1],
        vec[2],
        up_grad,
        vec[4:].reshape(-1),
        down_grad,
        vec[3],
    )


def solution(mesh):
    placed = (
        P(("dp", "head"), None),
        P(("dp", "head"), None),
        P(),
        P(),
        P(),
        P(),
        P(),
        P("dp", "head"),
        P(),
        P("dp", "head"),
        P("dp", "head"),
        P(),
        P("head", "dp"),
        P(),
        P(),
        P(),
        P(None, ("dp", "head")),
        P(),
        P(("dp", "head"), None),
        P(),
    )
    dp_size, head_size = mesh.shape["dp"], mesh.shape["head"]
    step = on_device
    if dp_size == 16 and head_size == SLOTS:
        step = functools.partial(on_whole_windows, dp_size)
    return jax.shard_map(
        step,
        mesh=mesh,
        in_specs=placed,
        out_specs=(
            P(("dp", "head"), None),
            P(("dp", "head"), None),
            P(),
            P(),
            P("dp", "head"),
            P(),
            P("dp", "head"),
            P("dp", "head"),
            P(),
            P("head", "dp"),
            P(),
            P(),
            P(),
            P(None, ("dp", "head")),
            P(),
            P(("dp", "head"), None),
            P(),
        ),
        check_vma=False,
    )
```

```python
import functools

import jax
import jax.numpy as jnp
from jax import lax
from jax.experimental import pallas as pl
from jax.experimental.pallas import tpu as pltpu
from jax.sharding import PartitionSpec as P

FRAMES = 1500
LANGS = 99
TASKS = 2
SLOTS = 2
HEAD_DIM = 64


def layer_norm(values, gain_vec, offset_vec):
    center = jnp.mean(values, axis=-1, keepdims=True)
    centred = values - center
    spread = jnp.mean(centred * centred, axis=-1, keepdims=True)
    return centred * lax.rsqrt(spread + 1e-05) * gain_vec + offset_vec


def gelu_exact(values):
    return jax.nn.gelu(values, approximate=False)


def contract(first_mat, second_mat):
    return lax.dot_general(
        first_mat, second_mat, (((0,), (0,)), ((), ())), preferred_element_type=jnp.float32
    )


def times_t(first_mat, second_mat):
    return lax.dot_general(
        first_mat, second_mat, (((1,), (1,)), ((), ())), preferred_element_type=jnp.float32
    )


def window_weights(window_live, language, task):
    groups = language * TASKS + task
    labels = jnp.arange(LANGS * TASKS, dtype=jnp.int32)
    matches = groups[:, None] == labels[None, :]
    live_float = window_live.astype(jnp.float32)
    counts = jnp.sum(jnp.where(matches, live_float[:, None], 0.0), axis=0)
    present = jnp.sum((counts > 0.5).astype(jnp.float32))
    own_count = jnp.sum(jnp.where(matches, counts[None, :], 0.0), axis=1)
    return live_float * jnp.sum(live_float) / (present * jnp.maximum(own_count, 1.0))


def window_scores(queries, keys_all):
    return jnp.einsum("qhd,khd->hqk", queries, keys_all, preferred_element_type=jnp.float32) * 0.125


def attend_forward(record):
    queries, keys_all, values_all = record
    scores = window_scores(queries, keys_all)
    highest_score = jnp.max(scores, axis=-1, keepdims=True)
    expo = jnp.exp(scores - highest_score)
    totals = jnp.sum(expo, axis=-1, keepdims=True)
    attn_probs = (expo / totals).astype(jnp.bfloat16)
    context = jnp.einsum("hqk,khd->qhd", attn_probs, values_all, preferred_element_type=jnp.float32)
    return (context.astype(jnp.bfloat16), (highest_score + jnp.log(totals))[..., 0])


def attend_backward(record):
    queries, keys_all, values_all, log_totals, grad_context = record
    scores = window_scores(queries, keys_all)
    attn_probs = jnp.exp(scores - log_totals[..., None])
    grad_probs = jnp.einsum(
        "qhd,khd->hqk", grad_context, values_all, preferred_element_type=jnp.float32
    )
    grad_values = jnp.einsum(
        "hqk,qhd->khd",
        attn_probs.astype(jnp.bfloat16),
        grad_context,
        preferred_element_type=jnp.float32,
    )
    row_delta = jnp.sum(grad_probs * attn_probs, axis=-1, keepdims=True)
    grad_scores = (attn_probs * (grad_probs - row_delta)).astype(jnp.bfloat16)
    grad_queries = (
        jnp.einsum("hqk,khd->qhd", grad_scores, keys_all, preferred_element_type=jnp.float32)
        * 0.125
    )
    grad_keys = (
        jnp.einsum("hqk,qhd->khd", grad_scores, queries, preferred_element_type=jnp.float32) * 0.125
    )
    return (
        grad_queries.astype(jnp.bfloat16),
        grad_keys.astype(jnp.bfloat16),
        grad_values.astype(jnp.bfloat16),
    )


def on_device(
    frames,
    cotangent,
    window_live,
    language,
    task,
    ln1_gain,
    ln1_offset,
    query_weight,
    query_bias,
    key_weight,
    value_weight,
    value_bias,
    out_weight,
    out_bias,
    ln2_gain,
    ln2_offset,
    up_weight,
    up_bias,
    down_weight,
    down_bias,
):
    local_rows = frames.shape[0]
    head_index = lax.axis_index("head")
    data_index = lax.axis_index("dp")
    per_window = window_weights(window_live, language, task)
    slot_ids = (
        head_index * local_rows + jnp.arange(local_rows, dtype=jnp.int32)
    ) // FRAMES + data_index * SLOTS
    window_ids = jnp.arange(per_window.shape[0], dtype=jnp.int32)
    frame_match = slot_ids[:, None] == window_ids[None, :]
    frame_weight = jnp.sum(jnp.where(frame_match, per_window[None, :], 0.0), axis=1)
    frame_live = jnp.sum(
        jnp.where(frame_match, window_live.astype(jnp.float32)[None, :], 0.0), axis=1
    )
    inputs = frames.astype(jnp.float32)
    normed, ln1_back = jax.vjp(layer_norm, inputs, ln1_gain, ln1_offset)
    normed_low = normed.astype(jnp.bfloat16)
    query_head, key_head, value_head, out_head = (
        lax.all_gather(query_weight, "dp", axis=0, tiled=True),
        lax.all_gather(key_weight, "dp", axis=0, tiled=True),
        lax.all_gather(value_weight, "dp", axis=0, tiled=True),
        lax.all_gather(out_weight, "dp", axis=1, tiled=True),
    )
    head_width = query_head.shape[1]
    local_heads = head_width // HEAD_DIM
    joint_weight = jnp.concatenate([query_head, key_head, value_head], axis=1)
    joint_bias = jnp.concatenate(
        [
            lax.dynamic_slice_in_dim(query_bias, head_index * head_width, head_width),
            jnp.zeros((head_width,), jnp.float32),
            lax.dynamic_slice_in_dim(value_bias, head_index * head_width, head_width),
        ]
    )
    normed_all = lax.all_gather(normed_low, "head", axis=0, tiled=True)
    projected = (
        jnp.dot(normed_all, joint_weight, preferred_element_type=jnp.float32) + joint_bias
    ).astype(jnp.bfloat16)
    shaped = projected.reshape(-1, FRAMES, 3, local_heads, HEAD_DIM)
    queries = shaped[:, :, 0]
    keys_all = shaped[:, :, 1]
    values_all = shaped[:, :, 2]
    context, log_totals = lax.map(attend_forward, (queries, keys_all, values_all))
    context_flat = context.reshape(-1, head_width)
    branch = lax.psum_scatter(
        jnp.dot(context_flat, out_head, preferred_element_type=jnp.float32),
        "head",
        scatter_dimension=0,
        tiled=True,
    )
    hidden = inputs + branch + out_bias
    normed_two, ln2_back = jax.vjp(layer_norm, hidden, ln2_gain, ln2_offset)
    normed_two_low = normed_two.astype(jnp.bfloat16)
    up_full, down_full = (
        lax.all_gather(up_weight, ("dp", "head"), axis=1, tiled=True),
        lax.all_gather(down_weight, ("dp", "head"), axis=0, tiled=True),
    )
    pre_act = jnp.dot(normed_two_low, up_full, preferred_element_type=jnp.float32) + up_bias
    activated, gelu_back = jax.vjp(gelu_exact, pre_act)
    activated_low = activated.astype(jnp.bfloat16)
    result = (
        hidden + jnp.dot(activated_low, down_full, preferred_element_type=jnp.float32) + down_bias
    )
    output = (result * frame_live[:, None]).astype(jnp.bfloat16)
    grad_result = cotangent.astype(jnp.float32) * frame_weight[:, None]
    grad_two = grad_result.astype(jnp.bfloat16)
    grad_down = contract(activated_low, grad_two)
    grad_down_bias = jnp.sum(grad_two.astype(jnp.float32), axis=0)
    grad_activated = times_t(grad_two, down_full)
    grad_pre = gelu_back(grad_activated)[0].astype(jnp.bfloat16)
    grad_up = contract(normed_two_low, grad_pre)
    grad_up_bias = jnp.sum(grad_pre.astype(jnp.float32), axis=0)
    grad_normed_two = times_t(grad_pre, up_full)
    grad_hidden_ln, grad_ln2_gain, grad_ln2_offset = ln2_back(grad_normed_two)
    grad_hidden = grad_result + grad_hidden_ln
    grad_branch = grad_hidden.astype(jnp.bfloat16)
    grad_out_bias = jnp.sum(grad_branch.astype(jnp.float32), axis=0)
    branch_all = lax.all_gather(grad_branch, "head", axis=0, tiled=True)
    grad_context = times_t(branch_all, out_head).astype(jnp.bfloat16)
    grad_out_head = contract(context_flat, branch_all)
    grad_context_win = grad_context.reshape(-1, FRAMES, local_heads, HEAD_DIM)
    grad_queries, grad_keys, grad_values = lax.map(
        attend_backward, (queries, keys_all, values_all, log_totals, grad_context_win)
    )
    grad_joint = jnp.concatenate(
        [
            grad_queries.reshape(-1, head_width),
            grad_keys.reshape(-1, head_width),
            grad_values.reshape(-1, head_width),
        ],
        axis=1,
    )
    grad_joint_weight = contract(normed_all, grad_joint)
    joint_sums = jnp.sum(grad_joint.astype(jnp.float32), axis=0)
    empty_vec = jnp.zeros((query_bias.shape[0],), jnp.float32)
    grad_query_bias = lax.dynamic_update_slice(
        empty_vec, joint_sums[:head_width], (head_index * head_width,)
    )
    grad_value_bias = lax.dynamic_update_slice(
        empty_vec, joint_sums[2 * head_width :], (head_index * head_width,)
    )
    grad_normed = lax.psum_scatter(
        times_t(grad_joint, joint_weight), "head", scatter_dimension=0, tiled=True
    )
    grad_inputs_ln, grad_ln1_gain, grad_ln1_offset = ln1_back(grad_normed)
    grad_frames = (grad_hidden + grad_inputs_ln).astype(jnp.bfloat16)
    grad_query_w, grad_key_w, grad_value_w, grad_out_w = (
        lax.psum_scatter(grad_joint_weight[:, :head_width], "dp", scatter_dimension=0, tiled=True),
        lax.psum_scatter(
            grad_joint_weight[:, head_width : 2 * head_width], "dp", scatter_dimension=0, tiled=True
        ),
        lax.psum_scatter(
            grad_joint_weight[:, 2 * head_width :], "dp", scatter_dimension=0, tiled=True
        ),
        lax.psum_scatter(grad_out_head, "dp", scatter_dimension=1, tiled=True),
    )
    grad_up_w, grad_down_w = (
        lax.psum_scatter(grad_up, ("dp", "head"), scatter_dimension=1, tiled=True),
        lax.psum_scatter(grad_down, ("dp", "head"), scatter_dimension=0, tiled=True),
    )
    (
        sum_ln1_gain,
        sum_ln1_offset,
        sum_query_bias,
        sum_value_bias,
        sum_out_bias,
        sum_ln2_gain,
        sum_ln2_offset,
        sum_up_bias,
        sum_down_bias,
    ) = lax.psum(
        (
            grad_ln1_gain,
            grad_ln1_offset,
            grad_query_bias,
            grad_value_bias,
            grad_out_bias,
            grad_ln2_gain,
            grad_ln2_offset,
            grad_up_bias,
            grad_down_bias,
        ),
        ("dp", "head"),
    )
    return (
        output,
        grad_frames,
        sum_ln1_gain,
        sum_ln1_offset,
        grad_query_w,
        sum_query_bias,
        grad_key_w,
        grad_value_w,
        sum_value_bias,
        grad_out_w,
        sum_out_bias,
        sum_ln2_gain,
        sum_ln2_offset,
        grad_up_w,
        sum_up_bias,
        grad_down_w,
        sum_down_bias,
    )


LANES = 128
PADDED = 1536
LOG2E = 1.4426950408889634
MASKED = -30000.0
F32 = jnp.float32
BF16 = jnp.bfloat16
VMEM_BYTES = 58 << 20
LN1_GAIN, LN1_OFFSET, OUT_BIAS, LN2_GAIN, LN2_OFFSET, DOWN_BIAS = range(6)
WEIGHT, LIVE, QUERY_BIAS, VALUE_BIAS, UP_BIAS = 6, 7, 8, 10, 11
BIT_X, BIT_CORE, BIT_Y, BIT_Z = 1, 2, 4, 8
LAYERS = 4


def dot_on(first_mat, second_mat, first_dim, second_dim):
    return lax.dot_general(
        first_mat,
        second_mat,
        (((first_dim,), (second_dim,)), ((), ())),
        preferred_element_type=F32,
    )


def params(microseconds):
    return dict(
        compiler_params=pltpu.CompilerParams(vmem_limit_bytes=VMEM_BYTES),
        cost_estimate=pl.CostEstimate(
            flops=int(microseconds * 1e9), bytes_accessed=1 << 20, transcendentals=0
        ),
    )


def whole(shape):
    return pl.BlockSpec(shape, lambda *_: (0,) * len(shape), pipeline_mode=pl.Buffered(1))


def struct(shape, dtype):
    return jax.ShapeDtypeStruct(shape, dtype)


def place():
    dp = lax.axis_index("dp")
    return dp, lax.axis_index("head")


def pack_kernel(
    live_ref,
    language_ref,
    task_ref,
    query_ref,
    key_ref,
    value_ref,
    out_ref,
    up_ref,
    down_ref,
    upb_ref,
    qb_ref,
    vb_ref,
    *refs,
):
    vectors, (pieces_ref, big_ref, table_ref) = refs[:6], refs[6:]
    rows, half = query_ref.shape
    ff = down_ref.shape[0]
    dp, side = place()
    for j, ref in enumerate((query_ref, key_ref, value_ref)):
        pieces_ref[0, j * rows : (j + 1) * rows, :] = ref[...]
    up = up_ref[...].astype(F32).T.astype(BF16)
    big_ref[0:ff, :] = down_ref[:, 0:half]
    big_ref[ff : 2 * ff, :] = down_ref[:, half:]
    big_ref[2 * ff : 3 * ff, :] = up[:, 0:half]
    big_ref[3 * ff : 4 * ff, :] = up[:, half:]
    big_ref[4 * ff :, :] = out_ref[...].astype(F32).T.astype(BF16)
    for j, ref in enumerate(vectors):
        table_ref[j : j + 1, :] = ref[...]
    for j, ref in ((QUERY_BIAS, qb_ref), (VALUE_BIAS, vb_ref)):
        first, second = ref[:, 0:half], ref[:, half:]
        table_ref[j : j + 1, 0:half] = jnp.where(side == 0, second, first)
        table_ref[j : j + 1, half:] = jnp.where(side == 0, first, second)
    table_ref[QUERY_BIAS + 1 : QUERY_BIAS + 2, :] = jnp.zeros((1, 2 * half), F32)
    for j in range(4):
        table_ref[UP_BIAS + j : UP_BIAS + j + 1, :] = upb_ref[:, j * 2 * half : (j + 1) * 2 * half]
    slots = live_ref.shape[0]
    lane = lax.broadcasted_iota(jnp.int32, (1, LANES), 1)
    groups = jnp.full((1, LANES), -1, jnp.int32)
    live = jnp.zeros((1, LANES), F32)
    for t in range(slots):
        groups = jnp.where(lane == t, language_ref[t] * TASKS + task_ref[t], groups)
        live = jnp.where(lane == t, live_ref[t].astype(F32), live)
    counts = jnp.zeros((1, LANES), F32)
    for t in range(slots):
        group = language_ref[t] * TASKS + task_ref[t]
        counts = counts + jnp.where(groups == group, live_ref[t].astype(F32), 0.0)
    counts = jnp.maximum(counts, 1.0)
    shares = jnp.broadcast_to(live / counts, (8, LANES))
    present = jnp.floor(jnp.sum(shares, axis=1, keepdims=True)[0:1] + 0.5)
    total = jnp.sum(jnp.broadcast_to(live, (8, LANES)), axis=1, keepdims=True)[0:1]
    weights = live * total / (present * counts)
    mine = lane == dp * SLOTS + side
    for j, values in ((WEIGHT, weights), (LIVE, live)):
        picked = jnp.broadcast_to(jnp.where(mine, values, 0.0), (8, LANES))
        picked = jnp.sum(picked, axis=1, keepdims=True)[0:1]
        table_ref[j : j + 1, :] = jnp.broadcast_to(picked, (1, 2 * half))


def pack(live, language, task, query, key, value, out, up, down, up_bias, qb, vb, vectors):
    rows, half = query.shape
    ff, width = down.shape
    scalars = pl.BlockSpec(memory_space=pltpu.SMEM)
    row = lambda values: values.reshape(1, -1)
    rest = [query, key, value, out, up, down, row(up_bias), row(qb), row(vb)] + [
        row(v) for v in vectors
    ]
    return pl.pallas_call(
        pack_kernel,
        in_specs=[scalars] * 3 + [pl.BlockSpec(memory_space=pltpu.VMEM)] * len(rest),
        out_shape=[
            struct((1, 3 * rows, half), BF16),
            struct((4 * ff + rows, half), BF16),
            struct((16, width), F32),
        ],
        name="pack",
        **params(3),
    )(live, language, task, *rest)


def real_rows(x_ref):
    row = pl.program_id(0) * x_ref.shape[0] + lax.broadcasted_iota(jnp.int32, x_ref.shape, 0)
    return row < FRAMES


def unit_rows(values):
    centred = values - jnp.mean(values, axis=1, keepdims=True)
    scale = lax.rsqrt(jnp.mean(centred * centred, axis=1, keepdims=True) + 1e-05)
    return centred * scale, scale


def unit_back(lifted, unit, scale):
    mean_one = jnp.mean(lifted, axis=1, keepdims=True)
    mean_two = jnp.mean(lifted * unit, axis=1, keepdims=True)
    return scale * (lifted - mean_one - unit * mean_two)


def norm_kernel(x_ref, table_ref, n_ref, nt_ref):
    unit, _ = unit_rows(jnp.where(real_rows(x_ref), x_ref[...].astype(F32), 0.0))
    normed = unit * table_ref[LN1_GAIN : LN1_GAIN + 1, :] + table_ref[LN1_OFFSET : LN1_OFFSET + 1, :]
    n_ref[...] = normed.astype(BF16)
    nt_ref[...] = normed.T.astype(BF16)


def first_norm(frames, table):
    width = frames.shape[1]
    tile = 512
    return pl.pallas_call(
        norm_kernel,
        grid=(PADDED // tile,),
        in_specs=[pl.BlockSpec((tile, width), lambda i: (i, 0)), whole(table.shape)],
        out_specs=[
            pl.BlockSpec((tile, width), lambda i: (i, 0)),
            pl.BlockSpec((width, tile), lambda i: (0, i)),
        ],
        out_shape=[struct((PADDED, width), BF16), struct((width, PADDED), BF16)],
        name="first_norm",
        **params(4),
    )(frames, table)


def lane_masks(shape, h):
    lane = lax.broadcasted_iota(jnp.int32, shape, 1)
    if h == 0:
        return lane < HEAD_DIM, lane - HEAD_DIM
    return lane >= HEAD_DIM, jnp.where(lane < HEAD_DIM, lane, -1)


def spread_three(extra, values, base):
    high = values.astype(BF16).astype(F32)
    rest = values - high
    middle = rest.astype(BF16).astype(F32)
    return jnp.where(
        extra == 0, high, jnp.where(extra == 1, middle, jnp.where(extra == 2, rest - middle, base))
    )


def store_keys(keys, keys_ref, h):
    own, extra = lane_masks(keys.shape, h)
    row = lax.broadcasted_iota(jnp.int32, keys.shape, 0)
    ones = (extra >= 0) & (extra < 3)
    fill = jnp.where(ones, 1.0, jnp.where((extra == 3) & (row >= FRAMES), MASKED, 0.0))
    keys_ref[h, :, 0:LANES] = jnp.where(own, keys, fill).astype(BF16)
    keys_ref[h, :, LANES:] = jnp.where(own, keys, 0.0).astype(BF16)


def wide_queries(scaled, h, log_totals):
    own, extra = lane_masks(scaled.shape, h)
    high = scaled.astype(BF16).astype(F32)
    fill = jnp.where(extra == 3, 1.0, 0.0)
    if log_totals is not None:
        fill = spread_three(extra, -log_totals, fill)
    return jnp.concatenate(
        [
            jnp.where(own, high, fill).astype(BF16),
            jnp.where(own, scaled - high, 0.0).astype(BF16),
        ],
        axis=1,
    )


def reversed_bits(value):
    return (value & 1) * 8 + (value & 2) * 2 + ((value & 4) >> 1) + ((value & 8) >> 3)


def forward_kernel(side_at, n_ref, pieces_ref, table_ref, *refs):
    q_ref, k_ref, v_ref, c_ref, lse_ref, w_ref, keys_ref, vt_ref = refs[-8:]
    pair, step = pl.program_id(0), pl.program_id(1)
    count, rows3, half = pieces_ref.shape
    rows = rows3 // 3

    @pl.when((pair == 0) & (step == 0))
    def _():
        mask = reversed_bits(place()[0])
        for d in range(count):
            at = reversed_bits(d) ^ mask
            for j in range(3):
                w_ref[j, d * rows : (d + 1) * rows, :] = pieces_ref[at, j * rows : (j + 1) * rows, :]

    @pl.when(step == 0)
    def _():
        columns = pl.ds(pl.multiple_of(pair * LANES, LANES), LANES)
        places = pl.ds(pl.multiple_of(pair * LANES + side_at * half, LANES), LANES)
        for j, out in enumerate((q_ref, k_ref, v_ref)):
            bias = table_ref[QUERY_BIAS + j : QUERY_BIAS + j + 1, places]
            out[...] = (dot_on(n_ref[...], w_ref[j, :, columns], 1, 0) + bias).astype(BF16)
        keys = k_ref[...].astype(F32)
        flipped = v_ref[...].astype(F32).T.astype(BF16)
        shape = (vt_ref.shape[1] - HEAD_DIM, flipped.shape[1])
        ones = jnp.where(lax.broadcasted_iota(jnp.int32, shape, 0) == 0, 1.0, 0.0).astype(BF16)
        for h in (0, 1):
            store_keys(keys, keys_ref, h)
            vt_ref[h, 0:HEAD_DIM, :] = flipped[HEAD_DIM * h : HEAD_DIM * (h + 1), :]
            vt_ref[h, HEAD_DIM:, :] = ones

    tile = c_ref.shape[0]
    scaled = q_ref[pl.ds(step * tile, tile), :].astype(F32) * (LOG2E * 0.125)
    contexts, totals = [], []
    for h in (0, 1):
        scores = dot_on(keys_ref[h], wide_queries(scaled, h, None), 1, 1)
        highest = jnp.max(scores, axis=0, keepdims=True)
        probs = jnp.exp2(scores - highest).astype(BF16)
        summed = dot_on(vt_ref[h], probs, 1, 0)
        total = summed[HEAD_DIM : HEAD_DIM + 1, :]
        contexts.append(summed[0:HEAD_DIM, :] / total)
        log_total = highest + jnp.log2(total)
        totals.append(jnp.broadcast_to(log_total, (HEAD_DIM, log_total.shape[1])))
    c_ref[...] = jnp.concatenate(contexts, axis=0).T.astype(BF16)
    lse_ref[...] = jnp.concatenate(totals, axis=0).T


def attend_forward_fast(side_at, normed, pieces, table, before=()):
    rows, width = normed.shape
    half = pieces.shape[2]
    pairs = half // LANES
    tile = 768
    at = side_at * pairs
    block = pl.BlockSpec((tile, LANES), lambda p, i: (i, p + at))
    full = pl.BlockSpec((rows, LANES), lambda p, i: (0, p + at))
    weights = pl.BlockSpec((3, width, half), lambda p, i: (0, 0, side_at))
    return pl.pallas_call(
        functools.partial(forward_kernel, side_at),
        grid=(pairs, rows // tile),
        in_specs=[whole(normed.shape), whole(pieces.shape), whole(table.shape)]
        + [pl.BlockSpec(memory_space=pl.ANY)] * len(before),
        out_specs=[full, full, full, block, block, weights],
        out_shape=[struct((rows, width), BF16)] * 4
        + [struct((rows, width), F32), struct((3, width, width), BF16)],
        scratch_shapes=[
            pltpu.VMEM((2, rows, 2 * LANES), BF16),
            pltpu.VMEM((2, HEAD_DIM + 16, rows), BF16),
        ],
        input_output_aliases={3 + j: j for j in range(len(before))},
        name="attend_forward",
        **params(19),
    )(normed, pieces, table, *before)


def backward_kernel(
    q_ref, k_ref, v_ref, lse_ref, c_ref, g_ref, nt_ref, w_ref,
    dq_ref, dk_ref, dv_ref, dw_ref, vec_ref,
    keys_ref, vals_ref, kt_ref, acck, accv, acc_one, acc_two,
):
    pair, step = pl.program_id(0), pl.program_id(1)
    last = step == pl.num_programs(1) - 1

    @pl.when(step == 0)
    def _():
        keys = k_ref[...].astype(F32)
        values = v_ref[...].astype(F32)
        for h in (0, 1):
            store_keys(keys, keys_ref, h)
            own, _ = lane_masks(values.shape, h)
            vals_ref[h] = jnp.where(own, values, 1.0).astype(BF16)
        kt_ref[...] = keys.T.astype(BF16)
        acck[...] = jnp.zeros_like(acck)
        accv[...] = jnp.zeros_like(accv)

    tile = q_ref.shape[0]
    plain = q_ref[...].astype(F32)
    scaled = plain * (LOG2E * 0.125)
    grads = g_ref[...].astype(F32)
    products = grads * c_ref[...].astype(F32)
    log_totals = pltpu.roll(lse_ref[...], HEAD_DIM, 1)
    probs, diffs, queries, outers, flipped = [], [], [], [], []
    for h in (0, 1):
        own, extra = lane_masks(grads.shape, h)
        row_delta = jnp.sum(jnp.where(own, products, 0.0), axis=1, keepdims=True)
        wide = jnp.where(own, grads, spread_three(extra, -row_delta, 0.0)).astype(BF16)
        prob = jnp.exp2(dot_on(keys_ref[h], wide_queries(scaled, h, log_totals), 1, 1))
        diff = (prob * dot_on(vals_ref[h], wide, 1, 1)).astype(BF16)
        probs.append(prob.astype(BF16))
        diffs.append(diff)
        outers.append(jnp.where(own, grads, 0.0).astype(BF16))
        queries.append(jnp.where(own, plain, 0.0).astype(BF16))
        flipped.append(dot_on(kt_ref[HEAD_DIM * h : HEAD_DIM * (h + 1), :], diff, 1, 0))
    accv[...] += dot_on(probs[0], outers[0], 1, 0) + dot_on(probs[1], outers[1], 1, 0)
    acck[...] += dot_on(diffs[0], queries[0], 1, 0) + dot_on(diffs[1], queries[1], 1, 0)
    dq_ref[pl.ds(step * tile, tile), :] = (jnp.concatenate(flipped, axis=0) * 0.125).T.astype(BF16)

    @pl.when(last & (pair == 0))
    def _():
        acc_one[...] = jnp.zeros_like(acc_one)
        acc_two[...] = jnp.zeros_like(acc_two)
        vec_ref[...] = jnp.zeros_like(vec_ref)

    @pl.when(last)
    def _():
        dk_ref[...] = (acck[...] * 0.125).astype(BF16)
        dv_ref[...] = accv[...].astype(BF16)
        for j, ref in enumerate((dq_ref, dk_ref, dv_ref)):
            dw = dot_on(nt_ref[...], ref[...], 1, 0)
            dw_ref[j] = dw.astype(dw_ref.dtype)
            sums = jnp.sum(ref[...].astype(F32), axis=0, keepdims=True)
            weights = w_ref[j].astype(F32)
            acc_one[...] += weights * dw
            acc_two[...] += weights * sums
            if j != 1:
                columns = pl.ds(pl.multiple_of(pair * LANES, LANES), LANES)
                vec_ref[2 + j // 2 : 3 + j // 2, columns] = sums

    @pl.when(last & (pair == pl.num_programs(0) - 1))
    def _():
        for j, ref in enumerate((acc_one, acc_two)):
            vec_ref[j : j + 1, :] = jnp.sum(ref[...].T, axis=0, keepdims=True)


def attend_backward_fast(first, pairs, q, k, v, lse, context, grads, normed_t, weights):
    rows, width = q.shape
    tile = 512
    block = pl.BlockSpec((tile, LANES), lambda p, i: (i, p + first))
    full = pl.BlockSpec((rows, LANES), lambda p, i: (0, p + first))
    outs = pl.BlockSpec((rows, LANES), lambda p, i: (0, p))
    return pl.pallas_call(
        backward_kernel,
        grid=(pairs, rows // tile),
        in_specs=[
            block, full, full, block, block, block, whole(normed_t.shape),
            pl.BlockSpec((3, width, LANES), lambda p, i: (0, 0, p + first)),
        ],
        out_specs=[
            outs, outs, outs,
            pl.BlockSpec((3, width, LANES), lambda p, i: (0, 0, p)),
            whole((8, width)),
        ],
        out_shape=[struct((rows, pairs * LANES), BF16)] * 3
        + [struct((3, width, pairs * LANES), BF16), struct((8, width), F32)],
        scratch_shapes=[
            pltpu.VMEM((2, rows, 2 * LANES), BF16),
            pltpu.VMEM((2, rows, LANES), BF16),
            pltpu.VMEM((LANES, rows), BF16),
            pltpu.VMEM((rows, LANES), F32),
            pltpu.VMEM((rows, LANES), F32),
            pltpu.VMEM((width, LANES), F32),
            pltpu.VMEM((width, LANES), F32),
        ],
        name="attend_backward",
        **params(16 * pairs),
    )(q, k, v, lse, context, grads, normed_t, weights)


def middle_kernel(
    c_ref, x_ref, cot_ref, pieces_ref, table_ref,
    out_ref, g_ref, gh_ref, send_ref, keep_ref, vec_ref,
    up_t, up_n, down_n, down_t, out_t, upb_t, acc_up, acc_down, acc_out, acc_upb, acc_vec,
):
    step = pl.program_id(0)
    dp, side = place()
    core = lax.rem(dp, 2)
    devices, piece_rows, half = pieces_ref.shape
    width = 2 * half
    ow = width // (devices // 2)
    ff = (piece_rows - ow) // 4
    hidden_all = devices * ff
    chunk = 512
    chunks = hidden_all // chunk

    @pl.when(step == 0)
    def _():
        for d in range(devices):
            rows = slice(d * ff, (d + 1) * ff)
            down_n[rows, 0:half] = pieces_ref[d, 0:ff, :]
            down_n[rows, half:] = pieces_ref[d, ff : 2 * ff, :]
            up_t[rows, 0:half] = pieces_ref[d, 2 * ff : 3 * ff, :]
            up_t[rows, half:] = pieces_ref[d, 3 * ff : 4 * ff, :]
        for d in range(devices // 2):
            rows = slice(d * ow, (d + 1) * ow)
            out_t[rows, 0:half] = pieces_ref[2 * d + 1 - side, 4 * ff :, :]
            out_t[rows, half:] = pieces_ref[2 * d + side, 4 * ff :, :]
        for j in range(chunks):
            rows = slice(j * chunk, (j + 1) * chunk)
            up_n[:, rows] = up_t[rows, :].T
            down_t[:, rows] = down_n[rows, :].T
            bias = table_ref[UP_BIAS + j : UP_BIAS + j + 1, :]
            upb_t[rows, :] = jnp.broadcast_to(bias, (LANES, chunk)).T
        acc_up[...] = jnp.zeros_like(acc_up)
        acc_down[...] = jnp.zeros_like(acc_down)
        acc_out[...] = jnp.zeros_like(acc_out)
        acc_upb[...] = jnp.zeros_like(acc_upb)
        acc_vec[...] = jnp.zeros_like(acc_vec)

    def row_of(j):
        return table_ref[j : j + 1, :]

    tile = x_ref.shape[0]
    real = real_rows(x_ref)
    branch = dot_on(c_ref[...], out_t[...], 1, 1)
    hidden = jnp.where(real, x_ref[...].astype(F32), 0.0) + branch + row_of(OUT_BIAS)
    unit, scale = unit_rows(hidden)
    normed = (unit * row_of(LN2_GAIN) + row_of(LN2_OFFSET)).astype(BF16)
    grad_result = jnp.where(real, cot_ref[...].astype(F32), 0.0) * row_of(WEIGHT)
    grad_two = grad_result.astype(BF16)
    result_t = jnp.zeros((width, tile), F32)
    grad_normed_t = jnp.zeros((width, tile), F32)
    for j in range(chunks):
        rows = slice(j * chunk, (j + 1) * chunk)
        slots = slice(j * chunk // ff, (j + 1) * chunk // ff)
        pre = dot_on(up_t[rows, :], normed, 1, 1) + upb_t[rows, 0:1]
        bell = 0.5 + 0.5 * lax.erf(pre * 0.7071067811865476)
        slope = bell + pre * (jnp.exp2(pre * pre * (-0.5 * LOG2E)) * 0.3989422804014327)
        activated = (pre * bell).astype(BF16)
        result_t += dot_on(down_t[:, rows], activated, 1, 0)
        acc_down[slots] += dot_on(activated, grad_two, 1, 0).reshape(-1, ff, width)
        grad_pre = (dot_on(down_n[rows, :], grad_two, 1, 1) * slope).astype(BF16)
        rounded = grad_pre.astype(F32)
        partial = rounded[:, 0:LANES]
        for lanes in range(LANES, tile, LANES):
            partial += rounded[:, lanes : lanes + LANES]
        acc_upb[rows, :] += partial
        acc_up[slots] += dot_on(grad_pre, normed, 1, 0).reshape(-1, ff, width)
        grad_normed_t += dot_on(up_n[:, rows], grad_pre, 1, 0)
    result = hidden + result_t.T + row_of(DOWN_BIAS)
    out_ref[...] = (result * row_of(LIVE)).astype(BF16)
    grad_normed = grad_normed_t.T
    grad_hidden = grad_result + unit_back(grad_normed * row_of(LN2_GAIN), unit, scale)
    gh_ref[...] = grad_hidden
    grad_branch = grad_hidden.astype(BF16)
    g_ref[...] = dot_on(grad_branch, out_t[...], 1, 0).astype(BF16)
    acc_out[...] += dot_on(grad_hidden.T.astype(BF16), c_ref[...], 1, 0).reshape(-1, ow, width)
    for j, term in enumerate(
        (grad_branch.astype(F32), grad_normed * unit, grad_normed, grad_two.astype(F32))
    ):
        acc_vec[8 * j : 8 * j + 8, :] += jnp.sum(term.reshape(-1, 8, width), axis=0)

    @pl.when(step == pl.num_programs(0) - 1)
    def _():
        targets = devices // 2
        for ref, bit in ((keep_ref, core), (send_ref, 1 - core)):
            for t in range(targets):
                y, x, z = t // (2 * LAYERS), t // LAYERS % 2, t % LAYERS
                at = t * piece_rows
                chip = z * 2 + y
                slot = chip * 4 + bit * 2 + x
                near = pl.ds(pl.multiple_of((1 - (side ^ x)) * half, half), half)
                ref[at : at + ff, :] = acc_down[slot, :, 0:half].astype(BF16)
                ref[at + ff : at + 2 * ff, :] = acc_down[slot, :, half:].astype(BF16)
                ref[at + 2 * ff : at + 3 * ff, :] = acc_up[slot, :, 0:half].astype(BF16)
                ref[at + 3 * ff : at + 4 * ff, :] = acc_up[slot, :, half:].astype(BF16)
                ref[at + 4 * ff : at + piece_rows, :] = acc_out[chip * 2 + bit, :, near].astype(BF16)
        for j in range(4):
            total = jnp.sum(acc_vec[8 * j : 8 * j + 8, :], axis=0, keepdims=True)
            vec_ref[2 * j : 2 * j + 1, :] = total[:, 0:half]
            vec_ref[2 * j + 1 : 2 * j + 2, :] = total[:, half:]
        for j in range(chunks):
            total = jnp.sum(acc_upb[j * chunk : (j + 1) * chunk, :].T, axis=0, keepdims=True)
            for i in range(chunk // half):
                at = 8 + j * (chunk // half) + i
                vec_ref[at : at + 1, :] = total[:, i * half : (i + 1) * half]
        store_two(send_ref, targets * piece_rows, vec_ref[...])


def middle(context, frames, cotangent, pieces, table):
    rows, width = context.shape
    devices, piece_rows, half = pieces.shape
    tile = 512
    ow = width // (devices // 2)
    ff = (piece_rows - ow) // 4
    hidden_all = devices * ff
    body = devices // 2 * piece_rows
    wide = pl.BlockSpec((tile, width), lambda i: (i, 0))
    return pl.pallas_call(
        middle_kernel,
        grid=(rows // tile,),
        in_specs=[wide, wide, wide, whole(pieces.shape), whole(table.shape)],
        out_specs=[wide, wide, wide, whole((body + 32, half)), whole((body, half)), whole((16, half))],
        out_shape=[
            struct(frames.shape, BF16),
            struct((rows, width), BF16),
            struct((rows, width), F32),
            struct((body + 32, half), BF16),
            struct((body, half), BF16),
            struct((16, half), F32),
        ],
        scratch_shapes=[
            pltpu.VMEM((hidden_all, width), BF16),
            pltpu.VMEM((width, hidden_all), BF16),
            pltpu.VMEM((hidden_all, width), BF16),
            pltpu.VMEM((width, hidden_all), BF16),
            pltpu.VMEM((width, width), BF16),
            pltpu.VMEM((hidden_all, LANES), F32),
            pltpu.VMEM((devices, ff, width), F32),
            pltpu.VMEM((devices, ff, width), F32),
            pltpu.VMEM((width // ow, ow, width), F32),
            pltpu.VMEM((hidden_all, LANES), F32),
            pltpu.VMEM((32, width), F32),
        ],
        name="middle",
        **params(38),
    )(context, frames, cotangent, pieces, table)


def store_two(ref, at, values):
    count = values.shape[0]
    high = values.astype(BF16)
    ref[at : at + count, :] = high
    ref[at + count : at + 2 * count, :] = (values - high.astype(F32)).astype(BF16)


def load_two(ref, at, count):
    return ref[at : at + count, :].astype(F32) + ref[at + count : at + 2 * count, :].astype(F32)


def spread_kernel(count, masks, keep_ref, vec_ref, *refs):
    came, (mine_ref, sum_ref, *sends) = refs[:count], refs[count:]
    size, half = mine_ref.shape
    dp, side = place()
    parts = keep_ref.shape[0] // size
    vec_rows = vec_ref.shape[0]
    vec = vec_ref[...]
    for ref in came:
        vec += load_two(ref, ref.shape[0] - 2 * vec_rows, vec_rows)
    sum_ref[...] = vec

    def total(part):
        rows = pl.ds(pl.multiple_of(part * size, 32), size)
        values = keep_ref[rows, :].astype(F32)
        for ref in came:
            if ref.shape[0] > 2 * vec_rows:
                values += ref[rows, :].astype(F32)
        return values

    own = masks[0](dp, side)
    mine_ref[...] = total(own)
    for mask, ref in zip(masks[1:], sends):
        if mask is not None:
            ref[0:size, :] = total(own ^ mask).astype(BF16)
        store_two(ref, ref.shape[0] - 2 * vec_rows, vec)


def spread(keep, vec, came, own_part, masks, parts):
    rows, half = keep.shape
    size = rows // parts
    tail = 2 * vec.shape[0]
    vmem = pl.BlockSpec(memory_space=pltpu.VMEM)
    return pl.pallas_call(
        functools.partial(spread_kernel, len(came), (own_part, *masks)),
        in_specs=[vmem] * (2 + len(came)),
        out_specs=[vmem] * (2 + len(masks)),
        out_shape=[struct((size, half), F32), struct(vec.shape, F32)]
        + [struct(((0 if m is None else size) + tail, half), BF16) for m in masks],
        name="spread",
        **params(3),
    )(keep, vec, *came)


def swap(values, mask):
    devices = lax.axis_size("dp") * lax.axis_size("head")
    return lax.ppermute(values, ("dp", "head"), [(i, i ^ mask) for i in range(devices)])


def part_xy(dp, side):
    return ((dp >> 1) & 1) * 2 + side


def part_y(dp, side):
    return (dp >> 1) & 1


def part_z(dp, side):
    return dp >> 2


def finish_kernel(count, ff, ow, mine_ref, vec_ref, *refs):
    came, outs = refs[:count], refs[count:]
    down_ref, up_ref, out_ref, *vectors = outs
    vec_rows, half = vec_ref.shape
    size = mine_ref.shape[0]
    values, vec = mine_ref[...], vec_ref[...]
    for ref in came:
        values += ref[0:size, :].astype(F32)
        vec += load_two(ref, size, vec_rows)
    down_ref[:, 0:half] = values[0:ff]
    down_ref[:, half:] = values[ff : 2 * ff]
    up_ref[0:half, :] = values[2 * ff : 3 * ff].T
    up_ref[half:, :] = values[3 * ff : 4 * ff].T
    out_ref[...] = values[4 * ff :].T
    at = 0
    for ref in vectors:
        for j in range(ref.shape[1] // half):
            ref[:, j * half : (j + 1) * half] = vec[at : at + 1, :]
            at += 1


def finish(mine, vec, came, ff, ow):
    half = mine.shape[1]
    vmem = pl.BlockSpec(memory_space=pltpu.VMEM)
    return pl.pallas_call(
        functools.partial(finish_kernel, len(came), ff, ow),
        in_specs=[vmem] * (2 + len(came)),
        out_specs=[vmem] * 8,
        out_shape=[
            struct((ff, 2 * half), F32),
            struct((2 * half, ff), F32),
            struct((half, ow), F32),
        ]
        + [struct((1, 2 * half), F32)] * 4
        + [struct((1, 8 * half), F32)],
        name="finish",
        **params(2),
    )(mine, vec, *came)


def gather_kernel(table_ref, dwb_ref, dwc_ref, gota_ref, gotb_ref, *refs):
    *vecs, send_ref, keep_ref, vec_ref = refs
    dp, side = place()
    core = lax.rem(dp, 2)
    width = table_ref.shape[1]
    half = width // 2
    ow = width // 16
    for ref, bit in ((keep_ref, core), (send_ref, 1 - core)):
        for t in range(2 * LAYERS):
            chip = t % LAYERS * 2 + t // LAYERS
            rows = pl.ds(pl.multiple_of((chip * 2 + bit) * ow, ow), ow)
            for j in range(3):
                at = t * 3 * ow + j * ow
                first = dwb_ref[j, rows, LANES:].astype(F32) + gota_ref[j, rows, :].astype(F32)
                second = dwc_ref[j, rows, :].astype(F32) + gotb_ref[j, rows, :].astype(F32)
                ref[at : at + ow, 0:LANES] = first.astype(ref.dtype)
                ref[at : at + ow, LANES:] = second.astype(ref.dtype)
    one = vecs[0][0:1, :] + vecs[1][0:1, :] + vecs[2][0:1, :]
    two = vecs[0][1:2, :] + vecs[1][1:2, :] + vecs[2][1:2, :]
    gain = table_ref[LN1_GAIN : LN1_GAIN + 1, :]
    offset = table_ref[LN1_OFFSET : LN1_OFFSET + 1, :]
    grad_gain = (one - offset * two) / gain
    for j, values in ((0, grad_gain), (2, two)):
        vec_ref[j : j + 1, :] = values[:, 0:half]
        vec_ref[j + 1 : j + 2, :] = values[:, half:]
    for j in (0, 1):
        row = slice(2 + j, 3 + j)
        other = jnp.concatenate([vecs[0][row, 0:LANES], vecs[1][row, 0:LANES]], axis=1)
        own = jnp.concatenate([vecs[1][row, LANES : 2 * LANES], vecs[2][row, 0:LANES]], axis=1)
        vec_ref[4 + 2 * j : 5 + 2 * j, :] = jnp.where(side == 0, own, other)
        vec_ref[5 + 2 * j : 6 + 2 * j, :] = jnp.where(side == 0, other, own)
    store_two(send_ref, 24 * ow, vec_ref[...])


def gather_grads(table, dwb, dwc, gota, gotb, vecs):
    width = table.shape[1]
    half = width // 2
    rows = 24 * (width // 16)
    vmem = pl.BlockSpec(memory_space=pltpu.VMEM)
    return pl.pallas_call(
        gather_kernel,
        in_specs=[vmem] * 8,
        out_specs=[vmem] * 3,
        out_shape=[
            struct((rows + 16, half), BF16),
            struct((rows, half), F32),
            struct((8, half), F32),
        ],
        name="gather_grads",
        **params(2),
    )(table, dwb, dwc, gota, gotb, *vecs)


def close_kernel(count, mine_ref, vec_ref, *refs):
    came, outs = refs[:count], refs[count:]
    vec_rows, half = vec_ref.shape
    size = mine_ref.shape[0]
    ow = size // 3
    values, vec = mine_ref[...], vec_ref[...]
    for ref in came:
        values += ref[0:size, :].astype(F32)
        vec += load_two(ref, size, vec_rows)
    for j in range(3):
        outs[j][...] = values[j * ow : (j + 1) * ow]
    for j in range(4):
        outs[3 + j][:, 0:half] = vec[2 * j : 2 * j + 1]
        outs[3 + j][:, half:] = vec[2 * j + 1 : 2 * j + 2]


def close(mine, vec, came):
    size, half = mine.shape
    vmem = pl.BlockSpec(memory_space=pltpu.VMEM)
    return pl.pallas_call(
        functools.partial(close_kernel, len(came)),
        in_specs=[vmem] * (2 + len(came)),
        out_specs=[vmem] * 7,
        out_shape=[struct((size // 3, half), F32)] * 3 + [struct((1, 2 * half), F32)] * 4,
        name="close",
        **params(2),
    )(mine, vec, *came)


def input_grad_kernel(count, x_ref, gh_ref, table_ref, w_ref, *refs):
    *grads, gf_ref = refs
    at = 0
    total = jnp.zeros(x_ref.shape, F32)
    for c in range(count):
        for j in range(3):
            ref = grads[3 * c + j]
            total += dot_on(ref[...], w_ref[j, :, at : at + ref.shape[1]], 1, 1)
        at += ref.shape[1]
    unit, scale = unit_rows(jnp.where(real_rows(x_ref), x_ref[...].astype(F32), 0.0))
    lifted = total * table_ref[LN1_GAIN : LN1_GAIN + 1, :]
    gf_ref[...] = (gh_ref[...] + unit_back(lifted, unit, scale)).astype(BF16)


def input_grads(frames, grad_hidden, table, weights, grads):
    rows, width = grad_hidden.shape
    tile = 512
    wide = pl.BlockSpec((tile, width), lambda i: (i, 0))
    flat = [g for group in grads for g in group]
    return pl.pallas_call(
        functools.partial(input_grad_kernel, len(grads)),
        grid=(rows // tile,),
        in_specs=[wide, wide, whole(table.shape), whole(weights.shape)]
        + [pl.BlockSpec((tile, g.shape[1]), lambda i: (i, 0)) for g in flat],
        out_specs=wide,
        out_shape=struct(frames.shape, BF16),
        name="input_grads",
        **params(10),
    )(frames, grad_hidden, table, weights, *flat)


def on_whole_windows(
    frames,
    cotangent,
    window_live,
    language,
    task,
    ln1_gain,
    ln1_offset,
    query_weight,
    query_bias,
    key_weight,
    value_weight,
    value_bias,
    out_weight,
    out_bias,
    ln2_gain,
    ln2_offset,
    up_weight,
    up_bias,
    down_weight,
    down_bias,
):
    ow, ff = query_weight.shape[0], up_weight.shape[1]
    pieces, big, table = pack(
        window_live,
        language,
        task,
        query_weight,
        key_weight,
        value_weight,
        out_weight,
        up_weight,
        down_weight,
        up_bias,
        query_bias,
        value_bias,
        [ln1_gain, ln1_offset, out_bias, ln2_gain, ln2_offset, down_bias],
    )
    for bit in (2 * BIT_Z, BIT_Z, BIT_Y, BIT_CORE):
        pieces = jnp.concatenate([pieces, swap(pieces, bit)], axis=0)
    other_pieces = swap(pieces, BIT_X)
    big = lax.all_gather(big, ("dp", "head"), axis=0, tiled=False)

    normed, normed_t = first_norm(frames, table)
    half_done = attend_forward_fast(1, normed, pieces, table)
    q, k, v, context, lse, weights = attend_forward_fast(0, normed, other_pieces, table, half_done)

    output, grads, grad_hidden, send, keep, vec = middle(context, frames, cotangent, big, table)

    def backward(first, pairs, grads):
        return attend_backward_fast(
            first, pairs, q, k, v, lse, context, grads, normed_t, weights
        )

    came = swap(send, BIT_CORE)
    *da, dwa, vec_a = backward(0, 1, grads)
    came, grads = lax.optimization_barrier((came, grads))
    mine, vec, *sends = spread(keep, vec, [came], part_xy, (1, 2, 3), 4)
    *sends, grads, dwa, vec_a = lax.optimization_barrier((*sends, grads, dwa, vec_a))
    came_xy = [swap(s, m) for s, m in zip(sends, (BIT_X, BIT_Y, BIT_X | BIT_Y))]
    got_a = swap(dwa, BIT_X)
    *db, dwb, vec_b = backward(1, 2, grads)
    came_xy, grads, dwb, vec_b = lax.optimization_barrier((came_xy, grads, dwb, vec_b))
    mine, vec, *sends = spread(mine, vec, came_xy, part_z, (1, 2, 3), LAYERS)
    *sends, grads = lax.optimization_barrier((*sends, grads))
    came_z = [swap(s, m * BIT_Z) for s, m in zip(sends, (1, 2, 3))]
    got_b = swap(dwb[:, :, :LANES], BIT_X)
    *dc, dwc, vec_c = backward(3, 1, grads)

    send, keep_w, vec_w = gather_grads(table, dwb, dwc, got_a, got_b, (vec_a, vec_b, vec_c))
    came = swap(send, BIT_CORE)
    down_grad, up_grad, out_grad, *vectors = finish(mine, vec, came_z, ff, ow)
    mine_w, vec_w, *sends = spread(keep_w, vec_w, [came], part_y, (1, None, None), 2)
    came_y = [swap(s, m) for s, m in zip(sends, (BIT_Y, BIT_X, BIT_X | BIT_Y))]
    grad_frames = input_grads(frames, grad_hidden, table, weights, (da, db, dc))
    mine_w, vec_w, *sends = spread(mine_w, vec_w, came_y, part_z, (1, 2, 3), LAYERS)
    came_z = [swap(s, m * BIT_Z) for s, m in zip(sends, (1, 2, 3))]
    query_grad, key_grad, value_grad, *more = close(mine_w, vec_w, came_z)
    vectors = [v.reshape(-1) for v in vectors]
    more = [v.reshape(-1) for v in more]
    return (
        output,
        grad_frames,
        more[0],
        more[1],
        query_grad,
        more[2],
        key_grad,
        value_grad,
        more[3],
        out_grad,
        vectors[0],
        vectors[1],
        vectors[2],
        up_grad,
        vectors[4],
        down_grad,
        vectors[3],
    )


def solution(mesh):
    placed = (
        P(("dp", "head"), None),
        P(("dp", "head"), None),
        P(),
        P(),
        P(),
        P(),
        P(),
        P("dp", "head"),
        P(),
        P("dp", "head"),
        P("dp", "head"),
        P(),
        P("head", "dp"),
        P(),
        P(),
        P(),
        P(None, ("dp", "head")),
        P(),
        P(("dp", "head"), None),
        P(),
    )
    step = on_device
    if mesh.shape["dp"] == 4 * LAYERS and mesh.shape["head"] == SLOTS:
        step = on_whole_windows
    return jax.shard_map(
        step,
        mesh=mesh,
        in_specs=placed,
        out_specs=(
            P(("dp", "head"), None),
            P(("dp", "head"), None),
            P(),
            P(),
            P("dp", "head"),
            P(),
            P("dp", "head"),
            P("dp", "head"),
            P(),
            P("head", "dp"),
            P(),
            P(),
            P(),
            P(None, ("dp", "head")),
            P(),
            P(("dp", "head"), None),
            P(),
        ),
        check_vma=False,
    )
```

```python
import functools

import jax
import jax.numpy as jnp
from jax import lax
from jax.experimental import pallas as pl
from jax.experimental.pallas import tpu as pltpu
from jax.sharding import PartitionSpec as P

FRAMES = 1500
LANGS = 99
TASKS = 2
SLOTS = 2
HEAD_DIM = 64


def layer_norm(values, gain_vec, offset_vec):
    center = jnp.mean(values, axis=-1, keepdims=True)
    centred = values - center
    spread = jnp.mean(centred * centred, axis=-1, keepdims=True)
    return centred * lax.rsqrt(spread + 1e-05) * gain_vec + offset_vec


def gelu_exact(values):
    return jax.nn.gelu(values, approximate=False)


def contract(first_mat, second_mat):
    return lax.dot_general(
        first_mat, second_mat, (((0,), (0,)), ((), ())), preferred_element_type=jnp.float32
    )


def times_t(first_mat, second_mat):
    return lax.dot_general(
        first_mat, second_mat, (((1,), (1,)), ((), ())), preferred_element_type=jnp.float32
    )


def window_weights(window_live, language, task):
    groups = language * TASKS + task
    labels = jnp.arange(LANGS * TASKS, dtype=jnp.int32)
    matches = groups[:, None] == labels[None, :]
    live_float = window_live.astype(jnp.float32)
    counts = jnp.sum(jnp.where(matches, live_float[:, None], 0.0), axis=0)
    present = jnp.sum((counts > 0.5).astype(jnp.float32))
    own_count = jnp.sum(jnp.where(matches, counts[None, :], 0.0), axis=1)
    return live_float * jnp.sum(live_float) / (present * jnp.maximum(own_count, 1.0))


def window_scores(queries, keys_all):
    return jnp.einsum("qhd,khd->hqk", queries, keys_all, preferred_element_type=jnp.float32) * 0.125


def attend_forward(record):
    queries, keys_all, values_all = record
    scores = window_scores(queries, keys_all)
    highest_score = jnp.max(scores, axis=-1, keepdims=True)
    expo = jnp.exp(scores - highest_score)
    totals = jnp.sum(expo, axis=-1, keepdims=True)
    attn_probs = (expo / totals).astype(jnp.bfloat16)
    context = jnp.einsum("hqk,khd->qhd", attn_probs, values_all, preferred_element_type=jnp.float32)
    return (context.astype(jnp.bfloat16), (highest_score + jnp.log(totals))[..., 0])


def attend_backward(record):
    queries, keys_all, values_all, log_totals, grad_context = record
    scores = window_scores(queries, keys_all)
    attn_probs = jnp.exp(scores - log_totals[..., None])
    grad_probs = jnp.einsum(
        "qhd,khd->hqk", grad_context, values_all, preferred_element_type=jnp.float32
    )
    grad_values = jnp.einsum(
        "hqk,qhd->khd",
        attn_probs.astype(jnp.bfloat16),
        grad_context,
        preferred_element_type=jnp.float32,
    )
    row_delta = jnp.sum(grad_probs * attn_probs, axis=-1, keepdims=True)
    grad_scores = (attn_probs * (grad_probs - row_delta)).astype(jnp.bfloat16)
    grad_queries = (
        jnp.einsum("hqk,khd->qhd", grad_scores, keys_all, preferred_element_type=jnp.float32)
        * 0.125
    )
    grad_keys = (
        jnp.einsum("hqk,qhd->khd", grad_scores, queries, preferred_element_type=jnp.float32) * 0.125
    )
    return (
        grad_queries.astype(jnp.bfloat16),
        grad_keys.astype(jnp.bfloat16),
        grad_values.astype(jnp.bfloat16),
    )


def on_device(
    frames,
    cotangent,
    window_live,
    language,
    task,
    ln1_gain,
    ln1_offset,
    query_weight,
    query_bias,
    key_weight,
    value_weight,
    value_bias,
    out_weight,
    out_bias,
    ln2_gain,
    ln2_offset,
    up_weight,
    up_bias,
    down_weight,
    down_bias,
):
    local_rows = frames.shape[0]
    head_index = lax.axis_index("head")
    data_index = lax.axis_index("dp")
    per_window = window_weights(window_live, language, task)
    slot_ids = (
        head_index * local_rows + jnp.arange(local_rows, dtype=jnp.int32)
    ) // FRAMES + data_index * SLOTS
    window_ids = jnp.arange(per_window.shape[0], dtype=jnp.int32)
    frame_match = slot_ids[:, None] == window_ids[None, :]
    frame_weight = jnp.sum(jnp.where(frame_match, per_window[None, :], 0.0), axis=1)
    frame_live = jnp.sum(
        jnp.where(frame_match, window_live.astype(jnp.float32)[None, :], 0.0), axis=1
    )
    inputs = frames.astype(jnp.float32)
    normed, ln1_back = jax.vjp(layer_norm, inputs, ln1_gain, ln1_offset)
    normed_low = normed.astype(jnp.bfloat16)
    query_head, key_head, value_head, out_head = (
        lax.all_gather(query_weight, "dp", axis=0, tiled=True),
        lax.all_gather(key_weight, "dp", axis=0, tiled=True),
        lax.all_gather(value_weight, "dp", axis=0, tiled=True),
        lax.all_gather(out_weight, "dp", axis=1, tiled=True),
    )
    head_width = query_head.shape[1]
    local_heads = head_width // HEAD_DIM
    joint_weight = jnp.concatenate([query_head, key_head, value_head], axis=1)
    joint_bias = jnp.concatenate(
        [
            lax.dynamic_slice_in_dim(query_bias, head_index * head_width, head_width),
            jnp.zeros((head_width,), jnp.float32),
            lax.dynamic_slice_in_dim(value_bias, head_index * head_width, head_width),
        ]
    )
    normed_all = lax.all_gather(normed_low, "head", axis=0, tiled=True)
    projected = (
        jnp.dot(normed_all, joint_weight, preferred_element_type=jnp.float32) + joint_bias
    ).astype(jnp.bfloat16)
    shaped = projected.reshape(-1, FRAMES, 3, local_heads, HEAD_DIM)
    queries = shaped[:, :, 0]
    keys_all = shaped[:, :, 1]
    values_all = shaped[:, :, 2]
    context, log_totals = lax.map(attend_forward, (queries, keys_all, values_all))
    context_flat = context.reshape(-1, head_width)
    branch = lax.psum_scatter(
        jnp.dot(context_flat, out_head, preferred_element_type=jnp.float32),
        "head",
        scatter_dimension=0,
        tiled=True,
    )
    hidden = inputs + branch + out_bias
    normed_two, ln2_back = jax.vjp(layer_norm, hidden, ln2_gain, ln2_offset)
    normed_two_low = normed_two.astype(jnp.bfloat16)
    up_full, down_full = (
        lax.all_gather(up_weight, ("dp", "head"), axis=1, tiled=True),
        lax.all_gather(down_weight, ("dp", "head"), axis=0, tiled=True),
    )
    pre_act = jnp.dot(normed_two_low, up_full, preferred_element_type=jnp.float32) + up_bias
    activated, gelu_back = jax.vjp(gelu_exact, pre_act)
    activated_low = activated.astype(jnp.bfloat16)
    result = (
        hidden + jnp.dot(activated_low, down_full, preferred_element_type=jnp.float32) + down_bias
    )
    output = (result * frame_live[:, None]).astype(jnp.bfloat16)
    grad_result = cotangent.astype(jnp.float32) * frame_weight[:, None]
    grad_two = grad_result.astype(jnp.bfloat16)
    grad_down = contract(activated_low, grad_two)
    grad_down_bias = jnp.sum(grad_two.astype(jnp.float32), axis=0)
    grad_activated = times_t(grad_two, down_full)
    grad_pre = gelu_back(grad_activated)[0].astype(jnp.bfloat16)
    grad_up = contract(normed_two_low, grad_pre)
    grad_up_bias = jnp.sum(grad_pre.astype(jnp.float32), axis=0)
    grad_normed_two = times_t(grad_pre, up_full)
    grad_hidden_ln, grad_ln2_gain, grad_ln2_offset = ln2_back(grad_normed_two)
    grad_hidden = grad_result + grad_hidden_ln
    grad_branch = grad_hidden.astype(jnp.bfloat16)
    grad_out_bias = jnp.sum(grad_branch.astype(jnp.float32), axis=0)
    branch_all = lax.all_gather(grad_branch, "head", axis=0, tiled=True)
    grad_context = times_t(branch_all, out_head).astype(jnp.bfloat16)
    grad_out_head = contract(context_flat, branch_all)
    grad_context_win = grad_context.reshape(-1, FRAMES, local_heads, HEAD_DIM)
    grad_queries, grad_keys, grad_values = lax.map(
        attend_backward, (queries, keys_all, values_all, log_totals, grad_context_win)
    )
    grad_joint = jnp.concatenate(
        [
            grad_queries.reshape(-1, head_width),
            grad_keys.reshape(-1, head_width),
            grad_values.reshape(-1, head_width),
        ],
        axis=1,
    )
    grad_joint_weight = contract(normed_all, grad_joint)
    joint_sums = jnp.sum(grad_joint.astype(jnp.float32), axis=0)
    empty_vec = jnp.zeros((query_bias.shape[0],), jnp.float32)
    grad_query_bias = lax.dynamic_update_slice(
        empty_vec, joint_sums[:head_width], (head_index * head_width,)
    )
    grad_value_bias = lax.dynamic_update_slice(
        empty_vec, joint_sums[2 * head_width :], (head_index * head_width,)
    )
    grad_normed = lax.psum_scatter(
        times_t(grad_joint, joint_weight), "head", scatter_dimension=0, tiled=True
    )
    grad_inputs_ln, grad_ln1_gain, grad_ln1_offset = ln1_back(grad_normed)
    grad_frames = (grad_hidden + grad_inputs_ln).astype(jnp.bfloat16)
    grad_query_w, grad_key_w, grad_value_w, grad_out_w = (
        lax.psum_scatter(grad_joint_weight[:, :head_width], "dp", scatter_dimension=0, tiled=True),
        lax.psum_scatter(
            grad_joint_weight[:, head_width : 2 * head_width], "dp", scatter_dimension=0, tiled=True
        ),
        lax.psum_scatter(
            grad_joint_weight[:, 2 * head_width :], "dp", scatter_dimension=0, tiled=True
        ),
        lax.psum_scatter(grad_out_head, "dp", scatter_dimension=1, tiled=True),
    )
    grad_up_w, grad_down_w = (
        lax.psum_scatter(grad_up, ("dp", "head"), scatter_dimension=1, tiled=True),
        lax.psum_scatter(grad_down, ("dp", "head"), scatter_dimension=0, tiled=True),
    )
    (
        sum_ln1_gain,
        sum_ln1_offset,
        sum_query_bias,
        sum_value_bias,
        sum_out_bias,
        sum_ln2_gain,
        sum_ln2_offset,
        sum_up_bias,
        sum_down_bias,
    ) = lax.psum(
        (
            grad_ln1_gain,
            grad_ln1_offset,
            grad_query_bias,
            grad_value_bias,
            grad_out_bias,
            grad_ln2_gain,
            grad_ln2_offset,
            grad_up_bias,
            grad_down_bias,
        ),
        ("dp", "head"),
    )
    return (
        output,
        grad_frames,
        sum_ln1_gain,
        sum_ln1_offset,
        grad_query_w,
        sum_query_bias,
        grad_key_w,
        grad_value_w,
        sum_value_bias,
        grad_out_w,
        sum_out_bias,
        sum_ln2_gain,
        sum_ln2_offset,
        grad_up_w,
        sum_up_bias,
        grad_down_w,
        sum_down_bias,
    )


LANES = 128
PADDED = 1536
LOG2E = 1.4426950408889634
MASKED = -30000.0
F32 = jnp.float32
BF16 = jnp.bfloat16
LN1_GAIN, LN1_OFFSET, OUT_BIAS, LN2_GAIN, LN2_OFFSET, DOWN_BIAS = range(6)
WEIGHT, LIVE, QUERY_BIAS, VALUE_BIAS, UP_BIAS = 6, 7, 8, 10, 11
BIT_X, BIT_CORE, BIT_Y, BIT_Z = 1, 2, 4, 8
LAYERS = 4


def dot_on(first_mat, second_mat, first_dim, second_dim):
    return lax.dot_general(
        first_mat,
        second_mat,
        (((first_dim,), (second_dim,)), ((), ())),
        preferred_element_type=F32,
    )


def params(microseconds, mebibytes):
    return dict(
        compiler_params=pltpu.CompilerParams(vmem_limit_bytes=mebibytes << 20),
        cost_estimate=pl.CostEstimate(
            flops=int(microseconds * 1e9), bytes_accessed=1 << 20, transcendentals=0
        ),
    )


def whole(shape):
    return pl.BlockSpec(shape, lambda *_: (0,) * len(shape), pipeline_mode=pl.Buffered(1))


def struct(shape, dtype):
    return jax.ShapeDtypeStruct(shape, dtype)


def place():
    dp = lax.axis_index("dp")
    return dp, lax.axis_index("head")


def pack_kernel(
    live_ref,
    language_ref,
    task_ref,
    query_ref,
    key_ref,
    value_ref,
    out_ref,
    up_ref,
    down_ref,
    upb_ref,
    qb_ref,
    vb_ref,
    *refs,
):
    vectors, (pieces_ref, big_ref, table_ref) = refs[:6], refs[6:]
    rows, half = query_ref.shape
    ff = down_ref.shape[0]
    dp, side = place()
    for j, ref in enumerate((query_ref, key_ref, value_ref)):
        pieces_ref[0, j * rows : (j + 1) * rows, :] = ref[...]
    up = up_ref[...]
    big_ref[0:ff, :] = down_ref[:, 0:half]
    big_ref[ff : 2 * ff, :] = down_ref[:, half:]
    big_ref[2 * ff : 3 * ff, :] = up[:, 0:half]
    big_ref[3 * ff : 4 * ff, :] = up[:, half:]
    big_ref[4 * ff :, :] = out_ref[...]
    for j, ref in enumerate(vectors):
        table_ref[j : j + 1, :] = ref[...]
    for j, ref in ((QUERY_BIAS, qb_ref), (VALUE_BIAS, vb_ref)):
        first, second = ref[:, 0:half], ref[:, half:]
        table_ref[j : j + 1, 0:half] = jnp.where(side == 0, second, first)
        table_ref[j : j + 1, half:] = jnp.where(side == 0, first, second)
    table_ref[QUERY_BIAS + 1 : QUERY_BIAS + 2, :] = jnp.zeros((1, 2 * half), F32)
    for j in range(4):
        table_ref[UP_BIAS + j : UP_BIAS + j + 1, :] = upb_ref[:, j * 2 * half : (j + 1) * 2 * half]
    slots = live_ref.shape[0]
    lane = lax.broadcasted_iota(jnp.int32, (1, LANES), 1)
    groups = jnp.full((1, LANES), -1, jnp.int32)
    live = jnp.zeros((1, LANES), F32)
    for t in range(slots):
        groups = jnp.where(lane == t, language_ref[t] * TASKS + task_ref[t], groups)
        live = jnp.where(lane == t, live_ref[t].astype(F32), live)
    counts = jnp.zeros((1, LANES), F32)
    for t in range(slots):
        group = language_ref[t] * TASKS + task_ref[t]
        counts = counts + jnp.where(groups == group, live_ref[t].astype(F32), 0.0)
    counts = jnp.maximum(counts, 1.0)
    shares = jnp.broadcast_to(live / counts, (8, LANES))
    present = jnp.floor(jnp.sum(shares, axis=1, keepdims=True)[0:1] + 0.5)
    total = jnp.sum(jnp.broadcast_to(live, (8, LANES)), axis=1, keepdims=True)[0:1]
    weights = live * total / (present * counts)
    mine = lane == dp * SLOTS + side
    for j, values in ((WEIGHT, weights), (LIVE, live)):
        picked = jnp.broadcast_to(jnp.where(mine, values, 0.0), (8, LANES))
        picked = jnp.sum(picked, axis=1, keepdims=True)[0:1]
        table_ref[j : j + 1, :] = jnp.broadcast_to(picked, (1, 2 * half))


def pack(live, language, task, query, key, value, out, up, down, up_bias, qb, vb, vectors):
    rows, half = query.shape
    ff, width = down.shape
    scalars = pl.BlockSpec(memory_space=pltpu.SMEM)
    row = lambda values: values.reshape(1, -1)
    rest = [query, key, value, out.T, up.T, down, row(up_bias), row(qb), row(vb)] + [
        row(v) for v in vectors
    ]
    return pl.pallas_call(
        pack_kernel,
        in_specs=[scalars] * 3 + [pl.BlockSpec(memory_space=pltpu.VMEM)] * len(rest),
        out_shape=[
            struct((1, 3 * rows, half), BF16),
            struct((4 * ff + rows, half), BF16),
            struct((16, width), F32),
        ],
        name="pack",
        **params(3, 58),
    )(live, language, task, *rest)


def real_rows(x_ref):
    row = pl.program_id(0) * x_ref.shape[0] + lax.broadcasted_iota(jnp.int32, x_ref.shape, 0)
    return row < FRAMES


def unit_rows(values):
    centred = values - jnp.mean(values, axis=1, keepdims=True)
    scale = lax.rsqrt(jnp.mean(centred * centred, axis=1, keepdims=True) + 1e-05)
    return centred * scale, scale


def unit_back(lifted, unit, scale):
    mean_one = jnp.mean(lifted, axis=1, keepdims=True)
    mean_two = jnp.mean(lifted * unit, axis=1, keepdims=True)
    return scale * (lifted - mean_one - unit * mean_two)


def norm_kernel(x_ref, table_ref, n_ref, nt_ref):
    unit, _ = unit_rows(jnp.where(real_rows(x_ref), x_ref[...].astype(F32), 0.0))
    normed = unit * table_ref[LN1_GAIN : LN1_GAIN + 1, :] + table_ref[LN1_OFFSET : LN1_OFFSET + 1, :]
    n_ref[...] = normed.astype(BF16)
    nt_ref[...] = normed.T.astype(BF16)


def first_norm(frames, table):
    width = frames.shape[1]
    tile = 512
    return pl.pallas_call(
        norm_kernel,
        grid=(PADDED // tile,),
        in_specs=[pl.BlockSpec((tile, width), lambda i: (i, 0)), whole(table.shape)],
        out_specs=[
            pl.BlockSpec((tile, width), lambda i: (i, 0)),
            pl.BlockSpec((width, tile), lambda i: (0, i)),
        ],
        out_shape=[struct((PADDED, width), BF16), struct((width, PADDED), BF16)],
        name="first_norm",
        **params(4, 14),
    )(frames, table)


def lane_masks(shape, h):
    lane = lax.broadcasted_iota(jnp.int32, shape, 1)
    return lane >= HEAD_DIM if h else lane < HEAD_DIM


def masked(values, h):
    own = lane_masks(values.shape, h)
    return jnp.where(own, values, 0.0)


def forward_kernel(side_at, n_ref, near_ref, far_ref, table_ref, *refs):
    (
        q_ref, k_ref, v_ref, p_ref, c_ref, inv_ref, row_ref, w_ref, keys_ref, vt_ref, small_ref
    ) = refs[-11:]
    pair, step = pl.program_id(0), pl.program_id(1)
    count, rows3, half = near_ref.shape
    rows = rows3 // 3

    @pl.when((pair == 0) & (step == 0))
    def _():
        dp, _ = place()
        for core, ref in enumerate((near_ref, far_ref)):
            for t in range(count):
                owner = dp ^ ((t & 1) * 8 + (t & 2) * 2 + (t & 4) // 2 + core)
                at = pl.ds(pl.multiple_of(owner * rows, rows), rows)
                for j in range(3):
                    w_ref[j, at, :] = ref[t, j * rows : (j + 1) * rows, :]

    @pl.when(step == 0)
    def _():
        columns = pl.ds(pl.multiple_of(pair * LANES, LANES), LANES)
        places = pl.ds(pl.multiple_of(pair * LANES + side_at * half, LANES), LANES)
        for j, out in enumerate((q_ref, k_ref, v_ref)):
            bias = table_ref[QUERY_BIAS + j : QUERY_BIAS + j + 1, places]
            out[...] = (dot_on(n_ref[...], w_ref[j, :, columns], 1, 0) + bias).astype(BF16)
        keys = k_ref[...].astype(F32) * (LOG2E * 0.125)
        queries = q_ref[...].astype(F32)
        high = keys.astype(BF16).astype(F32)
        flipped = v_ref[...].astype(F32).T
        shape = (vt_ref.shape[1], flipped.shape[1])
        real = lax.broadcasted_iota(jnp.int32, shape, 1) < FRAMES
        first = lax.broadcasted_iota(jnp.int32, shape, 0) == HEAD_DIM
        small = None
        for h in (0, 1):
            keys_ref[h, :, 0:LANES] = masked(high, h).astype(BF16)
            keys_ref[h, :, LANES:] = masked(keys - high, h).astype(BF16)
            mine = flipped[HEAD_DIM * h : HEAD_DIM * (h + 1), :]
            mine = jnp.concatenate([mine, mine[0 : shape[0] - HEAD_DIM]], axis=0)
            vt_ref[h] = jnp.where(real, jnp.where(first, 1.0, mine), 0.0).astype(BF16)
            norms = [
                jnp.max(jnp.sum(masked(m * m, h), axis=1, keepdims=True)) for m in (queries, keys)
            ]
            fits = (norms[0] < 1e18) & (norms[1] < 1e18) & (norms[0] * norms[1] < 50.0 * 50.0)
            small = fits if small is None else small & fits
        small_ref[0] = small.astype(jnp.int32)

    tile = c_ref.shape[0]
    tail = FRAMES // 16 * 16

    def attend(start, size, at, shift):
        queries = q_ref[pl.ds(start, size), :]
        queries = jnp.concatenate([queries, queries], axis=1)
        contexts, inverses = [], []
        for h in (0, 1):
            scores = dot_on(keys_ref[h], queries, 1, 1)
            if shift:
                real = lax.broadcasted_iota(jnp.int32, scores.shape, 0) < FRAMES
                scores = jnp.where(real, scores, -1e30)
                scores = scores - jnp.max(scores, axis=0, keepdims=True)
            probs = jnp.exp2(scores)
            low = probs.astype(BF16)
            p_ref[h, 0:tail, at] = low[0:tail]
            last = probs[tail:]
            real = lax.broadcasted_iota(jnp.int32, last.shape, 0) < FRAMES - tail
            p_ref[h, tail:, at] = jnp.where(real, last, 0.0).astype(BF16)
            summed = dot_on(vt_ref[h], low, 1, 0)
            inverse = 1.0 / summed[HEAD_DIM : HEAD_DIM + 1, :]
            row_ref[h : h + 1, at] = inverse
            contexts.append(summed[0:HEAD_DIM, :] * inverse)
            inverses.append(jnp.broadcast_to(inverse, (HEAD_DIM, inverse.shape[1])))
        return jnp.concatenate(contexts, axis=0).T.astype(BF16), jnp.concatenate(inverses, axis=0).T

    @pl.when(small_ref[0] == 1)
    def _():
        c_ref[...], inv_ref[...] = attend(step * tile, tile, slice(0, tile), False)

    @pl.when(small_ref[0] == 0)
    def _():
        size = 2 * LANES

        @pl.loop(0, tile // size)
        def _(t):
            at = pl.ds(pl.multiple_of(t * size, size), size)
            start = pl.multiple_of(step * tile + t * size, size)
            c_ref[at, :], inv_ref[at, :] = attend(start, size, at, True)


def attend_forward_fast(side_at, normed, near, far, table, before=()):
    rows, width = normed.shape
    half = near.shape[2]
    pairs = half // LANES
    tile = 768
    at = side_at * pairs
    block = pl.BlockSpec((tile, LANES), lambda p, i: (i, p + at))
    full = pl.BlockSpec((rows, LANES), lambda p, i: (0, p + at))
    weights = pl.BlockSpec((3, width, half), lambda p, i: (0, 0, side_at))
    return pl.pallas_call(
        functools.partial(forward_kernel, side_at),
        grid=(pairs, rows // tile),
        in_specs=[whole(normed.shape), whole(near.shape), whole(far.shape), whole(table.shape)]
        + [pl.BlockSpec(memory_space=pl.ANY)] * len(before),
        out_specs=[
            full, full, full,
            pl.BlockSpec((2, rows, tile), lambda p, i: (p + at, 0, i)),
            block, block,
            pl.BlockSpec((None, 8, tile), lambda p, i: (p + at, 0, i)),
            weights,
        ],
        out_shape=[struct((rows, width), BF16)] * 3
        + [
            struct((width // HEAD_DIM, rows, rows), BF16),
            struct((rows, width), BF16),
            struct((rows, width), F32),
            struct((width // LANES, 8, rows), F32),
            struct((3, width, width), BF16),
        ],
        scratch_shapes=[
            pltpu.VMEM((2, rows, 2 * LANES), BF16),
            pltpu.VMEM((2, HEAD_DIM + 16, rows), BF16),
            pltpu.SMEM((1,), jnp.int32),
        ],
        input_output_aliases={4 + j: j for j in range(len(before))},
        name="attend_forward",
        **params(15, 40),
    )(normed, near, far, table, *before)


def backward_kernel(
    first, q_ref, k_ref, v_ref, p_ref, inv_ref, row_ref, c_ref, g_ref, nt_ref, w_ref, vec_in_ref, *refs
):
    dq_ref, dk_ref, dv_ref, dw_ref, vec_ref, vals_ref, kt_ref, acck, accv, acc_one, acc_two = refs[-11:]
    pair, step = pl.program_id(0), pl.program_id(1)
    last = step == pl.num_programs(1) - 1

    @pl.when(step == 0)
    def _():
        values = v_ref[...].astype(F32)
        for h in (0, 1):
            vals_ref[h] = masked(values, h).astype(BF16)
        kt_ref[...] = k_ref[...].astype(F32).T.astype(BF16)
        acck[...] = jnp.zeros_like(acck)
        accv[...] = jnp.zeros_like(accv)

    tile = q_ref.shape[0]
    plain = q_ref[...].astype(F32)
    grads = g_ref[...].astype(F32)
    products = (grads * c_ref[...].astype(F32)).T
    divided = grads * inv_ref[...]
    diffs, queries, outers, flipped = [], [], [], []
    for h in (0, 1):
        rows = slice(HEAD_DIM * h, HEAD_DIM * (h + 1))
        row_delta = jnp.sum(products[rows], axis=0, keepdims=True)
        grad_probs = dot_on(vals_ref[h], g_ref[...], 1, 1)
        scaled = (grad_probs - row_delta) * row_ref[h : h + 1, :]
        diff = (p_ref[h].astype(F32) * scaled).astype(BF16)
        diffs.append(diff)
        outers.append(masked(divided, h).astype(BF16))
        queries.append(masked(plain, h).astype(BF16))
        flipped.append(dot_on(kt_ref[rows, :], diff, 1, 0))
    accv[...] += dot_on(p_ref[0], outers[0], 1, 0) + dot_on(p_ref[1], outers[1], 1, 0)
    acck[...] += dot_on(diffs[0], queries[0], 1, 0) + dot_on(diffs[1], queries[1], 1, 0)
    at = pl.ds(pl.multiple_of(step * tile, tile), tile)
    dq_ref[at, :] = (jnp.concatenate(flipped, axis=0) * 0.125).T.astype(BF16)

    @pl.when(last & (pair == 0))
    def _():
        acc_one[...] = jnp.zeros_like(acc_one)
        acc_two[...] = jnp.zeros_like(acc_two)
        vec_ref[...] = vec_in_ref[...]

    @pl.when(last)
    def _():
        dk_ref[...] = (acck[...] * 0.125).astype(BF16)
        dv_ref[...] = accv[...].astype(BF16)
        columns = pl.ds(pl.multiple_of((pair + first) * LANES, LANES), LANES)
        for j, ref in enumerate((dq_ref, dk_ref, dv_ref)):
            dw = dot_on(nt_ref[...], ref[...], 1, 0)
            dw_ref[j] = dw.astype(dw_ref.dtype)
            column_sums = jnp.sum(ref[...].astype(F32), axis=0, keepdims=True)
            weights = w_ref[j].astype(F32)
            acc_one[...] += weights * dw
            acc_two[...] += weights * column_sums
            if j != 1:
                vec_ref[2 + j // 2 : 3 + j // 2, columns] = column_sums

    @pl.when(last & (pair == pl.num_programs(0) - 1))
    def _():
        for j, ref in enumerate((acc_one, acc_two)):
            vec_ref[j : j + 1, :] += jnp.sum(ref[...].T, axis=0, keepdims=True)


def attend_backward_fast(
    first, pairs, q, k, v, probs, inverse, rows_inverse, context, grads, normed_t, weights, vec,
    before=(),
):
    rows, width = q.shape
    half = width // 2
    tile = 512
    block = pl.BlockSpec((tile, LANES), lambda p, i: (i, p + first))
    full = pl.BlockSpec((rows, LANES), lambda p, i: (0, p + first))
    gradient = pl.BlockSpec(
        (None, 3, width, LANES), lambda p, i: ((p + first) // 2, 0, 0, (p + first) % 2)
    )
    in_specs = [
        block, full, full,
        pl.BlockSpec((2, rows, tile), lambda p, i: (p + first, 0, i)),
        block,
        pl.BlockSpec((None, 8, tile), lambda p, i: (p + first, 0, i)),
        block, block, whole(normed_t.shape),
        pl.BlockSpec((3, width, LANES), lambda p, i: (0, 0, p + first)),
        whole(vec.shape),
    ]
    count = len(in_specs)
    return pl.pallas_call(
        functools.partial(backward_kernel, first),
        grid=(pairs, rows // tile),
        in_specs=in_specs + [pl.BlockSpec(memory_space=pl.ANY)] * len(before),
        out_specs=[full, full, full, gradient, whole(vec.shape)],
        out_shape=[struct((rows, width), BF16)] * 3
        + [struct((2, 3, width, half), BF16), struct(vec.shape, F32)],
        scratch_shapes=[
            pltpu.VMEM((2, rows, LANES), BF16),
            pltpu.VMEM((LANES, rows), BF16),
            pltpu.VMEM((rows, LANES), F32),
            pltpu.VMEM((rows, LANES), F32),
            pltpu.VMEM((width, LANES), F32),
            pltpu.VMEM((width, LANES), F32),
        ],
        input_output_aliases={count + j: j for j in range(len(before))},
        name="attend_backward",
        **params(14 * pairs, 34),
    )(q, k, v, probs, inverse, rows_inverse, context, grads, normed_t, weights, vec, *before)


def middle_kernel(masks, c_ref, x_ref, cot_ref, table_ref, *refs):
    pieces, refs = refs[: len(masks)], refs[len(masks) :]
    out_ref, g_ref, gh_ref, send_ref, keep_ref, vec_ref = refs[:6]
    up_t, up_n, down_n, down_t, out_t, upb_t, acc_up, acc_down, acc_out, acc_upb, acc_vec = refs[6:]
    step = pl.program_id(0)
    dp, side = place()
    core = lax.rem(dp, 2)
    layers, piece_rows, half = pieces[0].shape
    devices = layers * len(masks)
    width = 2 * half
    ow = width // (devices // 2)
    ff = (piece_rows - ow) // 4
    hidden_all = devices * ff
    chunk = 512
    chunks = hidden_all // chunk

    @pl.when(step == 0)
    def _():
        for mask, ref in zip(masks, pieces):
            for t in range(layers):
                owner = (dp * 2 + side) ^ (mask + (t & 1) * 2 * BIT_Z + (t & 2) // 2 * BIT_Z)
                rows = pl.ds(pl.multiple_of(owner * ff, ff), ff)
                down_n[rows, 0:half] = ref[t, 0:ff, :]
                down_n[rows, half:] = ref[t, ff : 2 * ff, :]
                up_t[rows, 0:half] = ref[t, 2 * ff : 3 * ff, :]
                up_t[rows, half:] = ref[t, 3 * ff : 4 * ff, :]
                rows = pl.ds(pl.multiple_of((owner >> 1) * ow, ow), ow)
                at = slice(0, half) if mask & BIT_X else slice(half, width)
                out_t[rows, at] = ref[t, 4 * ff :, :]
        for j in range(chunks):
            rows = slice(j * chunk, (j + 1) * chunk)
            up_n[:, rows] = up_t[rows, :].T
            down_t[:, rows] = down_n[rows, :].T
            bias = table_ref[UP_BIAS + j : UP_BIAS + j + 1, :]
            upb_t[rows, :] = jnp.broadcast_to(bias, (LANES, chunk)).T
        acc_up[...] = jnp.zeros_like(acc_up)
        acc_down[...] = jnp.zeros_like(acc_down)
        acc_out[...] = jnp.zeros_like(acc_out)
        acc_upb[...] = jnp.zeros_like(acc_upb)
        acc_vec[...] = jnp.zeros_like(acc_vec)

    def row_of(j):
        return table_ref[j : j + 1, :]

    tile = x_ref.shape[0]
    real = real_rows(x_ref)
    branch = dot_on(c_ref[...], out_t[...], 1, 1)
    hidden = jnp.where(real, x_ref[...].astype(F32), 0.0) + branch + row_of(OUT_BIAS)
    unit, scale = unit_rows(hidden)
    normed = (unit * row_of(LN2_GAIN) + row_of(LN2_OFFSET)).astype(BF16)
    grad_result = jnp.where(real, cot_ref[...].astype(F32), 0.0) * row_of(WEIGHT)
    grad_two = grad_result.astype(BF16)
    result_t = jnp.zeros((width, tile), F32)
    grad_normed_t = jnp.zeros((width, tile), F32)
    for j in range(chunks):
        rows = slice(j * chunk, (j + 1) * chunk)
        slots = slice(j * chunk // ff, (j + 1) * chunk // ff)
        pre = dot_on(up_t[rows, :], normed, 1, 1) + upb_t[rows, 0:1]
        bell = 0.5 + 0.5 * lax.erf(pre * 0.7071067811865476)
        slope = bell + pre * (jnp.exp2(pre * pre * (-0.5 * LOG2E)) * 0.3989422804014327)
        activated = (pre * bell).astype(BF16)
        result_t += dot_on(down_t[:, rows], activated, 1, 0)
        acc_down[slots] += dot_on(activated, grad_two, 1, 0).reshape(-1, ff, width)
        grad_pre = (dot_on(down_n[rows, :], grad_two, 1, 1) * slope).astype(BF16)
        rounded = grad_pre.astype(F32)
        partial = rounded[:, 0:LANES]
        for lanes in range(LANES, tile, LANES):
            partial += rounded[:, lanes : lanes + LANES]
        acc_upb[rows, :] += partial
        acc_up[slots] += dot_on(grad_pre, normed, 1, 0).reshape(-1, ff, width)
        grad_normed_t += dot_on(up_n[:, rows], grad_pre, 1, 0)
    result = hidden + result_t.T + row_of(DOWN_BIAS)
    out_ref[...] = (result * row_of(LIVE)).astype(BF16)
    grad_normed = grad_normed_t.T
    grad_hidden = grad_result + unit_back(grad_normed * row_of(LN2_GAIN), unit, scale)
    gh_ref[...] = grad_hidden
    grad_branch = grad_hidden.astype(BF16)
    g_ref[...] = dot_on(grad_branch, out_t[...], 1, 0).astype(BF16)
    acc_out[...] += dot_on(grad_hidden.T.astype(BF16), c_ref[...], 1, 0).reshape(-1, ow, width)
    for j, term in enumerate(
        (grad_branch.astype(F32), grad_normed * unit, grad_normed, grad_two.astype(F32))
    ):
        acc_vec[8 * j : 8 * j + 8, :] += jnp.sum(term.reshape(-1, 8, width), axis=0)

    @pl.when(step == pl.num_programs(0) - 1)
    def _():
        targets = devices // 2
        for ref, bit in ((keep_ref, core), (send_ref, 1 - core)):
            for t in range(targets):
                y, x, z = t // (2 * LAYERS), t // LAYERS % 2, t % LAYERS
                at = t * piece_rows
                chip = z * 2 + y
                slot = chip * 4 + bit * 2 + x
                near = pl.ds(pl.multiple_of((1 - (side ^ x)) * half, half), half)
                ref[at : at + ff, :] = acc_down[slot, :, 0:half].astype(BF16)
                ref[at + ff : at + 2 * ff, :] = acc_down[slot, :, half:].astype(BF16)
                ref[at + 2 * ff : at + 3 * ff, :] = acc_up[slot, :, 0:half].astype(BF16)
                ref[at + 3 * ff : at + 4 * ff, :] = acc_up[slot, :, half:].astype(BF16)
                ref[at + 4 * ff : at + piece_rows, :] = acc_out[chip * 2 + bit, :, near].astype(BF16)
        for j in range(4):
            total = jnp.sum(acc_vec[8 * j : 8 * j + 8, :], axis=0, keepdims=True)
            vec_ref[2 * j : 2 * j + 1, :] = total[:, 0:half]
            vec_ref[2 * j + 1 : 2 * j + 2, :] = total[:, half:]
        for j in range(chunks):
            total = jnp.sum(acc_upb[j * chunk : (j + 1) * chunk, :].T, axis=0, keepdims=True)
            for i in range(chunk // half):
                at = 8 + j * (chunk // half) + i
                vec_ref[at : at + 1, :] = total[:, i * half : (i + 1) * half]
        store_two(send_ref, targets * piece_rows, vec_ref[...])


def middle(context, frames, cotangent, table, masks, pieces):
    rows, width = context.shape
    layers, piece_rows, half = pieces[0].shape
    devices = layers * len(masks)
    tile = 512
    ow = width // (devices // 2)
    ff = (piece_rows - ow) // 4
    hidden_all = devices * ff
    body = devices // 2 * piece_rows
    wide = pl.BlockSpec((tile, width), lambda i: (i, 0))
    return pl.pallas_call(
        functools.partial(middle_kernel, masks),
        grid=(rows // tile,),
        in_specs=[wide, wide, wide, whole(table.shape)] + [whole(p.shape) for p in pieces],
        out_specs=[wide, wide, wide, whole((body + 32, half)), whole((body, half)), whole((16, half))],
        out_shape=[
            struct(frames.shape, BF16),
            struct((rows, width), BF16),
            struct((rows, width), F32),
            struct((body + 32, half), BF16),
            struct((body, half), BF16),
            struct((16, half), F32),
        ],
        scratch_shapes=[
            pltpu.VMEM((hidden_all, width), BF16),
            pltpu.VMEM((width, hidden_all), BF16),
            pltpu.VMEM((hidden_all, width), BF16),
            pltpu.VMEM((width, hidden_all), BF16),
            pltpu.VMEM((width, width), BF16),
            pltpu.VMEM((hidden_all, LANES), F32),
            pltpu.VMEM((devices, ff, width), F32),
            pltpu.VMEM((devices, ff, width), F32),
            pltpu.VMEM((width // ow, ow, width), F32),
            pltpu.VMEM((hidden_all, LANES), F32),
            pltpu.VMEM((32, width), F32),
        ],
        name="middle",
        **params(38, 48),
    )(context, frames, cotangent, table, *pieces)


def store_two(ref, at, values):
    count = values.shape[0]
    high = values.astype(BF16)
    ref[at : at + count, :] = high
    ref[at + count : at + 2 * count, :] = (values - high.astype(F32)).astype(BF16)


def load_two(ref, at, count):
    return ref[at : at + count, :].astype(F32) + ref[at + count : at + 2 * count, :].astype(F32)


def spread_kernel(count, masks, keep_ref, vec_ref, *refs):
    came, (mine_ref, sum_ref, *sends) = refs[:count], refs[count:]
    size, half = mine_ref.shape
    dp, side = place()
    parts = keep_ref.shape[0] // size
    vec_rows = vec_ref.shape[0]
    vec = vec_ref[...]
    for ref in came:
        vec += load_two(ref, ref.shape[0] - 2 * vec_rows, vec_rows)
    sum_ref[...] = vec

    def total(part):
        rows = pl.ds(pl.multiple_of(part * size, 32), size)
        values = keep_ref[rows, :].astype(F32)
        for ref in came:
            if ref.shape[0] > 2 * vec_rows:
                values += ref[rows, :].astype(F32)
        return values

    own = masks[0](dp, side)
    mine_ref[...] = total(own)
    for mask, ref in zip(masks[1:], sends):
        if mask is not None:
            ref[0:size, :] = total(own ^ mask).astype(BF16)
        store_two(ref, ref.shape[0] - 2 * vec_rows, vec)


def spread(keep, vec, came, own_part, masks, parts):
    rows, half = keep.shape
    size = rows // parts
    tail = 2 * vec.shape[0]
    vmem = pl.BlockSpec(memory_space=pltpu.VMEM)
    return pl.pallas_call(
        functools.partial(spread_kernel, len(came), (own_part, *masks)),
        in_specs=[vmem] * (2 + len(came)),
        out_specs=[vmem] * (2 + len(masks)),
        out_shape=[struct((size, half), F32), struct(vec.shape, F32)]
        + [struct(((0 if m is None else size) + tail, half), BF16) for m in masks],
        name="spread",
        **params(3, 14),
    )(keep, vec, *came)


def swap(values, mask):
    devices = lax.axis_size("dp") * lax.axis_size("head")
    return lax.ppermute(values, ("dp", "head"), [(i, i ^ mask) for i in range(devices)])


def part_xy(dp, side):
    return ((dp >> 1) & 1) * 2 + side


def part_y(dp, side):
    return (dp >> 1) & 1


def part_z(dp, side):
    return dp >> 2


def gather_kernel(table_ref, dw_ref, got_ref, vec_in_ref, send_ref, keep_ref, vec_ref, vsend_ref):
    dp, side = place()
    core = lax.rem(dp, 2)
    width = table_ref.shape[1]
    half = width // 2
    ow = width // 16
    for ref, bit in ((keep_ref, core), (send_ref, 1 - core)):
        for t in range(2 * LAYERS):
            chip = t % LAYERS * 2 + t // LAYERS
            rows = pl.ds(pl.multiple_of((chip * 2 + bit) * ow, ow), ow)
            for j in range(3):
                at = t * 3 * ow + j * ow
                both = dw_ref[j, rows, :].astype(F32) + got_ref[j, rows, :].astype(F32)
                ref[at : at + ow, :] = both.astype(ref.dtype)
    one, two = vec_in_ref[0:1, :], vec_in_ref[1:2, :]
    gain = table_ref[LN1_GAIN : LN1_GAIN + 1, :]
    offset = table_ref[LN1_OFFSET : LN1_OFFSET + 1, :]
    grad_gain = (one - offset * two) / gain
    for j, values in ((0, grad_gain), (2, two)):
        vec_ref[j : j + 1, :] = values[:, 0:half]
        vec_ref[j + 1 : j + 2, :] = values[:, half:]
    for j in (0, 1):
        other, own = vec_in_ref[2 + j : 3 + j, 0:half], vec_in_ref[2 + j : 3 + j, half:]
        vec_ref[4 + 2 * j : 5 + 2 * j, :] = jnp.where(side == 0, own, other)
        vec_ref[5 + 2 * j : 6 + 2 * j, :] = jnp.where(side == 0, other, own)
    store_two(send_ref, 24 * ow, vec_ref[...])
    store_two(vsend_ref, 0, vec_ref[...])


def gather_grads(table, dw, got, vec):
    width = table.shape[1]
    half = width // 2
    rows = 24 * (width // 16)
    shapes = [((rows + 16, half), BF16), ((rows, half), F32), ((8, half), F32), ((16, half), BF16)]
    return pl.pallas_call(
        gather_kernel,
        grid=(1,),
        in_specs=[
            whole(table.shape),
            pl.BlockSpec((None, 3, width, half), lambda i: (1, 0, 0, 0)),
            whole(got.shape),
            whole(vec.shape),
        ],
        out_specs=[whole(shape) for shape, _ in shapes],
        out_shape=[struct(*shape) for shape in shapes],
        name="gather_grads",
        **params(2, 12),
    )(table, dw, got, vec)


def finish_kernel(ff, ow, mine_ref, vec_ref, mine_w_ref, vec_w_ref, *refs):
    came, came_w, outs = refs[: LAYERS - 1], refs[LAYERS - 1 : 2 * LAYERS - 2], refs[2 * LAYERS - 2 :]
    down_ref, up_ref, out_ref, *outs = outs

    def total(mine, vec, parts):
        size = mine.shape[0]
        values, sums = mine[...], vec[...]
        for ref in parts:
            values += ref[0:size, :].astype(F32)
            sums += load_two(ref, size, vec.shape[0])
        return values, sums

    half = mine_ref.shape[1]
    values, vec = total(mine_ref, vec_ref, came)
    down_ref[:, 0:half] = values[0:ff]
    down_ref[:, half:] = values[ff : 2 * ff]
    up_ref[:, 0:half] = values[2 * ff : 3 * ff]
    up_ref[:, half:] = values[3 * ff : 4 * ff]
    out_ref[...] = values[4 * ff :]
    values, vec_w = total(mine_w_ref, vec_w_ref, came_w)
    for j in range(3):
        outs[j][...] = values[j * ow : (j + 1) * ow]
    at = 0
    rows = [vec[j : j + 1] for j in range(vec.shape[0])] + [
        vec_w[j : j + 1] for j in range(vec_w.shape[0])
    ]
    for ref in outs[3:]:
        for j in range(ref.shape[1] // half):
            ref[:, j * half : (j + 1) * half] = rows[at]
            at += 1


def finish(mine, vec, mine_w, vec_w, came, came_w, ff, ow):
    half = mine.shape[1]
    vmem = pl.BlockSpec(memory_space=pltpu.VMEM)
    shapes = [(ff, 2 * half), (ff, 2 * half), (ow, half)] + [(ow, half)] * 3
    shapes += [(1, 2 * half)] * 4 + [(1, 8 * half)] + [(1, 2 * half)] * 4
    return pl.pallas_call(
        functools.partial(finish_kernel, ff, ow),
        in_specs=[vmem] * (4 + len(came) + len(came_w)),
        out_specs=[vmem] * len(shapes),
        out_shape=[struct(shape, F32) for shape in shapes],
        name="finish",
        **params(3, 12),
    )(mine, vec, mine_w, vec_w, *came, *came_w)


def input_grad_kernel(x_ref, gh_ref, table_ref, w_ref, dq_ref, dk_ref, dv_ref, gf_ref):
    total = dot_on(dq_ref[...], w_ref[0], 1, 1)
    total += dot_on(dk_ref[...], w_ref[1], 1, 1)
    total += dot_on(dv_ref[...], w_ref[2], 1, 1)
    unit, scale = unit_rows(jnp.where(real_rows(x_ref), x_ref[...].astype(F32), 0.0))
    lifted = total * table_ref[LN1_GAIN : LN1_GAIN + 1, :]
    gf_ref[...] = (gh_ref[...] + unit_back(lifted, unit, scale)).astype(BF16)


def input_grads(frames, grad_hidden, table, weights, grads):
    rows, width = grad_hidden.shape
    tile = 512
    wide = pl.BlockSpec((tile, width), lambda i: (i, 0))
    return pl.pallas_call(
        input_grad_kernel,
        grid=(rows // tile,),
        in_specs=[wide, wide, whole(table.shape), whole(weights.shape), wide, wide, wide],
        out_specs=wide,
        out_shape=struct(frames.shape, BF16),
        name="input_grads",
        **params(9, 20),
    )(frames, grad_hidden, table, weights, *grads)


def on_whole_windows(
    frames,
    cotangent,
    window_live,
    language,
    task,
    ln1_gain,
    ln1_offset,
    query_weight,
    query_bias,
    key_weight,
    value_weight,
    value_bias,
    out_weight,
    out_bias,
    ln2_gain,
    ln2_offset,
    up_weight,
    up_bias,
    down_weight,
    down_bias,
):
    ow, ff = query_weight.shape[0], up_weight.shape[1]
    pieces, big, table = pack(
        window_live,
        language,
        task,
        query_weight,
        key_weight,
        value_weight,
        out_weight,
        up_weight,
        down_weight,
        up_bias,
        query_bias,
        value_bias,
        [ln1_gain, ln1_offset, out_bias, ln2_gain, ln2_offset, down_bias],
    )
    together = lax.optimization_barrier

    def doubled(values, came):
        return jnp.concatenate([values, came], axis=0)

    came = swap(pieces, 2 * BIT_Z)
    normed, normed_t = first_norm(frames, table)
    came, normed, big = together((came, normed, big[None]))
    pieces = doubled(pieces, came)
    came, came_big = together((swap(pieces, BIT_Z), swap(big, 2 * BIT_Z)))
    pieces, big = doubled(pieces, came), doubled(big, came_big)
    came, came_big = together((swap(pieces, BIT_Y), swap(big, BIT_Z)))
    near, big = doubled(pieces, came), doubled(big, came_big)
    far = swap(near, BIT_CORE)
    near_other = swap(near, BIT_X)

    normed_one, big, far = together((normed, big, far))
    big_y = swap(big, BIT_Y)
    big_x = swap(big, BIT_X)
    half_done = list(attend_forward_fast(1, normed_one, near, far, table))
    near_other, big_y, big_x, half_done[4] = together((near_other, big_y, big_x, half_done[4]))
    far_other = swap(near_other, BIT_CORE)
    big_xy = swap(big_y, BIT_X)
    across = [swap(p, BIT_CORE) for p in (big, big_y, big_x)]
    q, k, v, probs, context, inverse, rows_inverse, weights = attend_forward_fast(
        0, normed, near_other, far_other, table, half_done
    )
    big_xy, context = together((big_xy, context))
    across.append(swap(big_xy, BIT_CORE))
    masks = (0, BIT_Y, BIT_X, BIT_X | BIT_Y)
    masks += tuple(m | BIT_CORE for m in masks)
    output, grads, grad_hidden, send, keep, vec = middle(
        context, frames, cotangent, table, masks, [big, big_y, big_x, big_xy, *across]
    )

    def backward(first, pairs, grads, vec, before=()):
        return attend_backward_fast(
            first, pairs, q, k, v, probs, inverse, rows_inverse, context, grads, normed_t, weights,
            vec, before,
        )

    came = swap(send, BIT_CORE)
    *done, vec_w = backward(0, 1, grads, jnp.zeros_like(table[0:8]))
    came, grads = lax.optimization_barrier((came, grads))
    mine, vec, *sends = spread(keep, vec, [came], part_xy, (1, 2, 3), 4)
    *sends, grads = lax.optimization_barrier((*sends, grads))
    came_xy = [swap(s, m) for s, m in zip(sends, (BIT_X, BIT_Y, BIT_X | BIT_Y))]
    *done, vec_w = backward(1, 2, grads, vec_w, done)
    across = done[3][0]
    came_xy, grads, across = lax.optimization_barrier((came_xy, grads, across))
    mine, vec, *sends = spread(mine, vec, came_xy, part_z, (1, 2, 3), LAYERS)
    *sends, grads, across = lax.optimization_barrier((*sends, grads, across))
    got = swap(across, BIT_X)
    came_z = [swap(s, m * BIT_Z) for s, m in zip(sends, (1, 2, 3))]
    *done, dw, vec_w = backward(3, 1, grads, vec_w, done)

    came_z, vec_w = lax.optimization_barrier((came_z, vec_w))
    send, keep_w, vec_w, vec_send = gather_grads(table, dw, got, vec_w)
    came = [swap(send, BIT_CORE), swap(vec_send, BIT_X), swap(vec_send, BIT_X | BIT_CORE)]
    mine_w, vec_w, send = spread(keep_w, vec_w, came, part_y, (1,), 2)
    came = [swap(send, BIT_Y)]
    grad_frames = input_grads(frames, grad_hidden, table, weights, done)
    came, grad_frames = lax.optimization_barrier((came, grad_frames))
    mine_w, vec_w, *sends = spread(mine_w, vec_w, came, part_z, (1, 2, 3), LAYERS)
    came_w = [swap(s, m * BIT_Z) for s, m in zip(sends, (1, 2, 3))]
    down_grad, up_grad, out_grad, query_grad, key_grad, value_grad, *vectors = finish(
        mine, vec, mine_w, vec_w, came_z, came_w, ff, ow
    )
    vectors = [v.reshape(-1) for v in vectors]
    out_bias_grad, gain_two, offset_two, down_bias_grad, up_bias_grad = vectors[:5]
    gain_one, offset_one, query_bias_grad, value_bias_grad = vectors[5:]
    return (
        output,
        grad_frames,
        gain_one,
        offset_one,
        query_grad,
        query_bias_grad,
        key_grad,
        value_grad,
        value_bias_grad,
        out_grad.T,
        out_bias_grad,
        gain_two,
        offset_two,
        up_grad.T,
        up_bias_grad,
        down_grad,
        down_bias_grad,
    )


def solution(mesh):
    placed = (
        P(("dp", "head"), None),
        P(("dp", "head"), None),
        P(),
        P(),
        P(),
        P(),
        P(),
        P("dp", "head"),
        P(),
        P("dp", "head"),
        P("dp", "head"),
        P(),
        P("head", "dp"),
        P(),
        P(),
        P(),
        P(None, ("dp", "head")),
        P(),
        P(("dp", "head"), None),
        P(),
    )
    step = on_device
    if mesh.shape["dp"] == 4 * LAYERS and mesh.shape["head"] == SLOTS:
        step = on_whole_windows
    return jax.shard_map(
        step,
        mesh=mesh,
        in_specs=placed,
        out_specs=(
            P(("dp", "head"), None),
            P(("dp", "head"), None),
            P(),
            P(),
            P("dp", "head"),
            P(),
            P("dp", "head"),
            P("dp", "head"),
            P(),
            P("head", "dp"),
            P(),
            P(),
            P(),
            P(None, ("dp", "head")),
            P(),
            P(("dp", "head"), None),
            P(),
        ),
        check_vma=False,
    )
```

```python
import functools

import jax
import jax.numpy as jnp
from jax import lax
from jax.experimental import pallas as pl
from jax.experimental.pallas import tpu as pltpu
from jax.sharding import PartitionSpec as P

FRAMES = 1500
LANGS = 99
TASKS = 2
SLOTS = 2
HEAD_DIM = 64


def layer_norm(values, gain_vec, offset_vec):
    center = jnp.mean(values, axis=-1, keepdims=True)
    centred = values - center
    spread = jnp.mean(centred * centred, axis=-1, keepdims=True)
    return centred * lax.rsqrt(spread + 1e-05) * gain_vec + offset_vec


def gelu_exact(values):
    return jax.nn.gelu(values, approximate=False)


def contract(first_mat, second_mat):
    return lax.dot_general(
        first_mat, second_mat, (((0,), (0,)), ((), ())), preferred_element_type=jnp.float32
    )


def times_t(first_mat, second_mat):
    return lax.dot_general(
        first_mat, second_mat, (((1,), (1,)), ((), ())), preferred_element_type=jnp.float32
    )


def window_weights(window_live, language, task):
    groups = language * TASKS + task
    labels = jnp.arange(LANGS * TASKS, dtype=jnp.int32)
    matches = groups[:, None] == labels[None, :]
    live_float = window_live.astype(jnp.float32)
    counts = jnp.sum(jnp.where(matches, live_float[:, None], 0.0), axis=0)
    present = jnp.sum((counts > 0.5).astype(jnp.float32))
    own_count = jnp.sum(jnp.where(matches, counts[None, :], 0.0), axis=1)
    return live_float * jnp.sum(live_float) / (present * jnp.maximum(own_count, 1.0))


def window_scores(queries, keys_all):
    return jnp.einsum("qhd,khd->hqk", queries, keys_all, preferred_element_type=jnp.float32) * 0.125


def attend_forward(record):
    queries, keys_all, values_all = record
    scores = window_scores(queries, keys_all)
    highest_score = jnp.max(scores, axis=-1, keepdims=True)
    expo = jnp.exp(scores - highest_score)
    totals = jnp.sum(expo, axis=-1, keepdims=True)
    attn_probs = (expo / totals).astype(jnp.bfloat16)
    context = jnp.einsum("hqk,khd->qhd", attn_probs, values_all, preferred_element_type=jnp.float32)
    return (context.astype(jnp.bfloat16), (highest_score + jnp.log(totals))[..., 0])


def attend_backward(record):
    queries, keys_all, values_all, log_totals, grad_context = record
    scores = window_scores(queries, keys_all)
    attn_probs = jnp.exp(scores - log_totals[..., None])
    grad_probs = jnp.einsum(
        "qhd,khd->hqk", grad_context, values_all, preferred_element_type=jnp.float32
    )
    grad_values = jnp.einsum(
        "hqk,qhd->khd",
        attn_probs.astype(jnp.bfloat16),
        grad_context,
        preferred_element_type=jnp.float32,
    )
    row_delta = jnp.sum(grad_probs * attn_probs, axis=-1, keepdims=True)
    grad_scores = (attn_probs * (grad_probs - row_delta)).astype(jnp.bfloat16)
    grad_queries = (
        jnp.einsum("hqk,khd->qhd", grad_scores, keys_all, preferred_element_type=jnp.float32)
        * 0.125
    )
    grad_keys = (
        jnp.einsum("hqk,qhd->khd", grad_scores, queries, preferred_element_type=jnp.float32) * 0.125
    )
    return (
        grad_queries.astype(jnp.bfloat16),
        grad_keys.astype(jnp.bfloat16),
        grad_values.astype(jnp.bfloat16),
    )


def on_device(
    frames,
    cotangent,
    window_live,
    language,
    task,
    ln1_gain,
    ln1_offset,
    query_weight,
    query_bias,
    key_weight,
    value_weight,
    value_bias,
    out_weight,
    out_bias,
    ln2_gain,
    ln2_offset,
    up_weight,
    up_bias,
    down_weight,
    down_bias,
):
    local_rows = frames.shape[0]
    head_index = lax.axis_index("head")
    data_index = lax.axis_index("dp")
    per_window = window_weights(window_live, language, task)
    slot_ids = (
        head_index * local_rows + jnp.arange(local_rows, dtype=jnp.int32)
    ) // FRAMES + data_index * SLOTS
    window_ids = jnp.arange(per_window.shape[0], dtype=jnp.int32)
    frame_match = slot_ids[:, None] == window_ids[None, :]
    frame_weight = jnp.sum(jnp.where(frame_match, per_window[None, :], 0.0), axis=1)
    frame_live = jnp.sum(
        jnp.where(frame_match, window_live.astype(jnp.float32)[None, :], 0.0), axis=1
    )
    inputs = frames.astype(jnp.float32)
    normed, ln1_back = jax.vjp(layer_norm, inputs, ln1_gain, ln1_offset)
    normed_low = normed.astype(jnp.bfloat16)
    query_head, key_head, value_head, out_head = (
        lax.all_gather(query_weight, "dp", axis=0, tiled=True),
        lax.all_gather(key_weight, "dp", axis=0, tiled=True),
        lax.all_gather(value_weight, "dp", axis=0, tiled=True),
        lax.all_gather(out_weight, "dp", axis=1, tiled=True),
    )
    head_width = query_head.shape[1]
    local_heads = head_width // HEAD_DIM
    joint_weight = jnp.concatenate([query_head, key_head, value_head], axis=1)
    joint_bias = jnp.concatenate(
        [
            lax.dynamic_slice_in_dim(query_bias, head_index * head_width, head_width),
            jnp.zeros((head_width,), jnp.float32),
            lax.dynamic_slice_in_dim(value_bias, head_index * head_width, head_width),
        ]
    )
    normed_all = lax.all_gather(normed_low, "head", axis=0, tiled=True)
    projected = (
        jnp.dot(normed_all, joint_weight, preferred_element_type=jnp.float32) + joint_bias
    ).astype(jnp.bfloat16)
    shaped = projected.reshape(-1, FRAMES, 3, local_heads, HEAD_DIM)
    queries = shaped[:, :, 0]
    keys_all = shaped[:, :, 1]
    values_all = shaped[:, :, 2]
    context, log_totals = lax.map(attend_forward, (queries, keys_all, values_all))
    context_flat = context.reshape(-1, head_width)
    branch = lax.psum_scatter(
        jnp.dot(context_flat, out_head, preferred_element_type=jnp.float32),
        "head",
        scatter_dimension=0,
        tiled=True,
    )
    hidden = inputs + branch + out_bias
    normed_two, ln2_back = jax.vjp(layer_norm, hidden, ln2_gain, ln2_offset)
    normed_two_low = normed_two.astype(jnp.bfloat16)
    up_full, down_full = (
        lax.all_gather(up_weight, ("dp", "head"), axis=1, tiled=True),
        lax.all_gather(down_weight, ("dp", "head"), axis=0, tiled=True),
    )
    pre_act = jnp.dot(normed_two_low, up_full, preferred_element_type=jnp.float32) + up_bias
    activated, gelu_back = jax.vjp(gelu_exact, pre_act)
    activated_low = activated.astype(jnp.bfloat16)
    result = (
        hidden + jnp.dot(activated_low, down_full, preferred_element_type=jnp.float32) + down_bias
    )
    output = (result * frame_live[:, None]).astype(jnp.bfloat16)
    grad_result = cotangent.astype(jnp.float32) * frame_weight[:, None]
    grad_two = grad_result.astype(jnp.bfloat16)
    grad_down = contract(activated_low, grad_two)
    grad_down_bias = jnp.sum(grad_two.astype(jnp.float32), axis=0)
    grad_activated = times_t(grad_two, down_full)
    grad_pre = gelu_back(grad_activated)[0].astype(jnp.bfloat16)
    grad_up = contract(normed_two_low, grad_pre)
    grad_up_bias = jnp.sum(grad_pre.astype(jnp.float32), axis=0)
    grad_normed_two = times_t(grad_pre, up_full)
    grad_hidden_ln, grad_ln2_gain, grad_ln2_offset = ln2_back(grad_normed_two)
    grad_hidden = grad_result + grad_hidden_ln
    grad_branch = grad_hidden.astype(jnp.bfloat16)
    grad_out_bias = jnp.sum(grad_branch.astype(jnp.float32), axis=0)
    branch_all = lax.all_gather(grad_branch, "head", axis=0, tiled=True)
    grad_context = times_t(branch_all, out_head).astype(jnp.bfloat16)
    grad_out_head = contract(context_flat, branch_all)
    grad_context_win = grad_context.reshape(-1, FRAMES, local_heads, HEAD_DIM)
    grad_queries, grad_keys, grad_values = lax.map(
        attend_backward, (queries, keys_all, values_all, log_totals, grad_context_win)
    )
    grad_joint = jnp.concatenate(
        [
            grad_queries.reshape(-1, head_width),
            grad_keys.reshape(-1, head_width),
            grad_values.reshape(-1, head_width),
        ],
        axis=1,
    )
    grad_joint_weight = contract(normed_all, grad_joint)
    joint_sums = jnp.sum(grad_joint.astype(jnp.float32), axis=0)
    empty_vec = jnp.zeros((query_bias.shape[0],), jnp.float32)
    grad_query_bias = lax.dynamic_update_slice(
        empty_vec, joint_sums[:head_width], (head_index * head_width,)
    )
    grad_value_bias = lax.dynamic_update_slice(
        empty_vec, joint_sums[2 * head_width :], (head_index * head_width,)
    )
    grad_normed = lax.psum_scatter(
        times_t(grad_joint, joint_weight), "head", scatter_dimension=0, tiled=True
    )
    grad_inputs_ln, grad_ln1_gain, grad_ln1_offset = ln1_back(grad_normed)
    grad_frames = (grad_hidden + grad_inputs_ln).astype(jnp.bfloat16)
    grad_query_w, grad_key_w, grad_value_w, grad_out_w = (
        lax.psum_scatter(grad_joint_weight[:, :head_width], "dp", scatter_dimension=0, tiled=True),
        lax.psum_scatter(
            grad_joint_weight[:, head_width : 2 * head_width], "dp", scatter_dimension=0, tiled=True
        ),
        lax.psum_scatter(
            grad_joint_weight[:, 2 * head_width :], "dp", scatter_dimension=0, tiled=True
        ),
        lax.psum_scatter(grad_out_head, "dp", scatter_dimension=1, tiled=True),
    )
    grad_up_w, grad_down_w = (
        lax.psum_scatter(grad_up, ("dp", "head"), scatter_dimension=1, tiled=True),
        lax.psum_scatter(grad_down, ("dp", "head"), scatter_dimension=0, tiled=True),
    )
    (
        sum_ln1_gain,
        sum_ln1_offset,
        sum_query_bias,
        sum_value_bias,
        sum_out_bias,
        sum_ln2_gain,
        sum_ln2_offset,
        sum_up_bias,
        sum_down_bias,
    ) = lax.psum(
        (
            grad_ln1_gain,
            grad_ln1_offset,
            grad_query_bias,
            grad_value_bias,
            grad_out_bias,
            grad_ln2_gain,
            grad_ln2_offset,
            grad_up_bias,
            grad_down_bias,
        ),
        ("dp", "head"),
    )
    return (
        output,
        grad_frames,
        sum_ln1_gain,
        sum_ln1_offset,
        grad_query_w,
        sum_query_bias,
        grad_key_w,
        grad_value_w,
        sum_value_bias,
        grad_out_w,
        sum_out_bias,
        sum_ln2_gain,
        sum_ln2_offset,
        grad_up_w,
        sum_up_bias,
        grad_down_w,
        sum_down_bias,
    )


LANES = 128
PADDED = 1536
LOG2E = 1.4426950408889634
MASKED = -30000.0
F32 = jnp.float32
BF16 = jnp.bfloat16
LN1_GAIN, LN1_OFFSET, OUT_BIAS, LN2_GAIN, LN2_OFFSET, DOWN_BIAS = range(6)
WEIGHT, LIVE, QUERY_BIAS, VALUE_BIAS, UP_BIAS = 6, 7, 8, 10, 11
BIT_X, BIT_CORE, BIT_Y, BIT_Z = 1, 2, 4, 8
LAYERS = 4


def dot_on(first_mat, second_mat, first_dim, second_dim):
    return lax.dot_general(
        first_mat,
        second_mat,
        (((first_dim,), (second_dim,)), ((), ())),
        preferred_element_type=F32,
    )


def params(microseconds, mebibytes):
    return dict(
        compiler_params=pltpu.CompilerParams(vmem_limit_bytes=mebibytes << 20),
        cost_estimate=pl.CostEstimate(
            flops=int(microseconds * 1e9), bytes_accessed=1 << 20, transcendentals=0
        ),
    )


def whole(shape):
    return pl.BlockSpec(shape, lambda *_: (0,) * len(shape), pipeline_mode=pl.Buffered(1))


def struct(shape, dtype):
    return jax.ShapeDtypeStruct(shape, dtype)


def place():
    dp = lax.axis_index("dp")
    return dp, lax.axis_index("head")


def pack_kernel(
    live_ref,
    language_ref,
    task_ref,
    query_ref,
    key_ref,
    value_ref,
    out_ref,
    up_ref,
    down_ref,
    upb_ref,
    qb_ref,
    vb_ref,
    *refs,
):
    vectors, (pieces_ref, big_ref, table_ref) = refs[:6], refs[6:]
    rows, half = query_ref.shape
    ff = down_ref.shape[0]
    dp, side = place()
    for j, ref in enumerate((query_ref, key_ref, value_ref)):
        pieces_ref[0, j * rows : (j + 1) * rows, :] = ref[...]
    up = up_ref[...]
    big_ref[0:ff, :] = down_ref[:, 0:half]
    big_ref[ff : 2 * ff, :] = down_ref[:, half:]
    big_ref[2 * ff : 3 * ff, :] = up[:, 0:half]
    big_ref[3 * ff : 4 * ff, :] = up[:, half:]
    big_ref[4 * ff :, :] = out_ref[...]
    for j, ref in enumerate(vectors):
        table_ref[j : j + 1, :] = ref[...]
    for j, ref in ((QUERY_BIAS, qb_ref), (VALUE_BIAS, vb_ref)):
        first, second = ref[:, 0:half], ref[:, half:]
        table_ref[j : j + 1, 0:half] = jnp.where(side == 0, second, first)
        table_ref[j : j + 1, half:] = jnp.where(side == 0, first, second)
    table_ref[QUERY_BIAS + 1 : QUERY_BIAS + 2, :] = jnp.zeros((1, 2 * half), F32)
    for j in range(4):
        table_ref[UP_BIAS + j : UP_BIAS + j + 1, :] = upb_ref[:, j * 2 * half : (j + 1) * 2 * half]
    slots = live_ref.shape[0]
    lane = lax.broadcasted_iota(jnp.int32, (1, LANES), 1)
    groups = jnp.full((1, LANES), -1, jnp.int32)
    live = jnp.zeros((1, LANES), F32)
    for t in range(slots):
        groups = jnp.where(lane == t, language_ref[t] * TASKS + task_ref[t], groups)
        live = jnp.where(lane == t, live_ref[t].astype(F32), live)
    counts = jnp.zeros((1, LANES), F32)
    for t in range(slots):
        group = language_ref[t] * TASKS + task_ref[t]
        counts = counts + jnp.where(groups == group, live_ref[t].astype(F32), 0.0)
    counts = jnp.maximum(counts, 1.0)
    shares = jnp.broadcast_to(live / counts, (8, LANES))
    present = jnp.floor(jnp.sum(shares, axis=1, keepdims=True)[0:1] + 0.5)
    total = jnp.sum(jnp.broadcast_to(live, (8, LANES)), axis=1, keepdims=True)[0:1]
    weights = live * total / (present * counts)
    mine = lane == dp * SLOTS + side
    for j, values in ((WEIGHT, weights), (LIVE, live)):
        picked = jnp.broadcast_to(jnp.where(mine, values, 0.0), (8, LANES))
        picked = jnp.sum(picked, axis=1, keepdims=True)[0:1]
        table_ref[j : j + 1, :] = jnp.broadcast_to(picked, (1, 2 * half))


def pack(live, language, task, query, key, value, out, up, down, up_bias, qb, vb, vectors):
    rows, half = query.shape
    ff, width = down.shape
    scalars = pl.BlockSpec(memory_space=pltpu.SMEM)
    row = lambda values: values.reshape(1, -1)
    rest = [query, key, value, out.T, up.T, down, row(up_bias), row(qb), row(vb)] + [
        row(v) for v in vectors
    ]
    return pl.pallas_call(
        pack_kernel,
        in_specs=[scalars] * 3 + [pl.BlockSpec(memory_space=pltpu.VMEM)] * len(rest),
        out_shape=[
            struct((1, 3 * rows, half), BF16),
            struct((4 * ff + rows, half), BF16),
            struct((16, width), F32),
        ],
        name="pack",
        **params(3, 58),
    )(live, language, task, *rest)


def real_rows(x_ref, first=0):
    tile = pl.program_id(0) + first
    return tile * x_ref.shape[0] + lax.broadcasted_iota(jnp.int32, x_ref.shape, 0) < FRAMES


def unit_rows(values):
    centred = values - jnp.mean(values, axis=1, keepdims=True)
    scale = lax.rsqrt(jnp.mean(centred * centred, axis=1, keepdims=True) + 1e-05)
    return centred * scale, scale


def unit_back(lifted, unit, scale):
    mean_one = jnp.mean(lifted, axis=1, keepdims=True)
    mean_two = jnp.mean(lifted * unit, axis=1, keepdims=True)
    return scale * (lifted - mean_one - unit * mean_two)


def norm_kernel(x_ref, table_ref, n_ref, nt_ref):
    unit, _ = unit_rows(jnp.where(real_rows(x_ref), x_ref[...].astype(F32), 0.0))
    normed = unit * table_ref[LN1_GAIN : LN1_GAIN + 1, :] + table_ref[LN1_OFFSET : LN1_OFFSET + 1, :]
    n_ref[...] = normed.astype(BF16)
    nt_ref[...] = normed.T.astype(BF16)


def first_norm(frames, table):
    width = frames.shape[1]
    tile = 256
    return pl.pallas_call(
        norm_kernel,
        grid=(PADDED // tile,),
        in_specs=[pl.BlockSpec((tile, width), lambda i: (i, 0)), whole(table.shape)],
        out_specs=[
            pl.BlockSpec((tile, width), lambda i: (i, 0)),
            pl.BlockSpec((width, tile), lambda i: (0, i)),
        ],
        out_shape=[struct((PADDED, width), BF16), struct((width, PADDED), BF16)],
        name="first_norm",
        **params(4, 14),
    )(frames, table)


def lane_masks(shape, h):
    lane = lax.broadcasted_iota(jnp.int32, shape, 1)
    return lane >= HEAD_DIM if h else lane < HEAD_DIM


def masked(values, h):
    own = lane_masks(values.shape, h)
    return jnp.where(own, values, 0.0)


def forward_kernel(side_at, n_ref, near_ref, far_ref, table_ref, *refs):
    (
        q_ref, k_ref, v_ref, p_ref, c_ref, rest_ref, inv_ref, w_ref,
        keys_ref, vt_ref, both_ref, small_ref,
    ) = refs[-12:]
    pair, step = pl.program_id(0), pl.program_id(1)
    count, rows3, half = near_ref.shape
    rows = rows3 // 3

    @pl.when((pair == 0) & (step == 0))
    def _():
        dp, _ = place()
        for core, ref in enumerate((near_ref, far_ref)):
            for t in range(count):
                owner = dp ^ ((t & 1) * 8 + (t & 2) * 2 + (t & 4) // 2 + core)
                at = pl.ds(pl.multiple_of(owner * rows, rows), rows)
                for j in range(3):
                    w_ref[j, at, :] = ref[t, j * rows : (j + 1) * rows, :]

    @pl.when(step == 0)
    def _():
        columns = pl.ds(pl.multiple_of(pair * LANES, LANES), LANES)
        places = pl.ds(pl.multiple_of(pair * LANES + side_at * half, LANES), LANES)
        for j, out in enumerate((q_ref, k_ref, v_ref)):
            bias = table_ref[QUERY_BIAS + j : QUERY_BIAS + j + 1, places]
            out[...] = (dot_on(n_ref[...], w_ref[j, :, columns], 1, 0) + bias).astype(BF16)
        keys = k_ref[...].astype(F32) * (LOG2E * 0.125)
        queries = q_ref[...].astype(F32)
        high = keys.astype(BF16).astype(F32)
        flipped = v_ref[...].astype(F32).T
        spare = vt_ref.shape[1] - HEAD_DIM
        shape = (vt_ref.shape[1], flipped.shape[1])
        real = lax.broadcasted_iota(jnp.int32, shape, 1) < FRAMES
        first = lax.broadcasted_iota(jnp.int32, shape, 0) == HEAD_DIM
        shape = (LANES, LANES)
        one, two = (lax.broadcasted_iota(jnp.int32, shape, j) < HEAD_DIM for j in (0, 1))
        same = jnp.where(one == two, 1.0, 0.0).astype(BF16)
        norms = [
            jnp.max(dot_on((m * m).astype(BF16), same, 1, 0), axis=0, keepdims=True)
            for m in (queries, keys)
        ]
        bound = jnp.max(norms[0] * norms[1])
        small_ref[0] = (bound < 90.0 * 90.0).astype(jnp.int32)
        for h in (0, 1):
            keys_ref[h, :, 0:LANES] = masked(high, h).astype(BF16)
            keys_ref[h, :, LANES:] = masked(keys - high, h).astype(BF16)
            mine = flipped[HEAD_DIM * h : HEAD_DIM * (h + 1), :]
            mine = jnp.concatenate([mine, mine[0:spare]], axis=0)
            vt_ref[h] = jnp.where(real, jnp.where(first, 1.0, mine), 0.0).astype(BF16)

    tile = c_ref.shape[0]
    tail = FRAMES // 16 * 16

    def attend(h, start, size, at, shift):
        queries = q_ref[pl.ds(start, size), :]
        scores = dot_on(keys_ref[h], jnp.concatenate([queries, queries], axis=1), 1, 1)
        if shift:
            real = lax.broadcasted_iota(jnp.int32, scores.shape, 0) < FRAMES
            scores = jnp.where(real, scores, -1e30)
            scores = scores - jnp.max(scores, axis=0, keepdims=True)
        probs = jnp.exp2(scores)
        low = probs.astype(BF16)
        p_ref[h, 0:tail, at] = low[0:tail]
        last = probs[tail:]
        real = lax.broadcasted_iota(jnp.int32, last.shape, 0) < FRAMES - tail
        p_ref[h, tail:, at] = jnp.where(real, last, 0.0).astype(BF16)
        summed = dot_on(vt_ref[h], low, 1, 0)
        inverse = 1.0 / summed[HEAD_DIM : HEAD_DIM + 1, :]
        both_ref[0, h, :, at] = summed[0:HEAD_DIM, :] * inverse
        both_ref[1, h, :, at] = jnp.broadcast_to(inverse, (HEAD_DIM, inverse.shape[1]))

    @pl.when(small_ref[0] == 1)
    def _():
        for h in (0, 1):
            attend(h, step * tile, tile, slice(0, tile), False)

    @pl.when(small_ref[0] == 0)
    def _():
        size = LANES

        @pl.loop(0, 2 * tile // size)
        def _(t):
            h, t = t & 1, t >> 1
            at = pl.ds(pl.multiple_of(t * size, size), size)
            attend(h, pl.multiple_of(step * tile + t * size, size), size, at, True)

    context = both_ref[0].reshape(LANES, tile).T
    low = context.astype(BF16)
    c_ref[...] = low
    rest_ref[...] = (context - low.astype(F32)).astype(BF16)
    inv_ref[...] = both_ref[1].reshape(LANES, tile).T


def attend_forward_fast(side_at, normed, near, far, table, before=()):
    rows, width = normed.shape
    half = near.shape[2]
    pairs = half // LANES
    tile = 768
    at = side_at * pairs
    block = pl.BlockSpec((tile, LANES), lambda p, i: (i, p + at))
    full = pl.BlockSpec((rows, LANES), lambda p, i: (0, p + at))
    weights = pl.BlockSpec((3, width, half), lambda p, i: (0, 0, side_at))
    return pl.pallas_call(
        functools.partial(forward_kernel, side_at),
        grid=(pairs, rows // tile),
        in_specs=[whole(normed.shape), whole(near.shape), whole(far.shape), whole(table.shape)]
        + [pl.BlockSpec(memory_space=pl.ANY)] * len(before),
        out_specs=[
            full, full, full,
            pl.BlockSpec((2, rows, tile), lambda p, i: (p + at, 0, i)),
            block, block, block, weights,
        ],
        out_shape=[struct((rows, width), BF16)] * 3
        + [
            struct((width // HEAD_DIM, rows, rows), BF16),
            pltpu.HBM((rows, width), BF16),
            pltpu.HBM((rows, width), BF16),
            struct((rows, width), F32),
            pltpu.HBM((3, width, width), BF16),
        ],
        scratch_shapes=[
            pltpu.VMEM((2, rows, 2 * LANES), BF16),
            pltpu.VMEM((2, HEAD_DIM + 16, rows), BF16),
            pltpu.VMEM((2, 2, HEAD_DIM, tile), F32),
            pltpu.SMEM((1,), jnp.int32),
        ],
        input_output_aliases={4 + j: j for j in range(len(before))},
        name="attend_forward",
        **params(15, 40),
    )(normed, near, far, table, *before)


def backward_kernel(
    first, q_ref, k_ref, v_ref, p_ref, inv_ref, c_ref, rest_ref, g_ref, nt_ref, w_ref,
    vec_in_ref, *refs
):
    dq_ref, dk_ref, dv_ref, dw_ref, vec_ref, vals_ref, kt_ref, acck, accv, acc_one, acc_two = refs[-11:]
    pair, step = pl.program_id(0), pl.program_id(1)
    last = step == pl.num_programs(1) - 1

    @pl.when(step == 0)
    def _():
        values = v_ref[...].astype(F32)
        for h in (0, 1):
            vals_ref[h] = masked(values, h).astype(BF16)
        kt_ref[...] = k_ref[...].astype(F32).T.astype(BF16)
        acck[...] = jnp.zeros_like(acck)
        accv[...] = jnp.zeros_like(accv)

    tile = q_ref.shape[0]
    plain = q_ref[...].astype(F32)
    divided = g_ref[...].astype(F32) * inv_ref[...]
    low = divided.astype(BF16)
    divided = low.astype(F32)
    products = (divided * (c_ref[...].astype(F32) + rest_ref[...].astype(F32))).T
    diffs, queries, flipped = [], [], []
    for h in (0, 1):
        rows = slice(HEAD_DIM * h, HEAD_DIM * (h + 1))
        row_delta = jnp.sum(products[rows], axis=0, keepdims=True)
        accv[...] += dot_on(p_ref[h], masked(divided, h).astype(BF16), 1, 0)
        grad_probs = dot_on(vals_ref[h], low, 1, 1)
        diff = p_ref[h] * (grad_probs - row_delta).astype(BF16)
        diffs.append(diff)
        queries.append(masked(plain, h).astype(BF16))
        flipped.append(dot_on(kt_ref[rows, :], diff, 1, 0))
    acck[...] += dot_on(diffs[0], queries[0], 1, 0) + dot_on(diffs[1], queries[1], 1, 0)
    at = pl.ds(pl.multiple_of(step * tile, tile), tile)
    dq_ref[at, :] = (jnp.concatenate(flipped, axis=0) * 0.125).T.astype(BF16)

    @pl.when(last & (pair == 0))
    def _():
        acc_one[...] = jnp.zeros_like(acc_one)
        acc_two[...] = jnp.zeros_like(acc_two)
        vec_ref[...] = vec_in_ref[...]

    @pl.when(last)
    def _():
        dk_ref[...] = (acck[...] * 0.125).astype(BF16)
        dv_ref[...] = accv[...].astype(BF16)
        columns = pl.ds(pl.multiple_of((pair + first) * LANES, LANES), LANES)
        both = jnp.concatenate([dq_ref[...], dk_ref[...]], axis=1)
        both = dot_on(nt_ref[...], both, 1, 0)
        products = [both[:, 0:LANES], both[:, LANES:], dot_on(nt_ref[...], dv_ref[...], 1, 0)]
        for j, ref in enumerate((dq_ref, dk_ref, dv_ref)):
            dw = products[j]
            dw_ref[j] = dw.astype(dw_ref.dtype)
            column_sums = jnp.sum(ref[...].astype(F32), axis=0, keepdims=True)
            weights = w_ref[j].astype(F32)
            acc_one[...] += weights * dw
            acc_two[...] += weights * column_sums
            if j != 1:
                vec_ref[2 + j // 2 : 3 + j // 2, columns] = column_sums

    @pl.when(last & (pair == pl.num_programs(0) - 1))
    def _():
        for j, ref in enumerate((acc_one, acc_two)):
            vec_ref[j : j + 1, :] += jnp.sum(ref[...].T, axis=0, keepdims=True)


def attend_backward_fast(
    first, pairs, q, k, v, probs, inverse, context, rest, grads, normed_t, weights, vec, before=()
):
    rows, width = q.shape
    half = width // 2
    context, rest, grads, weights = (
        pltpu.with_memory_space_constraint(x, pltpu.HBM) for x in (context, rest, grads, weights)
    )
    tile = 384 if pairs > 1 else 256
    block = pl.BlockSpec((tile, LANES), lambda p, i: (i, p + first))
    full = pl.BlockSpec((rows, LANES), lambda p, i: (0, p + first))
    gradient = pl.BlockSpec(
        (None, 3, width, LANES), lambda p, i: ((p + first) // 2, 0, 0, (p + first) % 2)
    )
    in_specs = [
        block, full, full,
        pl.BlockSpec((2, rows, tile), lambda p, i: (p + first, 0, i)),
        block, block, block, block, whole(normed_t.shape),
        pl.BlockSpec((3, width, LANES), lambda p, i: (0, 0, p + first)),
        whole(vec.shape),
    ]
    count = len(in_specs)
    return pl.pallas_call(
        functools.partial(backward_kernel, first),
        grid=(pairs, rows // tile),
        in_specs=in_specs + [pl.BlockSpec(memory_space=pl.ANY)] * len(before),
        out_specs=[full, full, full, gradient, whole(vec.shape)],
        out_shape=[struct((rows, width), BF16)] * 3
        + [struct((2, 3, width, half), BF16), struct(vec.shape, F32)],
        scratch_shapes=[
            pltpu.VMEM((2, rows, LANES), BF16),
            pltpu.VMEM((LANES, rows), BF16),
            pltpu.VMEM((rows, LANES), F32),
            pltpu.VMEM((rows, LANES), F32),
            pltpu.VMEM((width, LANES), F32),
            pltpu.VMEM((width, LANES), F32),
        ],
        input_output_aliases={count + j: j for j in range(len(before))},
        name="attend_backward",
        **params(14 * pairs, 34),
    )(q, k, v, probs, inverse, context, rest, grads, normed_t, weights, vec, *before)


def middle_kernel(masks, c_ref, x_ref, cot_ref, table_ref, *refs):
    pieces, refs = refs[: len(masks)], refs[len(masks) :]
    out_ref, g_ref, gh_ref, send_ref, keep_ref, vec_ref = refs[:6]
    up_t, up_n, down_n, down_t, out_t, upb_t, acc_up, acc_down, acc_out, acc_upb, acc_vec = refs[6:]
    step = pl.program_id(0)
    dp, side = place()
    core = lax.rem(dp, 2)
    layers, piece_rows, half = pieces[0].shape
    devices = layers * len(masks)
    width = 2 * half
    ow = width // (devices // 2)
    ff = (piece_rows - ow) // 4
    hidden_all = devices * ff
    chunk = 1024
    chunks = hidden_all // chunk

    @pl.when(step == 0)
    def _():
        for mask, ref in zip(masks, pieces):

            @pl.loop(0, layers)
            def _(t, mask=mask, ref=ref):
                owner = (dp * 2 + side) ^ (mask + (t & 1) * 2 * BIT_Z + (t >> 1) * BIT_Z)
                rows = pl.ds(pl.multiple_of(owner * ff, ff), ff)
                down_n[rows, 0:half] = ref[t, 0:ff, :]
                down_n[rows, half:] = ref[t, ff : 2 * ff, :]
                up_t[rows, 0:half] = ref[t, 2 * ff : 3 * ff, :]
                up_t[rows, half:] = ref[t, 3 * ff : 4 * ff, :]
                rows = pl.ds(pl.multiple_of((owner >> 1) * ow, ow), ow)
                at = slice(0, half) if mask & BIT_X else slice(half, width)
                out_t[rows, at] = ref[t, 4 * ff :, :]

        @pl.loop(0, hidden_all // width)
        def _(j):
            rows = pl.ds(pl.multiple_of(j * width, width), width)
            up_n[:, rows] = up_t[rows, :].T
            down_t[:, rows] = down_n[rows, :].T
            bias = table_ref[pl.ds(UP_BIAS + j, 1), :]
            upb_t[rows, :] = jnp.broadcast_to(bias, (LANES, width)).T
            acc_upb[rows, :] = jnp.zeros((width, LANES), F32)

        @pl.loop(0, acc_out.shape[0])
        def _(j):
            acc_out[j] = jnp.zeros(acc_out.shape[1:], F32)

        acc_vec[...] = jnp.zeros_like(acc_vec)

    def add_to(ref, at, values):
        ref[at] = jnp.where(step == 0, 0.0, ref[at]) + values

    def row_of(j):
        return table_ref[j : j + 1, :]

    tile = x_ref.shape[0]
    real = real_rows(x_ref)
    branch = dot_on(c_ref[...], out_t[...], 1, 1)
    hidden = jnp.where(real, x_ref[...].astype(F32), 0.0) + branch + row_of(OUT_BIAS)
    unit, scale = unit_rows(hidden)
    normed = (unit * row_of(LN2_GAIN) + row_of(LN2_OFFSET)).astype(BF16)
    grad_result = jnp.where(real, cot_ref[...].astype(F32), 0.0) * row_of(WEIGHT)
    grad_two = grad_result.astype(BF16)
    result_t = jnp.zeros((width, tile), F32)
    grad_normed_t = jnp.zeros((width, tile), F32)
    for j in range(chunks):
        rows = slice(j * chunk, (j + 1) * chunk)
        slots = slice(j * chunk // ff, (j + 1) * chunk // ff)
        pre = dot_on(up_t[rows, :], normed, 1, 1) + upb_t[rows, 0:1]
        bell = 0.5 + 0.5 * lax.erf(pre * 0.7071067811865476)
        slope = bell + pre * (jnp.exp2(pre * pre * (-0.5 * LOG2E)) * 0.3989422804014327)
        activated = (pre * bell).astype(BF16)
        result_t += dot_on(down_t[:, rows], activated, 1, 0)
        add_to(acc_down, slots, dot_on(activated, grad_two, 1, 0).reshape(-1, ff, width))
        grad_pre = (dot_on(down_n[rows, :], grad_two, 1, 1) * slope).astype(BF16)
        rounded = grad_pre.astype(F32)
        partial = rounded[:, 0:LANES]
        for lanes in range(LANES, tile, LANES):
            partial += rounded[:, lanes : lanes + LANES]
        acc_upb[rows, :] += partial
        add_to(acc_up, slots, dot_on(grad_pre, normed, 1, 0).reshape(-1, ff, width))
        grad_normed_t += dot_on(up_n[:, rows], grad_pre, 1, 0)
    result = hidden + result_t.T + row_of(DOWN_BIAS)
    out_ref[...] = (result * row_of(LIVE)).astype(BF16)
    grad_normed = grad_normed_t.T
    grad_hidden = grad_result + unit_back(grad_normed * row_of(LN2_GAIN), unit, scale)
    gh_ref[...] = grad_hidden
    grad_branch = grad_hidden.astype(BF16)
    g_ref[...] = dot_on(grad_branch, out_t[...], 1, 0).astype(BF16)
    acc_out[...] += dot_on(grad_hidden.T.astype(BF16), c_ref[...], 1, 0).reshape(-1, ow, width)
    for j, term in enumerate(
        (grad_branch.astype(F32), grad_normed * unit, grad_normed, grad_two.astype(F32))
    ):
        acc_vec[8 * j : 8 * j + 8, :] += jnp.sum(term.reshape(-1, 8, width), axis=0)

    @pl.when(step == pl.num_programs(0) - 1)
    def _():
        targets = devices // 2
        for ref, bit in ((keep_ref, core), (send_ref, 1 - core)):

            @pl.loop(0, targets)
            def _(t, ref=ref, bit=bit):
                y, x, z = t >> 3, (t >> 2) & 1, t & 3
                chip = z * 2 + y
                slot = chip * 4 + bit * 2 + x
                near = pl.ds(pl.multiple_of((1 - (side ^ x)) * half, half), half)

                def rows(j, count=ff):
                    return pl.ds(pl.multiple_of(t * piece_rows + j * ff, 32), count)

                ref[rows(0), :] = acc_down[slot, :, 0:half].astype(BF16)
                ref[rows(1), :] = acc_down[slot, :, half:].astype(BF16)
                ref[rows(2), :] = acc_up[slot, :, 0:half].astype(BF16)
                ref[rows(3), :] = acc_up[slot, :, half:].astype(BF16)
                ref[rows(4, ow), :] = acc_out[chip * 2 + bit, :, near].astype(BF16)

        for j in range(4):
            total = jnp.sum(acc_vec[8 * j : 8 * j + 8, :], axis=0, keepdims=True)
            vec_ref[2 * j : 2 * j + 1, :] = total[:, 0:half]
            vec_ref[2 * j + 1 : 2 * j + 2, :] = total[:, half:]
        for j in range(chunks):
            total = jnp.sum(acc_upb[j * chunk : (j + 1) * chunk, :].T, axis=0, keepdims=True)
            for i in range(chunk // half):
                at = 8 + j * (chunk // half) + i
                vec_ref[at : at + 1, :] = total[:, i * half : (i + 1) * half]
        store_two(send_ref, targets * piece_rows, vec_ref[...])


def middle(context, frames, cotangent, table, masks, pieces):
    context, frames, cotangent = (
        pltpu.with_memory_space_constraint(x, pltpu.HBM) for x in (context, frames, cotangent)
    )
    rows, width = context.shape
    layers, piece_rows, half = pieces[0].shape
    devices = layers * len(masks)
    tile = 512
    ow = width // (devices // 2)
    ff = (piece_rows - ow) // 4
    hidden_all = devices * ff
    body = devices // 2 * piece_rows
    wide = pl.BlockSpec((tile, width), lambda i: (i, 0))
    return pl.pallas_call(
        functools.partial(middle_kernel, masks),
        grid=(rows // tile,),
        in_specs=[wide, wide, wide, whole(table.shape)] + [whole(p.shape) for p in pieces],
        out_specs=[wide, wide, wide, whole((body + 32, half)), whole((body, half)), whole((16, half))],
        out_shape=[
            struct(frames.shape, BF16),
            pltpu.HBM((rows, width), BF16),
            pltpu.HBM((rows, width), F32),
            struct((body + 32, half), BF16),
            struct((body, half), BF16),
            struct((16, half), F32),
        ],
        scratch_shapes=[
            pltpu.VMEM((hidden_all, width), BF16),
            pltpu.VMEM((width, hidden_all), BF16),
            pltpu.VMEM((hidden_all, width), BF16),
            pltpu.VMEM((width, hidden_all), BF16),
            pltpu.VMEM((width, width), BF16),
            pltpu.VMEM((hidden_all, LANES), F32),
            pltpu.VMEM((devices, ff, width), F32),
            pltpu.VMEM((devices, ff, width), F32),
            pltpu.VMEM((width // ow, ow, width), F32),
            pltpu.VMEM((hidden_all, LANES), F32),
            pltpu.VMEM((32, width), F32),
        ],
        name="middle",
        **params(38, 40),
    )(context, frames, cotangent, table, *pieces)


def store_two(ref, at, values):
    count = values.shape[0]
    high = values.astype(BF16)
    ref[at : at + count, :] = high
    ref[at + count : at + 2 * count, :] = (values - high.astype(F32)).astype(BF16)


def load_two(ref, at, count):
    return ref[at : at + count, :].astype(F32) + ref[at + count : at + 2 * count, :].astype(F32)


def spread_kernel(count, masks, keep_ref, vec_ref, *refs):
    came, (mine_ref, sum_ref, *sends) = refs[:count], refs[count:]
    size, half = mine_ref.shape
    dp, side = place()
    parts = keep_ref.shape[0] // size
    vec_rows = vec_ref.shape[0]
    vec = vec_ref[...]
    for ref in came:
        vec += load_two(ref, ref.shape[0] - 2 * vec_rows, vec_rows)
    sum_ref[...] = vec

    own = masks[0](dp, side)
    block = 96

    def total(part, at):
        rows = pl.ds(pl.multiple_of(part * size + at, 32), block)
        values = keep_ref[rows, :].astype(F32)
        for ref in came:
            if ref.shape[0] > 2 * vec_rows:
                values += ref[rows, :].astype(F32)
        return values

    @pl.loop(0, size // block)
    def _(t):
        at = pl.multiple_of(t * block, 32)
        mine_ref[pl.ds(at, block), :] = total(own, at)
        for mask, ref in zip(masks[1:], sends):
            if mask is not None:
                ref[pl.ds(at, block), :] = total(own ^ mask, at).astype(BF16)

    for ref in sends:
        store_two(ref, ref.shape[0] - 2 * vec_rows, vec)


def spread(keep, vec, came, own_part, masks, parts):
    rows, half = keep.shape
    size = rows // parts
    tail = 2 * vec.shape[0]
    vmem = pl.BlockSpec(memory_space=pltpu.VMEM)
    return pl.pallas_call(
        functools.partial(spread_kernel, len(came), (own_part, *masks)),
        in_specs=[vmem] * (2 + len(came)),
        out_specs=[vmem] * (2 + len(masks)),
        out_shape=[struct((size, half), F32), struct(vec.shape, F32)]
        + [struct(((0 if m is None else size) + tail, half), BF16) for m in masks],
        name="spread",
        **params(3, 14),
    )(keep, vec, *came)


def swap(values, mask):
    devices = lax.axis_size("dp") * lax.axis_size("head")
    return lax.ppermute(values, ("dp", "head"), [(i, i ^ mask) for i in range(devices)])


def part_xy(dp, side):
    return ((dp >> 1) & 1) * 2 + side


def part_yz(dp, side):
    return ((dp >> 1) & 1) * 2 + ((dp >> 2) & 1)


def part_z(dp, side):
    return dp >> 2


def part_high(dp, side):
    return dp >> 3


def gather_kernel(table_ref, dw_ref, got_ref, vec_in_ref, send_ref, keep_ref, vec_ref):
    dp, side = place()
    core = lax.rem(dp, 2)
    width = table_ref.shape[1]
    half = width // 2
    ow = width // 16
    for ref, bit in ((keep_ref, core), (send_ref, 1 - core)):

        @pl.loop(0, 2 * LAYERS)
        def _(t, ref=ref, bit=bit):
            z = (t & 1) * 2 + ((t >> 1) & 1)
            chip = z * 2 + (t >> 2)
            rows = pl.ds(pl.multiple_of((chip * 2 + bit) * ow, ow), ow)
            for j in range(3):
                at = pl.ds(pl.multiple_of(t * 3 * ow + j * ow, ow), ow)
                both = dw_ref[j, rows, :].astype(F32) + got_ref[j, rows, :].astype(F32)
                ref[at, :] = both.astype(ref.dtype)

    one, two = vec_in_ref[0:1, :], vec_in_ref[1:2, :]
    gain = table_ref[LN1_GAIN : LN1_GAIN + 1, :]
    offset = table_ref[LN1_OFFSET : LN1_OFFSET + 1, :]
    grad_gain = (one - offset * two) / gain
    for j, values in ((0, grad_gain), (2, two)):
        vec_ref[j : j + 1, :] = values[:, 0:half]
        vec_ref[j + 1 : j + 2, :] = values[:, half:]
    for j in (0, 1):
        other, own = vec_in_ref[2 + j : 3 + j, 0:half], vec_in_ref[2 + j : 3 + j, half:]
        vec_ref[4 + 2 * j : 5 + 2 * j, :] = jnp.where(side == 0, own, other)
        vec_ref[5 + 2 * j : 6 + 2 * j, :] = jnp.where(side == 0, other, own)
    store_two(send_ref, 24 * ow, vec_ref[...])


def gather_grads(table, dw, got, vec):
    width = table.shape[1]
    half = width // 2
    rows = 24 * (width // 16)
    shapes = [((rows + 16, half), BF16), ((rows, half), F32), ((8, half), F32)]
    return pl.pallas_call(
        gather_kernel,
        grid=(1,),
        in_specs=[
            whole(table.shape),
            pl.BlockSpec((None, 3, width, half), lambda i: (1, 0, 0, 0)),
            whole(got.shape),
            whole(vec.shape),
        ],
        out_specs=[whole(shape) for shape, _ in shapes],
        out_shape=[struct(*shape) for shape in shapes],
        name="gather_grads",
        **params(2, 12),
    )(table, dw, got, vec)


def finish_kernel(ff, ow, mine_ref, vec_ref, mine_w_ref, vec_w_ref, *refs):
    came, came_w, outs = refs[: LAYERS - 1], refs[LAYERS - 1 : LAYERS + 2], refs[LAYERS + 2 :]
    down_ref, up_ref, out_ref, *outs = outs

    def total(mine, vec, parts):
        size = mine.shape[0]
        values, sums = mine[...], vec[...]
        for ref in parts:
            if ref.shape[0] > size:
                values += ref[0:size, :].astype(F32)
            sums += load_two(ref, ref.shape[0] - 2 * vec.shape[0], vec.shape[0])
        return values, sums

    half = mine_ref.shape[1]
    values, vec = total(mine_ref, vec_ref, came)
    down_ref[:, 0:half] = values[0:ff]
    down_ref[:, half:] = values[ff : 2 * ff]
    up_ref[:, 0:half] = values[2 * ff : 3 * ff]
    up_ref[:, half:] = values[3 * ff : 4 * ff]
    out_ref[...] = values[4 * ff :]
    values, vec_w = total(mine_w_ref, vec_w_ref, came_w)
    for j in range(3):
        outs[j][...] = values[j * ow : (j + 1) * ow]
    at = 0
    rows = [vec[j : j + 1] for j in range(vec.shape[0])] + [
        vec_w[j : j + 1] for j in range(vec_w.shape[0])
    ]
    for ref in outs[3:]:
        for j in range(ref.shape[1] // half):
            ref[:, j * half : (j + 1) * half] = rows[at]
            at += 1


def finish(mine, vec, mine_w, vec_w, came, came_w, ff, ow):
    half = mine.shape[1]
    vmem = pl.BlockSpec(memory_space=pltpu.VMEM)
    shapes = [(ff, 2 * half), (ff, 2 * half), (ow, half)] + [(ow, half)] * 3
    shapes += [(1, 2 * half)] * 4 + [(1, 8 * half)] + [(1, 2 * half)] * 4
    return pl.pallas_call(
        functools.partial(finish_kernel, ff, ow),
        in_specs=[vmem] * (4 + len(came) + len(came_w)),
        out_specs=[vmem] * len(shapes),
        out_shape=[struct(shape, F32) for shape in shapes],
        name="finish",
        **params(3, 12),
    )(mine, vec, mine_w, vec_w, *came, *came_w)


def input_grad_kernel(first, x_ref, gh_ref, table_ref, w_ref, dq_ref, dk_ref, dv_ref, *refs):
    gf_ref = refs[-1]
    total = dot_on(dq_ref[...], w_ref[0], 1, 1)
    total += dot_on(dk_ref[...], w_ref[1], 1, 1)
    total += dot_on(dv_ref[...], w_ref[2], 1, 1)
    unit, scale = unit_rows(jnp.where(real_rows(x_ref, first), x_ref[...].astype(F32), 0.0))
    lifted = total * table_ref[LN1_GAIN : LN1_GAIN + 1, :]
    gf_ref[...] = (gh_ref[...] + unit_back(lifted, unit, scale)).astype(BF16)


def input_grads(first, tiles, frames, grad_hidden, table, weights, grads, before=()):
    rows, width = grad_hidden.shape
    tile = 256
    wide = pl.BlockSpec((tile, width), lambda i: (i + first, 0))
    return pl.pallas_call(
        functools.partial(input_grad_kernel, first),
        grid=(tiles,),
        in_specs=[wide, wide, whole(table.shape), whole(weights.shape), wide, wide, wide]
        + [pl.BlockSpec(memory_space=pl.ANY)] * len(before),
        out_specs=wide,
        out_shape=struct(frames.shape, BF16),
        input_output_aliases={7 + j: j for j in range(len(before))},
        name="input_grads",
        **params(tiles, 20),
    )(frames, grad_hidden, table, weights, *grads, *before)


def on_whole_windows(
    frames,
    cotangent,
    window_live,
    language,
    task,
    ln1_gain,
    ln1_offset,
    query_weight,
    query_bias,
    key_weight,
    value_weight,
    value_bias,
    out_weight,
    out_bias,
    ln2_gain,
    ln2_offset,
    up_weight,
    up_bias,
    down_weight,
    down_bias,
):
    ow, ff = query_weight.shape[0], up_weight.shape[1]
    pieces, big, table = pack(
        window_live,
        language,
        task,
        query_weight,
        key_weight,
        value_weight,
        out_weight,
        up_weight,
        down_weight,
        up_bias,
        query_bias,
        value_bias,
        [ln1_gain, ln1_offset, out_bias, ln2_gain, ln2_offset, down_bias],
    )
    together = lax.optimization_barrier

    def after(values, first):
        return together((values, first))[0]

    def doubled(values, came):
        return jnp.concatenate([values, came], axis=0)

    came = swap(pieces, 2 * BIT_Z)
    normed, normed_t = first_norm(frames, table)
    came, normed = together((came, normed))
    big = after(big[None], came)
    pieces = doubled(pieces, came)
    big = doubled(big, swap(big, 2 * BIT_Z))
    came = swap(pieces, BIT_Z)
    big = after(big, came)
    pieces = doubled(pieces, came)
    near = doubled(pieces, swap(pieces, BIT_Y))
    big = doubled(big, swap(big, BIT_Z))
    far = swap(near, BIT_CORE)
    near_other = swap(near, BIT_X)

    normed_one, big, far = together((normed, big, far))
    big_y = swap(big, BIT_Y)
    big_x = swap(big, BIT_X)
    half_done = list(attend_forward_fast(1, normed_one, near, far, table))
    near_other, big_y, big_x, half_done[4] = together((near_other, big_y, big_x, half_done[4]))
    far_other = swap(near_other, BIT_CORE)
    big_xy = swap(big_y, BIT_X)
    across = [swap(p, BIT_CORE) for p in (big, big_y, big_x)]
    q, k, v, probs, context, rest, inverse, weights = attend_forward_fast(
        0, normed, near_other, far_other, table, half_done
    )
    big_xy, context = together((big_xy, context))
    across.append(swap(big_xy, BIT_CORE))
    masks = (0, BIT_Y, BIT_X, BIT_X | BIT_Y)
    masks += tuple(m | BIT_CORE for m in masks)
    output, grads, grad_hidden, send, keep, vec = middle(
        context, frames, cotangent, table, masks, [big, big_y, big_x, big_xy, *across]
    )

    def backward(first, pairs, grads, vec, before=()):
        return attend_backward_fast(
            first, pairs, q, k, v, probs, inverse, context, rest, grads, normed_t, weights, vec, before
        )

    came = swap(send, BIT_CORE)
    *done, vec_w = backward(0, 1, grads, jnp.zeros_like(table[0:8]))
    came, grads = lax.optimization_barrier((came, grads))
    mine, vec, *sends = spread(keep, vec, [came], part_xy, (1, 2, 3), 4)
    *sends, grads = lax.optimization_barrier((*sends, grads))
    came_xy = [swap(s, m) for s, m in zip(sends, (BIT_X, BIT_Y, BIT_X | BIT_Y))]
    *done, vec_w = backward(1, 2, grads, vec_w, done)
    across = done[3][0]
    came_xy, grads, across = lax.optimization_barrier((came_xy, grads, across))
    mine, vec, *sends = spread(mine, vec, came_xy, part_z, (1, 2, 3), LAYERS)
    *sends, grads, across = lax.optimization_barrier((*sends, grads, across))
    got = swap(across, BIT_X)
    came_z = [swap(s, m * BIT_Z) for s, m in zip(sends, (1, 2, 3))]
    *done, dw, vec_w = backward(3, 1, grads, vec_w, done)

    came_z, got, vec_w = together((came_z, got, vec_w))
    send, keep_w, vec_w = gather_grads(table, dw, got, vec_w)
    came = [swap(send, BIT_CORE)]
    mine_w, vec_w, *sends = spread(keep_w, vec_w, came, part_yz, (1, 2, 3), 4)
    came = [swap(s, m) for s, m in zip(sends, (BIT_Z, BIT_Y, BIT_Z | BIT_Y))]
    grad_frames = input_grads(0, 4, frames, grad_hidden, table, weights, done)
    came, grad_frames = together((came, grad_frames))
    mine_w, vec_w, *sends = spread(mine_w, vec_w, came, part_high, (1, None, None), 2)
    came_w = [
        swap(s, m) for s, m in zip(sends, (2 * BIT_Z, BIT_X, 2 * BIT_Z | BIT_X))
    ]
    grad_frames = input_grads(4, 2, frames, grad_hidden, table, weights, done, [grad_frames])
    came_w, grad_frames = together((came_w, grad_frames))
    down_grad, up_grad, out_grad, query_grad, key_grad, value_grad, *vectors = finish(
        mine, vec, mine_w, vec_w, came_z, came_w, ff, ow
    )
    vectors = [v.reshape(-1) for v in vectors]
    out_bias_grad, gain_two, offset_two, down_bias_grad, up_bias_grad = vectors[:5]
    gain_one, offset_one, query_bias_grad, value_bias_grad = vectors[5:]
    return (
        output,
        grad_frames,
        gain_one,
        offset_one,
        query_grad,
        query_bias_grad,
        key_grad,
        value_grad,
        value_bias_grad,
        out_grad.T,
        out_bias_grad,
        gain_two,
        offset_two,
        up_grad.T,
        up_bias_grad,
        down_grad,
        down_bias_grad,
    )


def solution(mesh):
    placed = (
        P(("dp", "head"), None),
        P(("dp", "head"), None),
        P(),
        P(),
        P(),
        P(),
        P(),
        P("dp", "head"),
        P(),
        P("dp", "head"),
        P("dp", "head"),
        P(),
        P("head", "dp"),
        P(),
        P(),
        P(),
        P(None, ("dp", "head")),
        P(),
        P(("dp", "head"), None),
        P(),
    )
    step = on_device
    if mesh.shape["dp"] == 4 * LAYERS and mesh.shape["head"] == SLOTS:
        step = on_whole_windows
    return jax.shard_map(
        step,
        mesh=mesh,
        in_specs=placed,
        out_specs=(
            P(("dp", "head"), None),
            P(("dp", "head"), None),
            P(),
            P(),
            P("dp", "head"),
            P(),
            P("dp", "head"),
            P("dp", "head"),
            P(),
            P("head", "dp"),
            P(),
            P(),
            P(),
            P(None, ("dp", "head")),
            P(),
            P(("dp", "head"), None),
            P(),
        ),
        check_vma=False,
    )
```

```python
import functools

import jax
import jax.numpy as jnp
from jax import lax
from jax.experimental import pallas as pl
from jax.experimental.pallas import tpu as pltpu
from jax.sharding import PartitionSpec as P

FRAMES = 1500
LANGS = 99
TASKS = 2
SLOTS = 2
HEAD_DIM = 64


def layer_norm(values, gain_vec, offset_vec):
    center = jnp.mean(values, axis=-1, keepdims=True)
    centred = values - center
    spread = jnp.mean(centred * centred, axis=-1, keepdims=True)
    return centred * lax.rsqrt(spread + 1e-05) * gain_vec + offset_vec


def gelu_exact(values):
    return jax.nn.gelu(values, approximate=False)


def contract(first_mat, second_mat):
    return lax.dot_general(
        first_mat, second_mat, (((0,), (0,)), ((), ())), preferred_element_type=jnp.float32
    )


def times_t(first_mat, second_mat):
    return lax.dot_general(
        first_mat, second_mat, (((1,), (1,)), ((), ())), preferred_element_type=jnp.float32
    )


def window_weights(window_live, language, task):
    groups = language * TASKS + task
    labels = jnp.arange(LANGS * TASKS, dtype=jnp.int32)
    matches = groups[:, None] == labels[None, :]
    live_float = window_live.astype(jnp.float32)
    counts = jnp.sum(jnp.where(matches, live_float[:, None], 0.0), axis=0)
    present = jnp.sum((counts > 0.5).astype(jnp.float32))
    own_count = jnp.sum(jnp.where(matches, counts[None, :], 0.0), axis=1)
    return live_float * jnp.sum(live_float) / (present * jnp.maximum(own_count, 1.0))


def window_scores(queries, keys_all):
    return jnp.einsum("qhd,khd->hqk", queries, keys_all, preferred_element_type=jnp.float32) * 0.125


def attend_forward(record):
    queries, keys_all, values_all = record
    scores = window_scores(queries, keys_all)
    highest_score = jnp.max(scores, axis=-1, keepdims=True)
    expo = jnp.exp(scores - highest_score)
    totals = jnp.sum(expo, axis=-1, keepdims=True)
    attn_probs = (expo / totals).astype(jnp.bfloat16)
    context = jnp.einsum("hqk,khd->qhd", attn_probs, values_all, preferred_element_type=jnp.float32)
    return (context.astype(jnp.bfloat16), (highest_score + jnp.log(totals))[..., 0])


def attend_backward(record):
    queries, keys_all, values_all, log_totals, grad_context = record
    scores = window_scores(queries, keys_all)
    attn_probs = jnp.exp(scores - log_totals[..., None])
    grad_probs = jnp.einsum(
        "qhd,khd->hqk", grad_context, values_all, preferred_element_type=jnp.float32
    )
    grad_values = jnp.einsum(
        "hqk,qhd->khd",
        attn_probs.astype(jnp.bfloat16),
        grad_context,
        preferred_element_type=jnp.float32,
    )
    row_delta = jnp.sum(grad_probs * attn_probs, axis=-1, keepdims=True)
    grad_scores = (attn_probs * (grad_probs - row_delta)).astype(jnp.bfloat16)
    grad_queries = (
        jnp.einsum("hqk,khd->qhd", grad_scores, keys_all, preferred_element_type=jnp.float32)
        * 0.125
    )
    grad_keys = (
        jnp.einsum("hqk,qhd->khd", grad_scores, queries, preferred_element_type=jnp.float32) * 0.125
    )
    return (
        grad_queries.astype(jnp.bfloat16),
        grad_keys.astype(jnp.bfloat16),
        grad_values.astype(jnp.bfloat16),
    )


def on_device(
    frames,
    cotangent,
    window_live,
    language,
    task,
    ln1_gain,
    ln1_offset,
    query_weight,
    query_bias,
    key_weight,
    value_weight,
    value_bias,
    out_weight,
    out_bias,
    ln2_gain,
    ln2_offset,
    up_weight,
    up_bias,
    down_weight,
    down_bias,
):
    local_rows = frames.shape[0]
    head_index = lax.axis_index("head")
    data_index = lax.axis_index("dp")
    per_window = window_weights(window_live, language, task)
    slot_ids = (
        head_index * local_rows + jnp.arange(local_rows, dtype=jnp.int32)
    ) // FRAMES + data_index * SLOTS
    window_ids = jnp.arange(per_window.shape[0], dtype=jnp.int32)
    frame_match = slot_ids[:, None] == window_ids[None, :]
    frame_weight = jnp.sum(jnp.where(frame_match, per_window[None, :], 0.0), axis=1)
    frame_live = jnp.sum(
        jnp.where(frame_match, window_live.astype(jnp.float32)[None, :], 0.0), axis=1
    )
    inputs = frames.astype(jnp.float32)
    normed, ln1_back = jax.vjp(layer_norm, inputs, ln1_gain, ln1_offset)
    normed_low = normed.astype(jnp.bfloat16)
    query_head, key_head, value_head, out_head = (
        lax.all_gather(query_weight, "dp", axis=0, tiled=True),
        lax.all_gather(key_weight, "dp", axis=0, tiled=True),
        lax.all_gather(value_weight, "dp", axis=0, tiled=True),
        lax.all_gather(out_weight, "dp", axis=1, tiled=True),
    )
    head_width = query_head.shape[1]
    local_heads = head_width // HEAD_DIM
    joint_weight = jnp.concatenate([query_head, key_head, value_head], axis=1)
    joint_bias = jnp.concatenate(
        [
            lax.dynamic_slice_in_dim(query_bias, head_index * head_width, head_width),
            jnp.zeros((head_width,), jnp.float32),
            lax.dynamic_slice_in_dim(value_bias, head_index * head_width, head_width),
        ]
    )
    normed_all = lax.all_gather(normed_low, "head", axis=0, tiled=True)
    projected = (
        jnp.dot(normed_all, joint_weight, preferred_element_type=jnp.float32) + joint_bias
    ).astype(jnp.bfloat16)
    shaped = projected.reshape(-1, FRAMES, 3, local_heads, HEAD_DIM)
    queries = shaped[:, :, 0]
    keys_all = shaped[:, :, 1]
    values_all = shaped[:, :, 2]
    context, log_totals = lax.map(attend_forward, (queries, keys_all, values_all))
    context_flat = context.reshape(-1, head_width)
    branch = lax.psum_scatter(
        jnp.dot(context_flat, out_head, preferred_element_type=jnp.float32),
        "head",
        scatter_dimension=0,
        tiled=True,
    )
    hidden = inputs + branch + out_bias
    normed_two, ln2_back = jax.vjp(layer_norm, hidden, ln2_gain, ln2_offset)
    normed_two_low = normed_two.astype(jnp.bfloat16)
    up_full, down_full = (
        lax.all_gather(up_weight, ("dp", "head"), axis=1, tiled=True),
        lax.all_gather(down_weight, ("dp", "head"), axis=0, tiled=True),
    )
    pre_act = jnp.dot(normed_two_low, up_full, preferred_element_type=jnp.float32) + up_bias
    activated, gelu_back = jax.vjp(gelu_exact, pre_act)
    activated_low = activated.astype(jnp.bfloat16)
    result = (
        hidden + jnp.dot(activated_low, down_full, preferred_element_type=jnp.float32) + down_bias
    )
    output = (result * frame_live[:, None]).astype(jnp.bfloat16)
    grad_result = cotangent.astype(jnp.float32) * frame_weight[:, None]
    grad_two = grad_result.astype(jnp.bfloat16)
    grad_down = contract(activated_low, grad_two)
    grad_down_bias = jnp.sum(grad_two.astype(jnp.float32), axis=0)
    grad_activated = times_t(grad_two, down_full)
    grad_pre = gelu_back(grad_activated)[0].astype(jnp.bfloat16)
    grad_up = contract(normed_two_low, grad_pre)
    grad_up_bias = jnp.sum(grad_pre.astype(jnp.float32), axis=0)
    grad_normed_two = times_t(grad_pre, up_full)
    grad_hidden_ln, grad_ln2_gain, grad_ln2_offset = ln2_back(grad_normed_two)
    grad_hidden = grad_result + grad_hidden_ln
    grad_branch = grad_hidden.astype(jnp.bfloat16)
    grad_out_bias = jnp.sum(grad_branch.astype(jnp.float32), axis=0)
    branch_all = lax.all_gather(grad_branch, "head", axis=0, tiled=True)
    grad_context = times_t(branch_all, out_head).astype(jnp.bfloat16)
    grad_out_head = contract(context_flat, branch_all)
    grad_context_win = grad_context.reshape(-1, FRAMES, local_heads, HEAD_DIM)
    grad_queries, grad_keys, grad_values = lax.map(
        attend_backward, (queries, keys_all, values_all, log_totals, grad_context_win)
    )
    grad_joint = jnp.concatenate(
        [
            grad_queries.reshape(-1, head_width),
            grad_keys.reshape(-1, head_width),
            grad_values.reshape(-1, head_width),
        ],
        axis=1,
    )
    grad_joint_weight = contract(normed_all, grad_joint)
    joint_sums = jnp.sum(grad_joint.astype(jnp.float32), axis=0)
    empty_vec = jnp.zeros((query_bias.shape[0],), jnp.float32)
    grad_query_bias = lax.dynamic_update_slice(
        empty_vec, joint_sums[:head_width], (head_index * head_width,)
    )
    grad_value_bias = lax.dynamic_update_slice(
        empty_vec, joint_sums[2 * head_width :], (head_index * head_width,)
    )
    grad_normed = lax.psum_scatter(
        times_t(grad_joint, joint_weight), "head", scatter_dimension=0, tiled=True
    )
    grad_inputs_ln, grad_ln1_gain, grad_ln1_offset = ln1_back(grad_normed)
    grad_frames = (grad_hidden + grad_inputs_ln).astype(jnp.bfloat16)
    grad_query_w, grad_key_w, grad_value_w, grad_out_w = (
        lax.psum_scatter(grad_joint_weight[:, :head_width], "dp", scatter_dimension=0, tiled=True),
        lax.psum_scatter(
            grad_joint_weight[:, head_width : 2 * head_width], "dp", scatter_dimension=0, tiled=True
        ),
        lax.psum_scatter(
            grad_joint_weight[:, 2 * head_width :], "dp", scatter_dimension=0, tiled=True
        ),
        lax.psum_scatter(grad_out_head, "dp", scatter_dimension=1, tiled=True),
    )
    grad_up_w, grad_down_w = (
        lax.psum_scatter(grad_up, ("dp", "head"), scatter_dimension=1, tiled=True),
        lax.psum_scatter(grad_down, ("dp", "head"), scatter_dimension=0, tiled=True),
    )
    (
        sum_ln1_gain,
        sum_ln1_offset,
        sum_query_bias,
        sum_value_bias,
        sum_out_bias,
        sum_ln2_gain,
        sum_ln2_offset,
        sum_up_bias,
        sum_down_bias,
    ) = lax.psum(
        (
            grad_ln1_gain,
            grad_ln1_offset,
            grad_query_bias,
            grad_value_bias,
            grad_out_bias,
            grad_ln2_gain,
            grad_ln2_offset,
            grad_up_bias,
            grad_down_bias,
        ),
        ("dp", "head"),
    )
    return (
        output,
        grad_frames,
        sum_ln1_gain,
        sum_ln1_offset,
        grad_query_w,
        sum_query_bias,
        grad_key_w,
        grad_value_w,
        sum_value_bias,
        grad_out_w,
        sum_out_bias,
        sum_ln2_gain,
        sum_ln2_offset,
        grad_up_w,
        sum_up_bias,
        grad_down_w,
        sum_down_bias,
    )


LANES = 128
PADDED = 1536
LOG2E = 1.4426950408889634
MASKED = -30000.0
F32 = jnp.float32
BF16 = jnp.bfloat16
LN1_GAIN, LN1_OFFSET, OUT_BIAS, LN2_GAIN, LN2_OFFSET, DOWN_BIAS = range(6)
WEIGHT, LIVE, QUERY_BIAS, VALUE_BIAS, UP_BIAS = 6, 7, 8, 10, 11
BIT_X, BIT_CORE, BIT_Y, BIT_Z = 1, 2, 4, 8
LAYERS = 4


def dot_on(first_mat, second_mat, first_dim, second_dim):
    return lax.dot_general(
        first_mat,
        second_mat,
        (((first_dim,), (second_dim,)), ((), ())),
        preferred_element_type=F32,
    )


def params(microseconds, mebibytes):
    return dict(
        compiler_params=pltpu.CompilerParams(vmem_limit_bytes=mebibytes << 20),
        cost_estimate=pl.CostEstimate(
            flops=int(microseconds * 1e9), bytes_accessed=1 << 20, transcendentals=0
        ),
    )


def whole(shape):
    return pl.BlockSpec(shape, lambda *_: (0,) * len(shape), pipeline_mode=pl.Buffered(1))


def struct(shape, dtype):
    return jax.ShapeDtypeStruct(shape, dtype)


def place():
    dp = lax.axis_index("dp")
    return dp, lax.axis_index("head")


def pack_kernel(
    live_ref,
    language_ref,
    task_ref,
    query_ref,
    key_ref,
    value_ref,
    out_ref,
    up_ref,
    down_ref,
    upb_ref,
    qb_ref,
    vb_ref,
    *refs,
):
    vectors, (pieces_ref, big_ref, table_ref) = refs[:6], refs[6:]
    rows, half = query_ref.shape
    ff = down_ref.shape[0]
    dp, side = place()
    for j, ref in enumerate((query_ref, key_ref, value_ref)):
        pieces_ref[0, j * rows : (j + 1) * rows, :] = ref[...]
    up = up_ref[...]
    big_ref[0:ff, :] = down_ref[:, 0:half]
    big_ref[ff : 2 * ff, :] = down_ref[:, half:]
    big_ref[2 * ff : 3 * ff, :] = up[:, 0:half]
    big_ref[3 * ff : 4 * ff, :] = up[:, half:]
    big_ref[4 * ff :, :] = out_ref[...]
    for j, ref in enumerate(vectors):
        table_ref[j : j + 1, :] = ref[...]
    for j, ref in ((QUERY_BIAS, qb_ref), (VALUE_BIAS, vb_ref)):
        first, second = ref[:, 0:half], ref[:, half:]
        table_ref[j : j + 1, 0:half] = jnp.where(side == 0, second, first)
        table_ref[j : j + 1, half:] = jnp.where(side == 0, first, second)
    table_ref[QUERY_BIAS + 1 : QUERY_BIAS + 2, :] = jnp.zeros((1, 2 * half), F32)
    for j in range(4):
        table_ref[UP_BIAS + j : UP_BIAS + j + 1, :] = upb_ref[:, j * 2 * half : (j + 1) * 2 * half]
    slots = live_ref.shape[0]
    lane = lax.broadcasted_iota(jnp.int32, (1, LANES), 1)
    groups = jnp.full((1, LANES), -1, jnp.int32)
    live = jnp.zeros((1, LANES), F32)
    for t in range(slots):
        groups = jnp.where(lane == t, language_ref[t] * TASKS + task_ref[t], groups)
        live = jnp.where(lane == t, live_ref[t].astype(F32), live)
    counts = jnp.zeros((1, LANES), F32)
    for t in range(slots):
        group = language_ref[t] * TASKS + task_ref[t]
        counts = counts + jnp.where(groups == group, live_ref[t].astype(F32), 0.0)
    counts = jnp.maximum(counts, 1.0)
    shares = jnp.broadcast_to(live / counts, (8, LANES))
    present = jnp.floor(jnp.sum(shares, axis=1, keepdims=True)[0:1] + 0.5)
    total = jnp.sum(jnp.broadcast_to(live, (8, LANES)), axis=1, keepdims=True)[0:1]
    weights = live * total / (present * counts)
    mine = lane == dp * SLOTS + side
    for j, values in ((WEIGHT, weights), (LIVE, live)):
        picked = jnp.broadcast_to(jnp.where(mine, values, 0.0), (8, LANES))
        picked = jnp.sum(picked, axis=1, keepdims=True)[0:1]
        table_ref[j : j + 1, :] = jnp.broadcast_to(picked, (1, 2 * half))


def pack(live, language, task, query, key, value, out, up, down, up_bias, qb, vb, vectors):
    rows, half = query.shape
    ff, width = down.shape
    scalars = pl.BlockSpec(memory_space=pltpu.SMEM)
    row = lambda values: values.reshape(1, -1)
    rest = [query, key, value, out.T, up.T, down, row(up_bias), row(qb), row(vb)] + [
        row(v) for v in vectors
    ]
    return pl.pallas_call(
        pack_kernel,
        in_specs=[scalars] * 3 + [pl.BlockSpec(memory_space=pltpu.VMEM)] * len(rest),
        out_shape=[
            struct((1, 3 * rows, half), BF16),
            struct((4 * ff + rows, half), BF16),
            struct((16, width), F32),
        ],
        name="pack",
        **params(3, 58),
    )(live, language, task, *rest)


def real_rows(x_ref, first=0):
    tile = pl.program_id(0) + first
    return tile * x_ref.shape[0] + lax.broadcasted_iota(jnp.int32, x_ref.shape, 0) < FRAMES


def unit_rows(values):
    centred = values - jnp.mean(values, axis=1, keepdims=True)
    scale = lax.rsqrt(jnp.mean(centred * centred, axis=1, keepdims=True) + 1e-05)
    return centred * scale, scale


def unit_back(lifted, unit, scale):
    mean_one = jnp.mean(lifted, axis=1, keepdims=True)
    mean_two = jnp.mean(lifted * unit, axis=1, keepdims=True)
    return scale * (lifted - mean_one - unit * mean_two)


def norm_kernel(x_ref, table_ref, n_ref, nt_ref):
    unit, _ = unit_rows(jnp.where(real_rows(x_ref), x_ref[...].astype(F32), 0.0))
    normed = unit * table_ref[LN1_GAIN : LN1_GAIN + 1, :] + table_ref[LN1_OFFSET : LN1_OFFSET + 1, :]
    n_ref[...] = normed.astype(BF16)
    nt_ref[...] = normed.T.astype(BF16)


def first_norm(frames, table):
    width = frames.shape[1]
    tile = 256
    return pl.pallas_call(
        norm_kernel,
        grid=(PADDED // tile,),
        in_specs=[pl.BlockSpec((tile, width), lambda i: (i, 0)), whole(table.shape)],
        out_specs=[
            pl.BlockSpec((tile, width), lambda i: (i, 0)),
            pl.BlockSpec((width, tile), lambda i: (0, i)),
        ],
        out_shape=[struct((PADDED, width), BF16), struct((width, PADDED), BF16)],
        name="first_norm",
        **params(4, 14),
    )(frames, table)


def lane_masks(shape, h):
    lane = lax.broadcasted_iota(jnp.int32, shape, 1)
    return lane >= HEAD_DIM if h else lane < HEAD_DIM


def masked(values, h):
    own = lane_masks(values.shape, h)
    return jnp.where(own, values, 0.0)


def forward_kernel(side_at, n_ref, near_ref, far_ref, table_ref, *refs):
    (
        q_ref, k_ref, v_ref, p_ref, c_ref, rest_ref, inv_ref, w_ref,
        keys_ref, vt_ref, both_ref, small_ref,
    ) = refs[-12:]
    pair, step = pl.program_id(0), pl.program_id(1)
    count, rows3, half = near_ref.shape
    rows = rows3 // 3

    @pl.when((pair == 0) & (step == 0))
    def _():
        dp, _ = place()
        for core, ref in enumerate((near_ref, far_ref)):
            for t in range(count):
                owner = dp ^ ((t & 1) * 8 + (t & 2) * 2 + (t & 4) // 2 + core)
                at = pl.ds(pl.multiple_of(owner * rows, rows), rows)
                for j in range(3):
                    w_ref[j, at, :] = ref[t, j * rows : (j + 1) * rows, :]

    @pl.when(step == 0)
    def _():
        columns = pl.ds(pl.multiple_of(pair * LANES, LANES), LANES)
        places = pl.ds(pl.multiple_of(pair * LANES + side_at * half, LANES), LANES)
        for j, out in enumerate((q_ref, k_ref, v_ref)):
            bias = table_ref[QUERY_BIAS + j : QUERY_BIAS + j + 1, places]
            out[...] = (dot_on(n_ref[...], w_ref[j, :, columns], 1, 0) + bias).astype(BF16)
        keys = k_ref[...].astype(F32) * (LOG2E * 0.125)
        queries = q_ref[...].astype(F32)
        high = keys.astype(BF16).astype(F32)
        flipped = v_ref[...].astype(F32).T
        spare = vt_ref.shape[1] - HEAD_DIM
        shape = (vt_ref.shape[1], flipped.shape[1])
        real = lax.broadcasted_iota(jnp.int32, shape, 1) < FRAMES
        first = lax.broadcasted_iota(jnp.int32, shape, 0) == HEAD_DIM
        shape = (LANES, LANES)
        one, two = (lax.broadcasted_iota(jnp.int32, shape, j) < HEAD_DIM for j in (0, 1))
        same = jnp.where(one == two, 1.0, 0.0).astype(BF16)
        norms = [
            jnp.max(dot_on((m * m).astype(BF16), same, 1, 0), axis=0, keepdims=True)
            for m in (queries, keys)
        ]
        bound = jnp.max(norms[0] * norms[1])
        small_ref[0] = (bound < 90.0 * 90.0).astype(jnp.int32)
        for h in (0, 1):
            keys_ref[h, :, 0:LANES] = masked(high, h).astype(BF16)
            keys_ref[h, :, LANES:] = masked(keys - high, h).astype(BF16)
            mine = flipped[HEAD_DIM * h : HEAD_DIM * (h + 1), :]
            mine = jnp.concatenate([mine, mine[0:spare]], axis=0)
            vt_ref[h] = jnp.where(real, jnp.where(first, 1.0, mine), 0.0).astype(BF16)

    tile = c_ref.shape[0]
    tail = FRAMES // 16 * 16

    def attend(h, start, size, at, shift):
        queries = q_ref[pl.ds(start, size), :]
        scores = dot_on(keys_ref[h], jnp.concatenate([queries, queries], axis=1), 1, 1)
        if shift:
            real = lax.broadcasted_iota(jnp.int32, scores.shape, 0) < FRAMES
            scores = jnp.where(real, scores, -1e30)
            scores = scores - jnp.max(scores, axis=0, keepdims=True)
        probs = jnp.exp2(scores)
        low = probs.astype(BF16)
        p_ref[h, 0:tail, at] = low[0:tail]
        last = probs[tail:]
        real = lax.broadcasted_iota(jnp.int32, last.shape, 0) < FRAMES - tail
        p_ref[h, tail:, at] = jnp.where(real, last, 0.0).astype(BF16)
        summed = dot_on(vt_ref[h], low, 1, 0)
        inverse = 1.0 / summed[HEAD_DIM : HEAD_DIM + 1, :]
        both_ref[0, h, :, at] = summed[0:HEAD_DIM, :] * inverse
        both_ref[1, h, :, at] = jnp.broadcast_to(inverse, (HEAD_DIM, inverse.shape[1]))

    @pl.when(small_ref[0] == 1)
    def _():
        for h in (0, 1):
            attend(h, step * tile, tile, slice(0, tile), False)

    @pl.when(small_ref[0] == 0)
    def _():
        size = LANES

        @pl.loop(0, 2 * tile // size)
        def _(t):
            h, t = t & 1, t >> 1
            at = pl.ds(pl.multiple_of(t * size, size), size)
            attend(h, pl.multiple_of(step * tile + t * size, size), size, at, True)

    context = both_ref[0].reshape(LANES, tile).T
    low = context.astype(BF16)
    c_ref[...] = low
    rest_ref[...] = (context - low.astype(F32)).astype(BF16)
    inv_ref[...] = both_ref[1].reshape(LANES, tile).T


def attend_forward_fast(side_at, normed, near, far, table, before=()):
    rows, width = normed.shape
    half = near.shape[2]
    pairs = half // LANES
    tile = 768
    at = side_at * pairs
    block = pl.BlockSpec((tile, LANES), lambda p, i: (i, p + at))
    full = pl.BlockSpec((rows, LANES), lambda p, i: (0, p + at))
    weights = pl.BlockSpec((3, width, half), lambda p, i: (0, 0, side_at))
    return pl.pallas_call(
        functools.partial(forward_kernel, side_at),
        grid=(pairs, rows // tile),
        in_specs=[whole(normed.shape), whole(near.shape), whole(far.shape), whole(table.shape)]
        + [pl.BlockSpec(memory_space=pl.ANY)] * len(before),
        out_specs=[
            full, full, full,
            pl.BlockSpec((2, rows, tile), lambda p, i: (p + at, 0, i)),
            block, block, block, weights,
        ],
        out_shape=[struct((rows, width), BF16)] * 3
        + [
            struct((width // HEAD_DIM, rows, rows), BF16),
            pltpu.HBM((rows, width), BF16),
            pltpu.HBM((rows, width), BF16),
            struct((rows, width), F32),
            pltpu.HBM((3, width, width), BF16),
        ],
        scratch_shapes=[
            pltpu.VMEM((2, rows, 2 * LANES), BF16),
            pltpu.VMEM((2, HEAD_DIM + 16, rows), BF16),
            pltpu.VMEM((2, 2, HEAD_DIM, tile), F32),
            pltpu.SMEM((1,), jnp.int32),
        ],
        input_output_aliases={4 + j: j for j in range(len(before))},
        name="attend_forward",
        **params(15, 40),
    )(normed, near, far, table, *before)


def backward_kernel(
    first, q_ref, k_ref, v_ref, p_ref, inv_ref, c_ref, rest_ref, g_ref, nt_ref, w_ref,
    vec_in_ref, *refs
):
    dq_ref, dk_ref, dv_ref, dw_ref, vec_ref, vals_ref, kt_ref, acck, accv, acc_one, acc_two = refs[-11:]
    pair, step = pl.program_id(0), pl.program_id(1)
    last = step == pl.num_programs(1) - 1

    @pl.when(step == 0)
    def _():
        values = v_ref[...].astype(F32)
        for h in (0, 1):
            vals_ref[h] = masked(values, h).astype(BF16)
        kt_ref[...] = k_ref[...].astype(F32).T.astype(BF16)
        acck[...] = jnp.zeros_like(acck)
        accv[...] = jnp.zeros_like(accv)

    tile = q_ref.shape[0]
    plain = q_ref[...].astype(F32)
    divided = g_ref[...].astype(F32) * inv_ref[...]
    low = divided.astype(BF16)
    divided = low.astype(F32)
    products = (divided * (c_ref[...].astype(F32) + rest_ref[...].astype(F32))).T
    diffs, queries, flipped = [], [], []
    for h in (0, 1):
        rows = slice(HEAD_DIM * h, HEAD_DIM * (h + 1))
        row_delta = jnp.sum(products[rows], axis=0, keepdims=True)
        accv[...] += dot_on(p_ref[h], masked(divided, h).astype(BF16), 1, 0)
        grad_probs = dot_on(vals_ref[h], low, 1, 1)
        diff = p_ref[h] * (grad_probs - row_delta).astype(BF16)
        diffs.append(diff)
        queries.append(masked(plain, h).astype(BF16))
        flipped.append(dot_on(kt_ref[rows, :], diff, 1, 0))
    acck[...] += dot_on(diffs[0], queries[0], 1, 0) + dot_on(diffs[1], queries[1], 1, 0)
    at = pl.ds(pl.multiple_of(step * tile, tile), tile)
    dq_ref[at, :] = (jnp.concatenate(flipped, axis=0) * 0.125).T.astype(BF16)

    @pl.when(last & (pair == 0))
    def _():
        acc_one[...] = jnp.zeros_like(acc_one)
        acc_two[...] = jnp.zeros_like(acc_two)
        vec_ref[...] = vec_in_ref[...]

    @pl.when(last)
    def _():
        dk_ref[...] = (acck[...] * 0.125).astype(BF16)
        dv_ref[...] = accv[...].astype(BF16)
        columns = pl.ds(pl.multiple_of((pair + first) * LANES, LANES), LANES)
        both = jnp.concatenate([dq_ref[...], dk_ref[...]], axis=1)
        both = dot_on(nt_ref[...], both, 1, 0)
        products = [both[:, 0:LANES], both[:, LANES:], dot_on(nt_ref[...], dv_ref[...], 1, 0)]
        for j, ref in enumerate((dq_ref, dk_ref, dv_ref)):
            dw = products[j]
            dw_ref[j] = dw.astype(dw_ref.dtype)
            column_sums = jnp.sum(ref[...].astype(F32), axis=0, keepdims=True)
            weights = w_ref[j].astype(F32)
            acc_one[...] += weights * dw
            acc_two[...] += weights * column_sums
            if j != 1:
                vec_ref[2 + j // 2 : 3 + j // 2, columns] = column_sums

    @pl.when(last & (pair == pl.num_programs(0) - 1))
    def _():
        for j, ref in enumerate((acc_one, acc_two)):
            vec_ref[j : j + 1, :] += jnp.sum(ref[...].T, axis=0, keepdims=True)


def attend_backward_fast(
    first, pairs, q, k, v, probs, inverse, context, rest, grads, normed_t, weights, vec, before=()
):
    rows, width = q.shape
    half = width // 2
    context, rest, grads, weights = (
        pltpu.with_memory_space_constraint(x, pltpu.HBM) for x in (context, rest, grads, weights)
    )
    tile = 384 if pairs > 1 else 256
    block = pl.BlockSpec((tile, LANES), lambda p, i: (i, p + first))
    full = pl.BlockSpec((rows, LANES), lambda p, i: (0, p + first))
    gradient = pl.BlockSpec(
        (None, 3, width, LANES), lambda p, i: ((p + first) // 2, 0, 0, (p + first) % 2)
    )
    in_specs = [
        block, full, full,
        pl.BlockSpec((2, rows, tile), lambda p, i: (p + first, 0, i)),
        block, block, block, block, whole(normed_t.shape),
        pl.BlockSpec((3, width, LANES), lambda p, i: (0, 0, p + first)),
        whole(vec.shape),
    ]
    count = len(in_specs)
    return pl.pallas_call(
        functools.partial(backward_kernel, first),
        grid=(pairs, rows // tile),
        in_specs=in_specs + [pl.BlockSpec(memory_space=pl.ANY)] * len(before),
        out_specs=[full, full, full, gradient, whole(vec.shape)],
        out_shape=[struct((rows, width), BF16)] * 3
        + [struct((2, 3, width, half), BF16), struct(vec.shape, F32)],
        scratch_shapes=[
            pltpu.VMEM((2, rows, LANES), BF16),
            pltpu.VMEM((LANES, rows), BF16),
            pltpu.VMEM((rows, LANES), F32),
            pltpu.VMEM((rows, LANES), F32),
            pltpu.VMEM((width, LANES), F32),
            pltpu.VMEM((width, LANES), F32),
        ],
        input_output_aliases={count + j: j for j in range(len(before))},
        name="attend_backward",
        **params(14 * pairs, 34),
    )(q, k, v, probs, inverse, context, rest, grads, normed_t, weights, vec, *before)


def middle_kernel(masks, c_ref, x_ref, cot_ref, table_ref, *refs):
    pieces, refs = refs[: len(masks)], refs[len(masks) :]
    out_ref, g_ref, gh_ref, send_ref, keep_ref, vec_ref = refs[:6]
    up_t, up_n, down_n, down_t, out_t, upb_t, acc_up, acc_down, acc_out, acc_upb, acc_vec = refs[6:]
    step = pl.program_id(0)
    dp, side = place()
    core = lax.rem(dp, 2)
    layers, piece_rows, half = pieces[0].shape
    devices = layers * len(masks)
    width = 2 * half
    ow = width // (devices // 2)
    ff = (piece_rows - ow) // 4
    hidden_all = devices * ff
    chunk = 1024
    chunks = hidden_all // chunk

    @pl.when(step == 0)
    def _():
        for mask, ref in zip(masks, pieces):

            @pl.loop(0, layers)
            def _(t, mask=mask, ref=ref):
                owner = (dp * 2 + side) ^ (mask + (t & 1) * 2 * BIT_Z + (t >> 1) * BIT_Z)
                rows = pl.ds(pl.multiple_of(owner * ff, ff), ff)
                down_n[rows, 0:half] = ref[t, 0:ff, :]
                down_n[rows, half:] = ref[t, ff : 2 * ff, :]
                up_t[rows, 0:half] = ref[t, 2 * ff : 3 * ff, :]
                up_t[rows, half:] = ref[t, 3 * ff : 4 * ff, :]
                rows = pl.ds(pl.multiple_of((owner >> 1) * ow, ow), ow)
                at = slice(0, half) if mask & BIT_X else slice(half, width)
                out_t[rows, at] = ref[t, 4 * ff :, :]

        @pl.loop(0, hidden_all // width)
        def _(j):
            rows = pl.ds(pl.multiple_of(j * width, width), width)
            up_n[:, rows] = up_t[rows, :].T
            down_t[:, rows] = down_n[rows, :].T
            bias = table_ref[pl.ds(UP_BIAS + j, 1), :]
            upb_t[rows, :] = jnp.broadcast_to(bias, (LANES, width)).T
            acc_upb[rows, :] = jnp.zeros((width, LANES), F32)

        @pl.loop(0, acc_out.shape[0])
        def _(j):
            acc_out[j] = jnp.zeros(acc_out.shape[1:], F32)

        acc_vec[...] = jnp.zeros_like(acc_vec)

    def add_to(ref, at, values):
        ref[at] = jnp.where(step == 0, 0.0, ref[at]) + values

    def row_of(j):
        return table_ref[j : j + 1, :]

    tile = x_ref.shape[0]
    real = real_rows(x_ref)
    branch = dot_on(c_ref[...], out_t[...], 1, 1)
    hidden = jnp.where(real, x_ref[...].astype(F32), 0.0) + branch + row_of(OUT_BIAS)
    unit, scale = unit_rows(hidden)
    normed = (unit * row_of(LN2_GAIN) + row_of(LN2_OFFSET)).astype(BF16)
    grad_result = jnp.where(real, cot_ref[...].astype(F32), 0.0) * row_of(WEIGHT)
    grad_two = grad_result.astype(BF16)
    result_t = jnp.zeros((width, tile), F32)
    grad_normed_t = jnp.zeros((width, tile), F32)
    for j in range(chunks):
        rows = slice(j * chunk, (j + 1) * chunk)
        slots = slice(j * chunk // ff, (j + 1) * chunk // ff)
        pre = dot_on(up_t[rows, :], normed, 1, 1) + upb_t[rows, 0:1]
        bell = 0.5 + 0.5 * lax.erf(pre * 0.7071067811865476)
        slope = bell + pre * (jnp.exp2(pre * pre * (-0.5 * LOG2E)) * 0.3989422804014327)
        activated = (pre * bell).astype(BF16)
        result_t += dot_on(down_t[:, rows], activated, 1, 0)
        add_to(acc_down, slots, dot_on(activated, grad_two, 1, 0).reshape(-1, ff, width))
        grad_pre = (dot_on(down_n[rows, :], grad_two, 1, 1) * slope).astype(BF16)
        rounded = grad_pre.astype(F32)
        partial = rounded[:, 0:LANES]
        for lanes in range(LANES, tile, LANES):
            partial += rounded[:, lanes : lanes + LANES]
        acc_upb[rows, :] += partial
        add_to(acc_up, slots, dot_on(grad_pre, normed, 1, 0).reshape(-1, ff, width))
        grad_normed_t += dot_on(up_n[:, rows], grad_pre, 1, 0)
    result = hidden + result_t.T + row_of(DOWN_BIAS)
    out_ref[...] = (result * row_of(LIVE)).astype(BF16)
    grad_normed = grad_normed_t.T
    grad_hidden = grad_result + unit_back(grad_normed * row_of(LN2_GAIN), unit, scale)
    gh_ref[...] = grad_hidden
    grad_branch = grad_hidden.astype(BF16)
    g_ref[...] = dot_on(grad_branch, out_t[...], 1, 0).astype(BF16)
    acc_out[...] += dot_on(grad_hidden.T.astype(BF16), c_ref[...], 1, 0).reshape(-1, ow, width)
    for j, term in enumerate(
        (grad_branch.astype(F32), grad_normed * unit, grad_normed, grad_two.astype(F32))
    ):
        acc_vec[8 * j : 8 * j + 8, :] += jnp.sum(term.reshape(-1, 8, width), axis=0)

    @pl.when(step == pl.num_programs(0) - 1)
    def _():
        targets = devices // 2
        for ref, bit in ((keep_ref, core), (send_ref, 1 - core)):

            @pl.loop(0, targets)
            def _(t, ref=ref, bit=bit):
                y, x, z = t >> 3, (t >> 2) & 1, t & 3
                chip = z * 2 + y
                slot = chip * 4 + bit * 2 + x
                near = pl.ds(pl.multiple_of((1 - (side ^ x)) * half, half), half)

                def rows(j, count=ff):
                    return pl.ds(pl.multiple_of(t * piece_rows + j * ff, 32), count)

                ref[rows(0), :] = acc_down[slot, :, 0:half].astype(BF16)
                ref[rows(1), :] = acc_down[slot, :, half:].astype(BF16)
                ref[rows(2), :] = acc_up[slot, :, 0:half].astype(BF16)
                ref[rows(3), :] = acc_up[slot, :, half:].astype(BF16)
                ref[rows(4, ow), :] = acc_out[chip * 2 + bit, :, near].astype(BF16)

        for j in range(4):
            total = jnp.sum(acc_vec[8 * j : 8 * j + 8, :], axis=0, keepdims=True)
            vec_ref[2 * j : 2 * j + 1, :] = total[:, 0:half]
            vec_ref[2 * j + 1 : 2 * j + 2, :] = total[:, half:]
        for j in range(chunks):
            total = jnp.sum(acc_upb[j * chunk : (j + 1) * chunk, :].T, axis=0, keepdims=True)
            for i in range(chunk // half):
                at = 8 + j * (chunk // half) + i
                vec_ref[at : at + 1, :] = total[:, i * half : (i + 1) * half]
        store_two(send_ref, targets * piece_rows, vec_ref[...])


def middle(context, frames, cotangent, table, masks, pieces):
    context, frames, cotangent = (
        pltpu.with_memory_space_constraint(x, pltpu.HBM) for x in (context, frames, cotangent)
    )
    rows, width = context.shape
    layers, piece_rows, half = pieces[0].shape
    devices = layers * len(masks)
    tile = 512
    ow = width // (devices // 2)
    ff = (piece_rows - ow) // 4
    hidden_all = devices * ff
    body = devices // 2 * piece_rows
    wide = pl.BlockSpec((tile, width), lambda i: (i, 0))
    return pl.pallas_call(
        functools.partial(middle_kernel, masks),
        grid=(rows // tile,),
        in_specs=[wide, wide, wide, whole(table.shape)] + [whole(p.shape) for p in pieces],
        out_specs=[wide, wide, wide, whole((body + 32, half)), whole((body, half)), whole((16, half))],
        out_shape=[
            struct(frames.shape, BF16),
            pltpu.HBM((rows, width), BF16),
            pltpu.HBM((rows, width), F32),
            struct((body + 32, half), BF16),
            struct((body, half), BF16),
            struct((16, half), F32),
        ],
        scratch_shapes=[
            pltpu.VMEM((hidden_all, width), BF16),
            pltpu.VMEM((width, hidden_all), BF16),
            pltpu.VMEM((hidden_all, width), BF16),
            pltpu.VMEM((width, hidden_all), BF16),
            pltpu.VMEM((width, width), BF16),
            pltpu.VMEM((hidden_all, LANES), F32),
            pltpu.VMEM((devices, ff, width), F32),
            pltpu.VMEM((devices, ff, width), F32),
            pltpu.VMEM((width // ow, ow, width), F32),
            pltpu.VMEM((hidden_all, LANES), F32),
            pltpu.VMEM((32, width), F32),
        ],
        name="middle",
        **params(38, 40),
    )(context, frames, cotangent, table, *pieces)


def store_two(ref, at, values):
    count = values.shape[0]
    high = values.astype(BF16)
    ref[at : at + count, :] = high
    ref[at + count : at + 2 * count, :] = (values - high.astype(F32)).astype(BF16)


def load_two(ref, at, count):
    return ref[at : at + count, :].astype(F32) + ref[at + count : at + 2 * count, :].astype(F32)


def spread_kernel(count, masks, keep_ref, vec_ref, *refs):
    came, (mine_ref, sum_ref, *sends) = refs[:count], refs[count:]
    size, half = mine_ref.shape
    dp, side = place()
    parts = keep_ref.shape[0] // size
    vec_rows = vec_ref.shape[0]
    vec = vec_ref[...]
    for ref in came:
        vec += load_two(ref, ref.shape[0] - 2 * vec_rows, vec_rows)
    sum_ref[...] = vec

    own = masks[0](dp, side)
    block = 96

    def total(part, at):
        rows = pl.ds(pl.multiple_of(part * size + at, 32), block)
        values = keep_ref[rows, :].astype(F32)
        for ref in came:
            if ref.shape[0] > 2 * vec_rows:
                values += ref[rows, :].astype(F32)
        return values

    @pl.loop(0, size // block)
    def _(t):
        at = pl.multiple_of(t * block, 32)
        mine_ref[pl.ds(at, block), :] = total(own, at)
        for mask, ref in zip(masks[1:], sends):
            if mask is not None:
                ref[pl.ds(at, block), :] = total(own ^ mask, at).astype(BF16)

    for ref in sends:
        store_two(ref, ref.shape[0] - 2 * vec_rows, vec)


def spread(keep, vec, came, own_part, masks, parts):
    rows, half = keep.shape
    size = rows // parts
    tail = 2 * vec.shape[0]
    vmem = pl.BlockSpec(memory_space=pltpu.VMEM)
    return pl.pallas_call(
        functools.partial(spread_kernel, len(came), (own_part, *masks)),
        in_specs=[vmem] * (2 + len(came)),
        out_specs=[vmem] * (2 + len(masks)),
        out_shape=[struct((size, half), F32), struct(vec.shape, F32)]
        + [struct(((0 if m is None else size) + tail, half), BF16) for m in masks],
        name="spread",
        **params(3, 14),
    )(keep, vec, *came)


def swap(values, mask):
    devices = lax.axis_size("dp") * lax.axis_size("head")
    return lax.ppermute(values, ("dp", "head"), [(i, i ^ mask) for i in range(devices)])


def part_xy(dp, side):
    return ((dp >> 1) & 1) * 2 + side


def part_yz(dp, side):
    return ((dp >> 1) & 1) * 2 + ((dp >> 2) & 1)


def part_z(dp, side):
    return dp >> 2


def part_high(dp, side):
    return dp >> 3


def gather_kernel(table_ref, dw_ref, got_ref, vec_in_ref, send_ref, keep_ref, vec_ref):
    dp, side = place()
    core = lax.rem(dp, 2)
    width = table_ref.shape[1]
    half = width // 2
    ow = width // 16
    for ref, bit in ((keep_ref, core), (send_ref, 1 - core)):

        @pl.loop(0, 2 * LAYERS)
        def _(t, ref=ref, bit=bit):
            z = (t & 1) * 2 + ((t >> 1) & 1)
            chip = z * 2 + (t >> 2)
            rows = pl.ds(pl.multiple_of((chip * 2 + bit) * ow, ow), ow)
            for j in range(3):
                at = pl.ds(pl.multiple_of(t * 3 * ow + j * ow, ow), ow)
                both = dw_ref[j, rows, :].astype(F32) + got_ref[j, rows, :].astype(F32)
                ref[at, :] = both.astype(ref.dtype)

    one, two = vec_in_ref[0:1, :], vec_in_ref[1:2, :]
    gain = table_ref[LN1_GAIN : LN1_GAIN + 1, :]
    offset = table_ref[LN1_OFFSET : LN1_OFFSET + 1, :]
    grad_gain = (one - offset * two) / gain
    for j, values in ((0, grad_gain), (2, two)):
        vec_ref[j : j + 1, :] = values[:, 0:half]
        vec_ref[j + 1 : j + 2, :] = values[:, half:]
    for j in (0, 1):
        other, own = vec_in_ref[2 + j : 3 + j, 0:half], vec_in_ref[2 + j : 3 + j, half:]
        vec_ref[4 + 2 * j : 5 + 2 * j, :] = jnp.where(side == 0, own, other)
        vec_ref[5 + 2 * j : 6 + 2 * j, :] = jnp.where(side == 0, other, own)
    store_two(send_ref, 24 * ow, vec_ref[...])


def gather_grads(table, dw, got, vec):
    width = table.shape[1]
    half = width // 2
    rows = 24 * (width // 16)
    shapes = [((rows + 16, half), BF16), ((rows, half), F32), ((8, half), F32)]
    return pl.pallas_call(
        gather_kernel,
        grid=(1,),
        in_specs=[
            whole(table.shape),
            pl.BlockSpec((None, 3, width, half), lambda i: (1, 0, 0, 0)),
            whole(got.shape),
            whole(vec.shape),
        ],
        out_specs=[whole(shape) for shape, _ in shapes],
        out_shape=[struct(*shape) for shape in shapes],
        name="gather_grads",
        **params(2, 12),
    )(table, dw, got, vec)


def finish_kernel(ff, ow, mine_ref, vec_ref, mine_w_ref, vec_w_ref, *refs):
    came, came_w, outs = refs[: LAYERS - 1], refs[LAYERS - 1 : LAYERS + 2], refs[LAYERS + 2 :]
    down_ref, up_ref, out_ref, *outs = outs

    def total(mine, vec, parts):
        size = mine.shape[0]
        values, sums = mine[...], vec[...]
        for ref in parts:
            if ref.shape[0] > size:
                values += ref[0:size, :].astype(F32)
            sums += load_two(ref, ref.shape[0] - 2 * vec.shape[0], vec.shape[0])
        return values, sums

    half = mine_ref.shape[1]
    values, vec = total(mine_ref, vec_ref, came)
    down_ref[:, 0:half] = values[0:ff]
    down_ref[:, half:] = values[ff : 2 * ff]
    up_ref[:, 0:half] = values[2 * ff : 3 * ff]
    up_ref[:, half:] = values[3 * ff : 4 * ff]
    out_ref[...] = values[4 * ff :]
    values, vec_w = total(mine_w_ref, vec_w_ref, came_w)
    for j in range(3):
        outs[j][...] = values[j * ow : (j + 1) * ow]
    at = 0
    rows = [vec[j : j + 1] for j in range(vec.shape[0])] + [
        vec_w[j : j + 1] for j in range(vec_w.shape[0])
    ]
    for ref in outs[3:]:
        for j in range(ref.shape[1] // half):
            ref[:, j * half : (j + 1) * half] = rows[at]
            at += 1


def finish(mine, vec, mine_w, vec_w, came, came_w, ff, ow):
    half = mine.shape[1]
    vmem = pl.BlockSpec(memory_space=pltpu.VMEM)
    shapes = [(ff, 2 * half), (ff, 2 * half), (ow, half)] + [(ow, half)] * 3
    shapes += [(1, 2 * half)] * 4 + [(1, 8 * half)] + [(1, 2 * half)] * 4
    return pl.pallas_call(
        functools.partial(finish_kernel, ff, ow),
        in_specs=[vmem] * (4 + len(came) + len(came_w)),
        out_specs=[vmem] * len(shapes),
        out_shape=[struct(shape, F32) for shape in shapes],
        name="finish",
        **params(3, 12),
    )(mine, vec, mine_w, vec_w, *came, *came_w)


def input_grad_kernel(first, x_ref, gh_ref, table_ref, w_ref, dq_ref, dk_ref, dv_ref, *refs):
    gf_ref = refs[-1]
    total = dot_on(dq_ref[...], w_ref[0], 1, 1)
    total += dot_on(dk_ref[...], w_ref[1], 1, 1)
    total += dot_on(dv_ref[...], w_ref[2], 1, 1)
    unit, scale = unit_rows(jnp.where(real_rows(x_ref, first), x_ref[...].astype(F32), 0.0))
    lifted = total * table_ref[LN1_GAIN : LN1_GAIN + 1, :]
    gf_ref[...] = (gh_ref[...] + unit_back(lifted, unit, scale)).astype(BF16)


def input_grads(first, tiles, frames, grad_hidden, table, weights, grads, before=()):
    rows, width = grad_hidden.shape
    tile = 256
    wide = pl.BlockSpec((tile, width), lambda i: (i + first, 0))
    return pl.pallas_call(
        functools.partial(input_grad_kernel, first),
        grid=(tiles,),
        in_specs=[wide, wide, whole(table.shape), whole(weights.shape), wide, wide, wide]
        + [pl.BlockSpec(memory_space=pl.ANY)] * len(before),
        out_specs=wide,
        out_shape=struct(frames.shape, BF16),
        input_output_aliases={7 + j: j for j in range(len(before))},
        name="input_grads",
        **params(tiles, 20),
    )(frames, grad_hidden, table, weights, *grads, *before)


def on_whole_windows(
    frames,
    cotangent,
    window_live,
    language,
    task,
    ln1_gain,
    ln1_offset,
    query_weight,
    query_bias,
    key_weight,
    value_weight,
    value_bias,
    out_weight,
    out_bias,
    ln2_gain,
    ln2_offset,
    up_weight,
    up_bias,
    down_weight,
    down_bias,
):
    ow, ff = query_weight.shape[0], up_weight.shape[1]
    pieces, big, table = pack(
        window_live,
        language,
        task,
        query_weight,
        key_weight,
        value_weight,
        out_weight,
        up_weight,
        down_weight,
        up_bias,
        query_bias,
        value_bias,
        [ln1_gain, ln1_offset, out_bias, ln2_gain, ln2_offset, down_bias],
    )
    together = lax.optimization_barrier

    def after(values, first):
        return together((values, first))[0]

    def doubled(values, came):
        return jnp.concatenate([values, came], axis=0)

    came = swap(pieces, 2 * BIT_Z)
    normed, normed_t = first_norm(frames, table)
    came, normed = together((came, normed))
    pieces = doubled(pieces, came)
    big = after(big[None], (pieces, normed_t))
    big = doubled(big, swap(big, 2 * BIT_Z))
    came = swap(pieces, BIT_Z)
    big = after(big, came)
    pieces = doubled(pieces, came)
    near = doubled(pieces, swap(pieces, BIT_Y))
    big = doubled(big, swap(big, BIT_Z))
    far = swap(near, BIT_CORE)
    near_other = swap(near, BIT_X)

    normed_one, big, far = together((normed, big, far))
    big_y = swap(big, BIT_Y)
    big_x = swap(big, BIT_X)
    half_done = list(attend_forward_fast(1, normed_one, near, far, table))
    near_other, big_y, big_x, half_done[4] = together((near_other, big_y, big_x, half_done[4]))
    far_other = swap(near_other, BIT_CORE)
    big_xy = swap(big_y, BIT_X)
    across = [swap(p, BIT_CORE) for p in (big, big_y, big_x)]
    q, k, v, probs, context, rest, inverse, weights = attend_forward_fast(
        0, normed, near_other, far_other, table, half_done
    )
    big_xy, context = together((big_xy, context))
    across.append(swap(big_xy, BIT_CORE))
    masks = (0, BIT_Y, BIT_X, BIT_X | BIT_Y)
    masks += tuple(m | BIT_CORE for m in masks)
    output, grads, grad_hidden, send, keep, vec = middle(
        context, frames, cotangent, table, masks, [big, big_y, big_x, big_xy, *across]
    )

    def backward(first, pairs, grads, vec, before=()):
        return attend_backward_fast(
            first, pairs, q, k, v, probs, inverse, context, rest, grads, normed_t, weights, vec, before
        )

    came = swap(send, BIT_CORE)
    *done, vec_w = backward(0, 1, grads, jnp.zeros_like(table[0:8]))
    came, grads = lax.optimization_barrier((came, grads))
    mine, vec, *sends = spread(keep, vec, [came], part_xy, (1, 2, 3), 4)
    *sends, grads = lax.optimization_barrier((*sends, grads))
    came_xy = [swap(s, m) for s, m in zip(sends, (BIT_X, BIT_Y, BIT_X | BIT_Y))]
    *done, vec_w = backward(1, 2, grads, vec_w, done)
    across = done[3][0]
    came_xy, grads, across = lax.optimization_barrier((came_xy, grads, across))
    mine, vec, *sends = spread(mine, vec, came_xy, part_z, (1, 2, 3), LAYERS)
    *sends, grads, across = lax.optimization_barrier((*sends, grads, across))
    got = swap(across, BIT_X)
    came_z = [swap(s, m * BIT_Z) for s, m in zip(sends, (1, 2, 3))]
    *done, dw, vec_w = backward(3, 1, grads, vec_w, done)

    came_z, got, vec_w = together((came_z, got, vec_w))
    send, keep_w, vec_w = gather_grads(table, dw, got, vec_w)
    came = [swap(send, BIT_CORE)]
    mine_w, vec_w, *sends = spread(keep_w, vec_w, came, part_yz, (1, 2, 3), 4)
    came = [swap(s, m) for s, m in zip(sends, (BIT_Z, BIT_Y, BIT_Z | BIT_Y))]
    grad_frames = input_grads(0, 4, frames, grad_hidden, table, weights, done)
    came, grad_frames = together((came, grad_frames))
    mine_w, vec_w, *sends = spread(mine_w, vec_w, came, part_high, (1, None, None), 2)
    came_w = [
        swap(s, m) for s, m in zip(sends, (2 * BIT_Z, BIT_X, 2 * BIT_Z | BIT_X))
    ]
    grad_frames = input_grads(4, 2, frames, grad_hidden, table, weights, done, [grad_frames])
    came_w, grad_frames = together((came_w, grad_frames))
    down_grad, up_grad, out_grad, query_grad, key_grad, value_grad, *vectors = finish(
        mine, vec, mine_w, vec_w, came_z, came_w, ff, ow
    )
    vectors = [v.reshape(-1) for v in vectors]
    out_bias_grad, gain_two, offset_two, down_bias_grad, up_bias_grad = vectors[:5]
    gain_one, offset_one, query_bias_grad, value_bias_grad = vectors[5:]
    return (
        output,
        grad_frames,
        gain_one,
        offset_one,
        query_grad,
        query_bias_grad,
        key_grad,
        value_grad,
        value_bias_grad,
        out_grad.T,
        out_bias_grad,
        gain_two,
        offset_two,
        up_grad.T,
        up_bias_grad,
        down_grad,
        down_bias_grad,
    )


def solution(mesh):
    placed = (
        P(("dp", "head"), None),
        P(("dp", "head"), None),
        P(),
        P(),
        P(),
        P(),
        P(),
        P("dp", "head"),
        P(),
        P("dp", "head"),
        P("dp", "head"),
        P(),
        P("head", "dp"),
        P(),
        P(),
        P(),
        P(None, ("dp", "head")),
        P(),
        P(("dp", "head"), None),
        P(),
    )
    step = on_device
    if mesh.shape["dp"] == 4 * LAYERS and mesh.shape["head"] == SLOTS:
        step = on_whole_windows
    return jax.shard_map(
        step,
        mesh=mesh,
        in_specs=placed,
        out_specs=(
            P(("dp", "head"), None),
            P(("dp", "head"), None),
            P(),
            P(),
            P("dp", "head"),
            P(),
            P("dp", "head"),
            P("dp", "head"),
            P(),
            P("head", "dp"),
            P(),
            P(),
            P(),
            P(None, ("dp", "head")),
            P(),
            P(("dp", "head"), None),
            P(),
        ),
        check_vma=False,
    )
```
